256 devices in a mesh: row: 16 (over y_lo, z), col: 16 (over x, y_hi, core).
Axes of the slice: x: 4, y: 4 (y_hi: 2, y_lo: 2; y = y_hi * 2 + y_lo), z: 8, core: 2. Of those that a mesh axis runs over, the one named last changes fastest.
Arguments:
- object_field: float32 [2, 2, 4096, 4096], P(None, None, 'row', 'col'), may hold values from -4 to 4
- probe: float32 [2, 128, 128], replicated, may hold values from -6 to 6
- intensity: float32 [16, 128, 128, 128], P('row', 'col'), may hold values from 0 to 2
- offset_row: int32 [16, 128], P('row', 'col'), may hold values from 0 to 255
- offset_col: int32 [16, 128], P('row', 'col'), may hold values from 0 to 255
- live: int32 [16, 16], P('row', 'col'), may hold values from 1 to 8, as said below
Outputs:
- new_object: float32 [2, 2, 4096, 4096], P(None, None, 'row', 'col')
- new_probe: float32 [2, 128, 128], replicated
The draws below stay inside these ranges and needn't reach their ends.
Inputs may be any that keep to these rules, and one draw needn't show every extreme that they name: Device (a, b) uses its first live[a, b] slots; at least one device uses all 8.
All inputs are finite; a program needn't handle non-finite values.
Results may differ from the reference program's by a relative error of at most 0.0003.
Values sent between devices are 32-bit elements; how exact they have to be, the bound alone decides.
No kernel may reach another device: no remote copies, remote signals or barrier semaphores. Data moves between devices by JAX's collectives and lax.ppermute only.
A program may use at most 64 MiB of HBM per device.

```python
import math
import jax
import jax.numpy as jnp
from jax import lax

DET = 128
TILE = 256
POS_DEV = 8
NR = 4096
NC = 4096
TOTAL_POS = 2048
N_ROW = 16
N_COL = 16


def draw_live(key, part):
    counts = jax.random.randint(jax.random.fold_in(key, 1), (N_ROW, N_COL), 1, POS_DEV + 1)
    chosen = jax.random.randint(jax.random.fold_in(key, 2), (), 0, N_ROW * N_COL)
    places = jnp.arange(N_ROW * N_COL, dtype=jnp.int32).reshape(N_ROW, N_COL)
    return jnp.where(places == chosen, POS_DEV, counts).astype(jnp.int32)


def set_ends(values, stream_key, smallest, high):
    index_at = [jax.random.randint(jax.random.fold_in(stream_key, axis), (), 0, length) for axis, length in enumerate(values.shape)]
    main_axis = values.shape.index(max(values.shape))
    beside = index_at[:main_axis] + [(index_at[main_axis] + 1) % values.shape[main_axis]] + index_at[main_axis + 1:]
    return values.at[tuple(index_at)].set(smallest).at[tuple(beside)].set(high)


def level_of(stream_key, shape, pieces, least, largest):
    def one(dim, parts):
        heights = jax.random.uniform(jax.random.fold_in(jax.random.fold_in(stream_key, 6), dim), (parts,), jnp.float32, least / len(pieces), largest / len(pieces))
        return jnp.repeat(jnp.exp(heights), shape[dim] // parts).reshape((-1,) + (1,) * (len(shape) - dim - 1))

    level = one(*pieces[0])
    for cut in pieces[1:]:
        level = level * one(*cut)
    return level


def scatter_about(key, dims, spread, limit, shards=(), kind=jnp.bfloat16):
    entries = jax.random.normal(key, dims, jnp.float32) * spread
    if len(shards) > 0:
        entries = level_of(key, dims, shards, -0.22, 0.18) * entries
    return jnp.clip(entries, min=-limit, max=limit).astype(kind)


def setup_inputs(seed: int = 0) -> dict:
    arg_keys = jax.random.split(jax.random.key(seed), 7)
    object_field = scatter_about(arg_keys[0], (2, 2, NR, NC), 0.7, 4.0, ((2, 16), (3, 16)), jnp.float32)
    probe = scatter_about(arg_keys[1], (2, DET, DET), 1.0, 6.0, (), jnp.float32)
    intensity = jnp.clip(2.0 * jax.random.uniform(arg_keys[2], (N_ROW, N_COL * POS_DEV, DET, DET), jnp.float32) ** level_of(arg_keys[2], (N_ROW, N_COL * POS_DEV, DET, DET), ((0, 16), (1, 16)), -0.2, 0.2), 0.0, 2.0)
    offset_row = set_ends(jax.random.randint(arg_keys[3], (N_ROW, N_COL * POS_DEV), 0, TILE), jax.random.fold_in(arg_keys[3], 1), 0, TILE - 1).astype(jnp.int32)
    offset_col = set_ends(jax.random.randint(arg_keys[4], (N_ROW, N_COL * POS_DEV), 0, TILE), jax.random.fold_in(arg_keys[4], 1), 0, TILE - 1).astype(jnp.int32)
    live = draw_live(jax.random.fold_in(arg_keys[6], 71), 0)
    return dict(object_field=object_field, probe=probe, intensity=intensity, offset_row=offset_row, offset_col=offset_col, live=live)


STEP_OBJECT = 0.03
STEP_PROBE = 2.0
FRESNEL_PHASE = 60.0

def make_tables(width):
    index = jnp.arange(width, dtype=jnp.int32)
    product = index[:, None] * index[None, :] % width
    angle = 2.0 * math.pi / width * product.astype(jnp.float32)
    scale = 1.0 / math.sqrt(width)
    four_re = jnp.cos(angle) * scale
    four_im = -jnp.sin(angle) * scale
    freq = jnp.where(index < width // 2, index, index - width).astype(jnp.float32) / width
    phase = -FRESNEL_PHASE * (freq[:, None] ** 2 + freq[None, :] ** 2)
    return (four_re, four_im, jnp.cos(phase), jnp.sin(phase))

def transform(wave_re, wave_im, four_re, four_im):
    high = lax.Precision.HIGHEST
    right_re = jnp.einsum('kab,bc->kac', wave_re, four_re, precision=high) - jnp.einsum('kab,bc->kac', wave_im, four_im, precision=high)
    right_im = jnp.einsum('kab,bc->kac', wave_re, four_im, precision=high) + jnp.einsum('kab,bc->kac', wave_im, four_re, precision=high)
    out_re = jnp.einsum('ab,kbc->kac', four_re, right_re, precision=high) - jnp.einsum('ab,kbc->kac', four_im, right_im, precision=high)
    out_im = jnp.einsum('ab,kbc->kac', four_im, right_re, precision=high) + jnp.einsum('ab,kbc->kac', four_re, right_im, precision=high)
    return (out_re, out_im)

def window_grads(windows, probe, measured, active, tabs):
    four_re, four_im, prop_re, prop_im = tabs
    probe_re, probe_im = (probe[0], probe[1])
    first_re, first_im = (windows[:, 0, 0], windows[:, 0, 1])
    second_re, second_im = (windows[:, 1, 0], windows[:, 1, 1])
    wave_re = probe_re * first_re - probe_im * first_im
    wave_im = probe_re * first_im + probe_im * first_re
    spec_re, spec_im = transform(wave_re, wave_im, four_re, four_im)
    spec_re, spec_im = (spec_re * prop_re - spec_im * prop_im, spec_re * prop_im + spec_im * prop_re)
    mid_re, mid_im = transform(spec_re, spec_im, four_re, -four_im)
    exit_re = mid_re * second_re - mid_im * second_im
    exit_im = mid_re * second_im + mid_im * second_re
    far_re, far_im = transform(exit_re, exit_im, four_re, four_im)
    weight = 2.0 * (far_re * far_re + far_im * far_im - measured) * active[:, None, None]
    chi_re, chi_im = transform(weight * far_re, weight * far_im, four_re, -four_im)
    back_re = second_re * chi_re + second_im * chi_im
    back_im = second_re * chi_im - second_im * chi_re
    grad2_re = mid_re * chi_re + mid_im * chi_im
    grad2_im = mid_re * chi_im - mid_im * chi_re
    spec_re, spec_im = transform(back_re, back_im, four_re, four_im)
    spec_re, spec_im = (spec_re * prop_re + spec_im * prop_im, spec_im * prop_re - spec_re * prop_im)
    down_re, down_im = transform(spec_re, spec_im, four_re, -four_im)
    grad1_re = probe_re * down_re + probe_im * down_im
    grad1_im = probe_re * down_im - probe_im * down_re
    probe_gre = lax.optimization_barrier(jnp.sum(first_re * down_re + first_im * down_im, axis=0))
    probe_gim = lax.optimization_barrier(jnp.sum(first_re * down_im - first_im * down_re, axis=0))
    grads = jnp.stack([jnp.stack([grad1_re, grad1_im], 1), jnp.stack([grad2_re, grad2_im], 1)], 1)
    return (grads, jnp.stack([probe_gre, probe_gim]))

def reference(object_field, probe, intensity, offset_row, offset_col, live):
    width = DET
    half = width // 2
    padded = jnp.pad(object_field, ((0, 0), (0, 0), (half, half), (half, half)))
    tabs = make_tables(width)

    def device_step(carried, device):
        grad_pad, probe_total = carried
        row_dev = (device // N_COL).astype(jnp.int32)
        col_dev = (device % N_COL).astype(jnp.int32)
        row_off = lax.dynamic_slice(offset_row, (row_dev, col_dev * POS_DEV), (1, POS_DEV))[0]
        col_off = lax.dynamic_slice(offset_col, (row_dev, col_dev * POS_DEV), (1, POS_DEV))[0]
        row_start = (row_dev * TILE + row_off).astype(jnp.int32)
        col_start = (col_dev * TILE + col_off).astype(jnp.int32)
        measured = lax.dynamic_slice(intensity, (row_dev, col_dev * POS_DEV, jnp.int32(0), jnp.int32(0)), (1, POS_DEV, width, width))[0]
        count_here = lax.dynamic_slice(live, (row_dev, col_dev), (1, 1))[0, 0]
        active = (jnp.arange(POS_DEV, dtype=jnp.int32) < count_here).astype(jnp.float32)
        windows = jax.vmap(lambda rstart, cstart: lax.dynamic_slice(padded, (jnp.int32(0), jnp.int32(0), rstart, cstart), (2, 2, width, width)))(row_start, col_start)
        grads, probe_part = window_grads(windows, probe, measured, active, tabs)

        def add_slot(slot, accum_grad):
            start = (jnp.int32(0), jnp.int32(0), row_start[slot], col_start[slot])
            current = lax.dynamic_slice(accum_grad, start, (2, 2, width, width))
            return lax.dynamic_update_slice(accum_grad, current + grads[slot], start)
        grad_pad = lax.fori_loop(0, POS_DEV, add_slot, grad_pad)
        return ((grad_pad, probe_total + probe_part), None)
    start_state = (jnp.zeros(padded.shape, jnp.float32), jnp.zeros(probe.shape, jnp.float32))
    (grad_pad, probe_total), _ = lax.scan(device_step, start_state, jnp.arange(N_ROW * N_COL, dtype=jnp.int32))
    grad = grad_pad[:, :, half:half + TILE * N_ROW, half:half + TILE * N_COL]
    new_object = object_field - STEP_OBJECT * grad
    new_probe = probe - STEP_PROBE / TOTAL_POS * probe_total
    return (new_object, new_probe)
```

```python
import functools
import math

import jax
import jax.numpy as jnp
import ml_dtypes
import numpy as np
from jax import lax
from jax.experimental import pallas as pl
from jax.experimental.pallas import tpu as pltpu
from jax.sharding import PartitionSpec as P

STEP_OBJECT = 0.03
STEP_PROBE = 2.0
FRESNEL_PHASE = 60.0
LANES = 128
BOTH = ("row", "col")
GRANT = 48 * 1024 * 1024


def split_table(table):
    high = table.astype(ml_dtypes.bfloat16)
    low = (table - high.astype(np.float64)).astype(ml_dtypes.bfloat16)
    return high, low


def make_tables(width):
    index = np.arange(width)
    four = np.exp(-2j * math.pi * (np.outer(index, index) % width) / width) / math.sqrt(width)
    freq = np.where(index < width // 2, index, index - width) / width
    hop = np.conj(four) @ np.diag(np.exp(-1j * FRESNEL_PHASE * freq**2)) @ four
    forms = []
    for table in (hop, four):
        forms.append(np.block([[table.real, table.imag], [-table.imag, table.real]]))
        forms.append(np.block([[table.real, -table.imag], [table.imag, table.real]]))
    pairs = [split_table(form) for form in forms]
    return np.stack([np.stack(pair) for pair in pairs])


def split(value):
    high = value.astype(jnp.bfloat16)
    low = (value - high.astype(jnp.float32)).astype(jnp.bfloat16)
    return high, low


def mul3(left, right):
    dot = functools.partial(jnp.dot, preferred_element_type=jnp.float32)
    return dot(left[0], right[0]) + (dot(left[1], right[0]) + dot(left[0], right[1]))


def two_sided(tabs_ref, right, left, real, imag):
    width = real.shape[1]
    field = split(jnp.concatenate([real, imag], axis=1))
    half = mul3(field, (tabs_ref[right, 0], tabs_ref[right, 1]))
    real, imag = half[:, :width], half[:, width:]
    field = jnp.concatenate(
        [
            jnp.concatenate([real[:width], real[width:]], axis=1),
            jnp.concatenate([imag[:width], imag[width:]], axis=1),
        ],
        axis=0,
    )
    full = mul3((tabs_ref[left, 0], tabs_ref[left, 1]), split(field))
    real = jnp.concatenate([full[:width, :width], full[:width, width:]], axis=0)
    imag = jnp.concatenate([full[width:, :width], full[width:, width:]], axis=0)
    return real, imag


def pack_kernel(obj_ref, low_ref, high_ref, *corner_refs):
    half = LANES // 2
    first = lax.broadcasted_iota(jnp.int32, (obj_ref.shape[2], LANES), 1) < half
    tile = obj_ref.shape[2]
    for piece in range(2):
        low = jnp.where(
            first, obj_ref[piece, 0, :, :LANES], pltpu.roll(obj_ref[piece, 1, :, :LANES], half, 1)
        )
        high = jnp.where(
            first, pltpu.roll(obj_ref[piece, 0, :, LANES:], half, 1), obj_ref[piece, 1, :, LANES:]
        )
        low_ref[piece] = low
        high_ref[piece] = high
        corner_refs[0][piece] = low[:half]
        corner_refs[1][piece] = high[:half]
        corner_refs[2][piece] = low[tile - half :]
        corner_refs[3][piece] = high[tile - half :]


def place_window(row_ref, col_ref, slot):
    col = col_ref[0, slot] + LANES // 2
    return row_ref[0, slot], col // LANES, lax.rem(col, LANES)


def step_kernel(
    row_ref, col_ref, live_ref, obj_ref, up_ref, down_ref, low_ref, high_ref,
    ul_ref, uh_ref, dl_ref, dh_ref, probe_ref, measured_ref, tabs_ref,
    new_ref, gup_ref, gdown_ref, glow_ref, ghigh_ref, gul_ref, guh_ref, gdl_ref, gdh_ref, gp_ref,
    ext, grad,
):
    width = probe_ref.shape[1]
    tile = obj_ref.shape[2]
    half = width // 2
    grad[...] = jnp.zeros_like(grad)
    gp_ref[...] = jnp.zeros_like(gp_ref)
    for piece in range(2):
        for part in range(2):
            for block in range(2):
                cols = pl.ds(block * LANES, LANES)
                ext[piece, part, 1 + block, :half] = up_ref[piece, part, :, cols]
                ext[piece, part, 1 + block, half : half + tile] = obj_ref[piece, part, :, cols]
                ext[piece, part, 1 + block, half + tile :] = down_ref[piece, part, :, cols]
            for block, sides in ((0, (ul_ref, low_ref, dl_ref)), (3, (uh_ref, high_ref, dh_ref))):
                for ref, start in zip(sides, (0, half, half + tile)):
                    strip = ref[piece]
                    if (block == 0) == (part == 0):
                        strip = pltpu.roll(strip, half, 1)
                    ext[piece, part, block, start : start + strip.shape[0]] = strip
    lane = lax.broadcasted_iota(jnp.int32, (width, LANES), 1)

    def window(slot, piece):
        row, block, shift = place_window(row_ref, col_ref, slot)
        back = lax.rem(LANES - shift, LANES)
        keep = lane < LANES - shift
        parts = []
        for part in range(2):
            near = pltpu.roll(ext[piece, part, block, pl.ds(row, width), :], back, 1)
            far = pltpu.roll(ext[piece, part, block + 1, pl.ds(row, width), :], back, 1)
            parts.append(jnp.where(keep, near, far))
        return parts

    def deposit(slot, piece, values):
        row, block, shift = place_window(row_ref, col_ref, slot)
        keep = lane >= shift
        for part in range(2):
            value = pltpu.roll(values[part], shift, 1)
            grad[piece, part, block, pl.ds(row, width), :] += jnp.where(keep, value, 0.0)
            grad[piece, part, block + 1, pl.ds(row, width), :] += jnp.where(keep, 0.0, value)

    def pair(index, _):
        slots = (2 * index, 2 * index + 1)
        firsts = [window(slot, 0) for slot in slots]
        seconds = [window(slot, 1) for slot in slots]
        first_re, first_im = (jnp.concatenate([f[p] for f in firsts], axis=0) for p in range(2))
        second_re, second_im = (jnp.concatenate([f[p] for f in seconds], axis=0) for p in range(2))
        probe_re = jnp.concatenate([probe_ref[0], probe_ref[0]], axis=0)
        probe_im = jnp.concatenate([probe_ref[1], probe_ref[1]], axis=0)
        wave_re = probe_re * first_re - probe_im * first_im
        wave_im = probe_re * first_im + probe_im * first_re
        mid_re, mid_im = two_sided(tabs_ref, 0, 1, wave_re, wave_im)
        exit_re = mid_re * second_re - mid_im * second_im
        exit_im = mid_re * second_im + mid_im * second_re
        far_re, far_im = two_sided(tabs_ref, 2, 3, exit_re, exit_im)
        weights = []
        for place, slot in enumerate(slots):
            rows = slice(place * width, (place + 1) * width)
            active = jnp.where(slot < live_ref[0, 0], 2.0, 0.0)
            power = far_re[rows] * far_re[rows] + far_im[rows] * far_im[rows]
            weights.append((power - measured_ref[slot]) * active)
        weight = jnp.concatenate(weights, axis=0)
        chi_re, chi_im = two_sided(tabs_ref, 3, 2, weight * far_re, weight * far_im)
        back_re = second_re * chi_re + second_im * chi_im
        back_im = second_re * chi_im - second_im * chi_re
        grad_re = mid_re * chi_re + mid_im * chi_im
        grad_im = mid_re * chi_im - mid_im * chi_re
        for place, slot in enumerate(slots):
            rows = slice(place * width, (place + 1) * width)
            deposit(slot, 1, (grad_re[rows], grad_im[rows]))
        down_re, down_im = two_sided(tabs_ref, 1, 0, back_re, back_im)
        grad_re = probe_re * down_re + probe_im * down_im
        grad_im = probe_re * down_im - probe_im * down_re
        for place, slot in enumerate(slots):
            rows = slice(place * width, (place + 1) * width)
            deposit(slot, 0, (grad_re[rows], grad_im[rows]))
        sum_re = first_re * down_re + first_im * down_im
        sum_im = first_re * down_im - first_im * down_re
        gp_ref[0] += sum_re[:width] + sum_re[width:]
        gp_ref[1] += sum_im[:width] + sum_im[width:]
        return 0

    lax.fori_loop(0, row_ref.shape[1] // 2, pair, 0)
    lower = lax.broadcasted_iota(jnp.int32, (half, LANES), 1) < half
    inner = lax.broadcasted_iota(jnp.int32, (tile, LANES), 1) < half
    for piece in range(2):
        for part in range(2):
            for block in range(2):
                cols = pl.ds(block * LANES, LANES)
                gup_ref[piece, part, :, cols] = grad[piece, part, 1 + block, :half]
                gdown_ref[piece, part, :, cols] = grad[piece, part, 1 + block, half + tile :]
                new_ref[piece, part, :, cols] = (
                    obj_ref[piece, part, :, cols]
                    - STEP_OBJECT * grad[piece, part, 1 + block, half : half + tile]
                )
        for block, outs in ((0, (gul_ref, glow_ref, gdl_ref)), (3, (guh_ref, ghigh_ref, gdh_ref))):
            for ref, start in zip(outs, (0, half, half + tile)):
                size = ref.shape[1]
                mask = inner if size == tile else lower
                real = grad[piece, 0, block, start : start + size]
                imag = grad[piece, 1, block, start : start + size]
                if block == 0:
                    real = pltpu.roll(real, half, 1)
                else:
                    imag = pltpu.roll(imag, half, 1)
                ref[piece] = jnp.where(mask, real, imag)


def finish_kernel(
    part_ref, up_ref, down_ref, low_ref, high_ref, ul_ref, uh_ref, dl_ref, dh_ref, probe_ref, sum_ref,
    new_ref, newp_ref, *, scale,
):
    tile = part_ref.shape[2]
    half = up_ref.shape[2]
    first = lax.broadcasted_iota(jnp.int32, (half, LANES), 1) < half
    newp_ref[...] = probe_ref[...] - scale * sum_ref[...]
    for piece in range(2):
        for part in range(2):
            for start in range(0, tile, half):
                rows = slice(start, start + half)
                for block in range(2):
                    cols = slice(block * LANES, (block + 1) * LANES)
                    strips = [(low_ref, high_ref)[block][piece, rows]]
                    total = None
                    if start == 0:
                        strips.append((ul_ref, uh_ref)[block][piece])
                        total = up_ref[piece, part, :, cols]
                    if start == tile - half:
                        strips.append((dl_ref, dh_ref)[block][piece])
                        total = down_ref[piece, part, :, cols]
                    strip = strips[0] if len(strips) == 1 else strips[0] + strips[1]
                    if block != part:
                        strip = pltpu.roll(strip, half, 1)
                    strip = jnp.where(first == (block == 0), strip, 0.0)
                    total = strip if total is None else total + strip
                    new_ref[piece, part, rows, cols] = (
                        part_ref[piece, part, rows, cols] - STEP_OBJECT * total
                    )


def vmem(count):
    return [pl.BlockSpec(memory_space=pltpu.VMEM)] * count


def smem(count):
    return [pl.BlockSpec(memory_space=pltpu.SMEM)] * count


def array(*shape):
    return jax.ShapeDtypeStruct(shape, jnp.float32)


def moves(rows, cols, row_step, col_step):
    pairs = []
    for a in range(rows):
        for b in range(cols):
            if 0 <= a + row_step < rows and 0 <= b + col_step < cols:
                pairs.append((a * cols + b, (a + row_step) * cols + b + col_step))
    return pairs


STEPS = ((-1, 0), (1, 0), (0, -1), (0, 1), (-1, -1), (-1, 1), (1, -1), (1, 1))


def exchange(strips):
    rows, cols = lax.axis_size("row"), lax.axis_size("col")
    got = [
        lax.ppermute(strip, BOTH, moves(rows, cols, *step)) for strip, step in zip(strips, STEPS)
    ]
    return [got[1], got[0], got[3], got[2], got[7], got[6], got[5], got[4]]


def swap(value, mask):
    return lax.ppermute(
        value, BOTH, [(i, i ^ mask) for i in range(lax.axis_size("row") * lax.axis_size("col"))]
    )


def on_device(object_field, probe, intensity, offset_row, offset_col, live):
    tile = object_field.shape[2]
    width = probe.shape[1]
    half = width // 2
    params = pltpu.CompilerParams(vmem_limit_bytes=GRANT)
    side, corner, edge = array(2, tile, LANES), array(2, half, LANES), array(2, 2, half, tile)
    packed = pl.pallas_call(
        pack_kernel, out_shape=(side,) * 2 + (corner,) * 4, in_specs=vmem(1),
        out_specs=tuple(vmem(6)), compiler_params=params,
    )(object_field)
    halo = exchange([object_field[:, :, :half], object_field[:, :, tile - half :], *packed])
    tabs = jnp.asarray(make_tables(width))
    count = offset_row.shape[1]
    outs = pl.pallas_call(
        step_kernel,
        out_shape=(array(2, 2, tile, tile), edge, edge, side, side) + (corner,) * 4
        + (array(2, width, width),),
        in_specs=smem(3) + vmem(12),
        out_specs=tuple(vmem(10)),
        scratch_shapes=[pltpu.VMEM((2, 2, 4, tile + width, LANES), jnp.float32)] * 2,
        compiler_params=params,
    )(offset_row, offset_col, live, object_field, *halo, probe, intensity[0], tabs)
    back = exchange(outs[1:9])
    total = outs[9]
    for bit in range(8):
        total = total + swap(total, 1 << bit)
    count_all = count * lax.axis_size("row") * lax.axis_size("col")
    return pl.pallas_call(
        functools.partial(finish_kernel, scale=STEP_PROBE / count_all),
        out_shape=(array(2, 2, tile, tile), array(2, width, width)),
        in_specs=vmem(11), out_specs=tuple(vmem(2)), compiler_params=params,
    )(outs[0], *back, probe, total)


def solution(mesh):
    placed = (
        P(None, None, "row", "col"),
        P(),
        P("row", "col", None, None),
        P("row", "col"),
        P("row", "col"),
        P("row", "col"),
    )
    return jax.shard_map(
        on_device,
        mesh=mesh,
        in_specs=placed,
        out_specs=(P(None, None, "row", "col"), P()),
        check_vma=False,
    )
```

```python
import functools
import math

import jax
import jax.numpy as jnp
import ml_dtypes
import numpy as np
from jax import lax
from jax.experimental import pallas as pl
from jax.experimental.pallas import tpu as pltpu
from jax.sharding import PartitionSpec as P

STEP_OBJECT = 0.03
STEP_PROBE = 2.0
FRESNEL_PHASE = 60.0
LANES = 128
BOTH = ("row", "col")
GRANT = 48 * 1024 * 1024
MASKS = (4, 12, 128, 130, 16, 32, 96)


def split_table(table):
    high = table.astype(ml_dtypes.bfloat16)
    low = (table - high.astype(np.float64)).astype(ml_dtypes.bfloat16)
    return high, low


def make_tables(width):
    index = np.arange(width)
    four = np.exp(-2j * math.pi * (np.outer(index, index) % width) / width) / math.sqrt(width)
    freq = np.where(index < width // 2, index, index - width) / width
    hop = np.conj(four) @ np.diag(np.exp(-1j * FRESNEL_PHASE * freq**2)) @ four
    forms = []
    for table in (hop, four):
        forms.append(np.block([[table.real, table.imag], [-table.imag, table.real]]))
        forms.append(np.block([[table.real, -table.imag], [table.imag, table.real]]))
    pairs = [split_table(form) for form in forms]
    return np.stack([np.stack(pair) for pair in pairs])


def split(value):
    high = value.astype(jnp.bfloat16)
    low = (value - high.astype(jnp.float32)).astype(jnp.bfloat16)
    return high, low


def mul3(left, right):
    dot = functools.partial(jnp.dot, preferred_element_type=jnp.float32)
    return dot(left[0], right[0]) + (dot(left[1], right[0]) + dot(left[0], right[1]))


def two_sided(tabs_ref, right, left, real, imag):
    width = real.shape[1]
    field = split(jnp.concatenate([real, imag], axis=1))
    half = mul3(field, (tabs_ref[right, 0], tabs_ref[right, 1]))
    real, imag = half[:, :width], half[:, width:]
    field = jnp.concatenate(
        [
            jnp.concatenate([real[:width], real[width:]], axis=1),
            jnp.concatenate([imag[:width], imag[width:]], axis=1),
        ],
        axis=0,
    )
    full = mul3((tabs_ref[left, 0], tabs_ref[left, 1]), split(field))
    real = jnp.concatenate([full[:width, :width], full[:width, width:]], axis=0)
    imag = jnp.concatenate([full[width:, :width], full[width:, width:]], axis=0)
    return real, imag


def pack_kernel(obj_ref, low_ref, high_ref):
    half = LANES // 2
    first = lax.broadcasted_iota(jnp.int32, (obj_ref.shape[2], LANES), 1) < half
    for piece in range(2):
        low_ref[piece] = jnp.where(
            first, obj_ref[piece, 0, :, :LANES], pltpu.roll(obj_ref[piece, 1, :, :LANES], half, 1)
        )
        high_ref[piece] = jnp.where(
            first, pltpu.roll(obj_ref[piece, 0, :, LANES:], half, 1), obj_ref[piece, 1, :, LANES:]
        )


def rows_kernel(obj_ref, low_ref, high_ref, up_ref, down_ref):
    half = LANES // 2
    tile = obj_ref.shape[2]
    for out, start in ((up_ref, 0), (down_ref, tile - half)):
        rows = slice(start, start + half)
        for piece in range(2):
            for part in range(2):
                for block in range(2):
                    cols = slice(block * LANES, (block + 1) * LANES)
                    out[piece, 2 * part + block] = obj_ref[piece, part, rows, cols]
            out[piece, 4] = low_ref[piece, rows]
            out[piece, 5] = high_ref[piece, rows]


def fold_kernel(low_ref, high_ref, up_ref, down_ref, low_out, high_out):
    half = LANES // 2
    tile = low_ref.shape[1]
    for ref, out, place in ((low_ref, low_out, 4), (high_ref, high_out, 5)):
        for piece in range(2):
            out[piece, :half] = ref[piece, :half] + up_ref[piece, place]
            out[piece, half : tile - half] = ref[piece, half : tile - half]
            out[piece, tile - half :] = ref[piece, tile - half :] + down_ref[piece, place]


def place_window(row_ref, col_ref, slot):
    col = col_ref[0, slot] + LANES // 2
    return row_ref[0, slot], col // LANES, lax.rem(col, LANES)


def step_kernel(
    row_ref, col_ref, live_ref, core_ref, obj_ref, up_ref, down_ref, low_ref, high_ref,
    probe_ref, measured_ref, tabs_ref,
    new_ref, gup_ref, gdown_ref, glow_ref, ghigh_ref, keep_ref, send_ref,
    ext, grad, gp_ref,
):
    width = probe_ref.shape[1]
    tile = obj_ref.shape[2]
    half = width // 2
    grad[...] = jnp.zeros_like(grad)
    gp_ref[...] = jnp.zeros_like(gp_ref)
    for piece in range(2):
        for part in range(2):
            for block in range(2):
                cols = pl.ds(block * LANES, LANES)
                ext[piece, part, 1 + block, :half] = up_ref[piece, 2 * part + block]
                ext[piece, part, 1 + block, half : half + tile] = obj_ref[piece, part, :, cols]
                ext[piece, part, 1 + block, half + tile :] = down_ref[piece, 2 * part + block]
            for block, side in ((0, low_ref), (3, high_ref)):
                place = 4 + block // 3
                strips = (up_ref[piece, place], side[piece], down_ref[piece, place])
                for strip, start in zip(strips, (0, half, half + tile)):
                    if (block == 0) == (part == 0):
                        strip = pltpu.roll(strip, half, 1)
                    ext[piece, part, block, start : start + strip.shape[0]] = strip
    lane = lax.broadcasted_iota(jnp.int32, (width, LANES), 1)

    def window(slot, piece):
        row, block, shift = place_window(row_ref, col_ref, slot)
        back = lax.rem(LANES - shift, LANES)
        keep = lane < LANES - shift
        parts = []
        for part in range(2):
            near = pltpu.roll(ext[piece, part, block, pl.ds(row, width), :], back, 1)
            far = pltpu.roll(ext[piece, part, block + 1, pl.ds(row, width), :], back, 1)
            parts.append(jnp.where(keep, near, far))
        return parts

    def deposit(slot, piece, values):
        row, block, shift = place_window(row_ref, col_ref, slot)
        keep = lane >= shift
        for part in range(2):
            value = pltpu.roll(values[part], shift, 1)
            grad[piece, part, block, pl.ds(row, width), :] += jnp.where(keep, value, 0.0)
            grad[piece, part, block + 1, pl.ds(row, width), :] += jnp.where(keep, 0.0, value)

    def pair(index, _):
        slots = (2 * index, 2 * index + 1)
        firsts = [window(slot, 0) for slot in slots]
        seconds = [window(slot, 1) for slot in slots]
        first_re, first_im = (jnp.concatenate([f[p] for f in firsts], axis=0) for p in range(2))
        second_re, second_im = (jnp.concatenate([f[p] for f in seconds], axis=0) for p in range(2))
        probe_re = jnp.concatenate([probe_ref[0], probe_ref[0]], axis=0)
        probe_im = jnp.concatenate([probe_ref[1], probe_ref[1]], axis=0)
        wave_re = probe_re * first_re - probe_im * first_im
        wave_im = probe_re * first_im + probe_im * first_re
        mid_re, mid_im = two_sided(tabs_ref, 0, 1, wave_re, wave_im)
        exit_re = mid_re * second_re - mid_im * second_im
        exit_im = mid_re * second_im + mid_im * second_re
        far_re, far_im = two_sided(tabs_ref, 2, 3, exit_re, exit_im)
        weights = []
        for place, slot in enumerate(slots):
            rows = slice(place * width, (place + 1) * width)
            active = jnp.where(slot < live_ref[0, 0], 2.0, 0.0)
            power = far_re[rows] * far_re[rows] + far_im[rows] * far_im[rows]
            weights.append((power - measured_ref[slot]) * active)
        weight = jnp.concatenate(weights, axis=0)
        chi_re, chi_im = two_sided(tabs_ref, 3, 2, weight * far_re, weight * far_im)
        back_re = second_re * chi_re + second_im * chi_im
        back_im = second_re * chi_im - second_im * chi_re
        grad_re = mid_re * chi_re + mid_im * chi_im
        grad_im = mid_re * chi_im - mid_im * chi_re
        for place, slot in enumerate(slots):
            rows = slice(place * width, (place + 1) * width)
            deposit(slot, 1, (grad_re[rows], grad_im[rows]))
        down_re, down_im = two_sided(tabs_ref, 1, 0, back_re, back_im)
        grad_re = probe_re * down_re + probe_im * down_im
        grad_im = probe_re * down_im - probe_im * down_re
        for place, slot in enumerate(slots):
            rows = slice(place * width, (place + 1) * width)
            deposit(slot, 0, (grad_re[rows], grad_im[rows]))
        sum_re = first_re * down_re + first_im * down_im
        sum_im = first_re * down_im - first_im * down_re
        gp_ref[0] += sum_re[:width] + sum_re[width:]
        gp_ref[1] += sum_im[:width] + sum_im[width:]
        return 0

    lax.fori_loop(0, row_ref.shape[1] // 2, pair, 0)
    first = lax.broadcasted_iota(jnp.int32, (half, LANES), 1) < half
    inner = lax.broadcasted_iota(jnp.int32, (tile, LANES), 1) < half
    core = core_ref[0, 0]
    keep_ref[...] = jnp.where(core == 0, gp_ref[0], gp_ref[1])
    send_ref[...] = jnp.where(core == 0, gp_ref[1], gp_ref[0])
    for piece in range(2):
        for part in range(2):
            for block in range(2):
                cols = pl.ds(block * LANES, LANES)
                gup_ref[piece, 2 * part + block] = grad[piece, part, 1 + block, :half]
                gdown_ref[piece, 2 * part + block] = grad[piece, part, 1 + block, half + tile :]
                new_ref[piece, part, :, cols] = (
                    obj_ref[piece, part, :, cols]
                    - STEP_OBJECT * grad[piece, part, 1 + block, half : half + tile]
                )
        for block, side in ((0, glow_ref), (3, ghigh_ref)):
            for start, size in ((0, half), (half, tile), (half + tile, half)):
                real = grad[piece, 0, block, start : start + size]
                imag = grad[piece, 1, block, start : start + size]
                if block == 0:
                    real = pltpu.roll(real, half, 1)
                else:
                    imag = pltpu.roll(imag, half, 1)
                strip = jnp.where(inner if size == tile else first, real, imag)
                if size == tile:
                    side[piece] = strip
                else:
                    (gup_ref if start == 0 else gdown_ref)[piece, 4 + block // 3] = strip


def finish_kernel(
    core_ref, part_ref, up_ref, down_ref, low_ref, high_ref, probe_ref, mine_ref, other_ref,
    new_ref, newp_ref, *, scale,
):
    tile = part_ref.shape[2]
    half = up_ref.shape[2]
    first = lax.broadcasted_iota(jnp.int32, (half, LANES), 1) < half
    core = core_ref[0, 0]
    newp_ref[0] = probe_ref[0] - scale * jnp.where(core == 0, mine_ref[...], other_ref[...])
    newp_ref[1] = probe_ref[1] - scale * jnp.where(core == 0, other_ref[...], mine_ref[...])
    for piece in range(2):
        for part in range(2):
            for start in range(0, tile, half):
                rows = slice(start, start + half)
                for block in range(2):
                    cols = slice(block * LANES, (block + 1) * LANES)
                    total = (low_ref, high_ref)[block][piece, rows]
                    if block != part:
                        total = pltpu.roll(total, half, 1)
                    total = jnp.where(first == (block == 0), total, 0.0)
                    if start == 0:
                        total += up_ref[piece, 2 * part + block]
                    if start == tile - half:
                        total += down_ref[piece, 2 * part + block]
                    new_ref[piece, part, rows, cols] = (
                        part_ref[piece, part, rows, cols] - STEP_OBJECT * total
                    )


def vmem(count):
    return [pl.BlockSpec(memory_space=pltpu.VMEM)] * count


def smem(count):
    return [pl.BlockSpec(memory_space=pltpu.SMEM)] * count


def array(*shape):
    return jax.ShapeDtypeStruct(shape, jnp.float32)


def moves(rows, cols, row_step, col_step):
    pairs = []
    for a in range(rows):
        for b in range(cols):
            if 0 <= a + row_step < rows and 0 <= b + col_step < cols:
                pairs.append((a * cols + b, (a + row_step) * cols + b + col_step))
    return pairs


def shift(value, row_step, col_step):
    rows, cols = lax.axis_size("row"), lax.axis_size("col")
    return lax.ppermute(value, BOTH, moves(rows, cols, row_step, col_step))


def swap(value, mask):
    count = lax.axis_size("row") * lax.axis_size("col")
    return lax.ppermute(value, BOTH, [(i, i ^ mask) for i in range(count)])


def call(kernel, out_shape, scalars, arrays, scratch=()):
    return pl.pallas_call(
        kernel, out_shape=tuple(out_shape), in_specs=smem(len(scalars)) + vmem(len(arrays)),
        out_specs=tuple(vmem(len(out_shape))), scratch_shapes=list(scratch),
        compiler_params=pltpu.CompilerParams(vmem_limit_bytes=GRANT),
    )(*scalars, *arrays)


def on_device(object_field, probe, intensity, offset_row, offset_col, live):
    tile = object_field.shape[2]
    width = probe.shape[1]
    half = width // 2
    side, edge, field = array(2, tile, LANES), array(2, 6, half, LANES), array(2, 2, tile, tile)
    core = lax.rem(lax.axis_index("col"), 2).astype(jnp.int32).reshape(1, 1)
    low, high = call(pack_kernel, (side, side), (), (object_field,))
    low, high = shift(high, 0, 1), shift(low, 0, -1)
    up, down = call(rows_kernel, (edge, edge), (), (object_field, low, high))
    up, down = shift(down, 1, 0), shift(up, -1, 0)
    tabs = jnp.asarray(make_tables(width))
    count = offset_row.shape[1]
    grown = pltpu.VMEM((2, 2, 4, tile + width, LANES), jnp.float32)
    part, gup, gdown, glow, ghigh, mine, send = call(
        step_kernel,
        (field, edge, edge, side, side, array(width, width), array(width, width)),
        (offset_row, offset_col, live, core),
        (object_field, up, down, low, high, probe, intensity[0], tabs),
        (grown, grown, pltpu.VMEM((2, width, width), jnp.float32)),
    )
    mine = mine + swap(send, 1)
    mine, gup, gdown = lax.optimization_barrier((mine, gup, gdown))
    up, down = shift(gdown, 1, 0), shift(gup, -1, 0)
    for mask in MASKS[:4]:
        mine = mine + swap(mine, mask)
    low, high = call(fold_kernel, (side, side), (), (glow, ghigh, up, down))
    mine, low, high = lax.optimization_barrier((mine, low, high))
    low, high = shift(high, 0, 1), shift(low, 0, -1)
    for mask in MASKS[4:]:
        mine = mine + swap(mine, mask)
    other = swap(mine, 1)
    count_all = count * lax.axis_size("row") * lax.axis_size("col")
    return call(
        functools.partial(finish_kernel, scale=STEP_PROBE / count_all),
        (field, array(2, width, width)),
        (core,),
        (part, up, down, low, high, probe, mine, other),
    )


def solution(mesh):
    placed = (
        P(None, None, "row", "col"),
        P(),
        P("row", "col", None, None),
        P("row", "col"),
        P("row", "col"),
        P("row", "col"),
    )
    return jax.shard_map(
        on_device,
        mesh=mesh,
        in_specs=placed,
        out_specs=(P(None, None, "row", "col"), P()),
        check_vma=False,
    )
```

```python
import functools
import math

import jax
import jax.numpy as jnp
import ml_dtypes
import numpy as np
from jax import lax
from jax.experimental import pallas as pl
from jax.experimental.pallas import tpu as pltpu
from jax.sharding import PartitionSpec as P

STEP_OBJECT = 0.03
STEP_PROBE = 2.0
FRESNEL_PHASE = 60.0
LANES = 128
BOTH = ("row", "col")
GRANT = 48 * 1024 * 1024
MASKS = (4, 12, 128, 130, 16, 32, 96)


def split_table(table):
    high = table.astype(ml_dtypes.bfloat16)
    low = (table - high.astype(np.float64)).astype(ml_dtypes.bfloat16)
    return high, low


def make_tables(width):
    index = np.arange(width)
    four = np.exp(-2j * math.pi * (np.outer(index, index) % width) / width) / math.sqrt(width)
    freq = np.where(index < width // 2, index, index - width) / width
    hop = np.conj(four) @ np.diag(np.exp(-1j * FRESNEL_PHASE * freq**2)) @ four
    forms = []
    for table in (hop, four):
        forms.append(np.block([[table.real, table.imag], [-table.imag, table.real]]))
        forms.append(np.block([[table.real, -table.imag], [table.imag, table.real]]))
    pairs = [split_table(form) for form in forms]
    return np.stack([np.stack(pair) for pair in pairs])


def split(value):
    high = value.astype(jnp.bfloat16)
    low = (value - high.astype(jnp.float32)).astype(jnp.bfloat16)
    return high, low


def mul3(left, right):
    dot = functools.partial(jnp.dot, preferred_element_type=jnp.float32)
    return dot(left[0], right[0]) + (dot(left[1], right[0]) + dot(left[0], right[1]))


def two_sided(tabs_ref, right, left, real, imag):
    width = real.shape[1]
    field = split(jnp.concatenate([real, imag], axis=1))
    half = mul3(field, (tabs_ref[right, 0], tabs_ref[right, 1]))
    real, imag = half[:, :width], half[:, width:]
    field = jnp.concatenate(
        [
            jnp.concatenate([real[:width], real[width:]], axis=1),
            jnp.concatenate([imag[:width], imag[width:]], axis=1),
        ],
        axis=0,
    )
    full = mul3((tabs_ref[left, 0], tabs_ref[left, 1]), split(field))
    real = jnp.concatenate([full[:width, :width], full[:width, width:]], axis=0)
    imag = jnp.concatenate([full[width:, :width], full[width:, width:]], axis=0)
    return real, imag


def columns(piece_ref, first):
    half = LANES // 2
    left = jnp.where(first, piece_ref[0, :, :LANES], pltpu.roll(piece_ref[1, :, :LANES], half, 1))
    right = jnp.where(first, pltpu.roll(piece_ref[0, :, LANES:], half, 1), piece_ref[1, :, LANES:])
    return left, right


def pick(spot_ref, axis, even, odd):
    return jnp.where(spot_ref[0, axis] == 0, even, odd)


def pack_kernel(spot_ref, obj_ref, *outs):
    first = lax.broadcasted_iota(jnp.int32, (obj_ref.shape[2], LANES), 1) < LANES // 2
    for piece in range(2):
        left, right = columns(obj_ref.at[piece], first)
        outs[2 * piece][...] = pick(spot_ref, 1, right, left)
        outs[2 * piece + 1][...] = pick(spot_ref, 1, left, right)


def rows_kernel(spot_ref, obj_ref, cola_ref, colb_ref, rowa_ref, rowb_ref, *, piece):
    half = LANES // 2
    low, high = slice(0, half), slice(obj_ref.shape[2] - half, obj_ref.shape[2])
    for part in range(2):
        for block in range(2):
            cols = slice(block * LANES, (block + 1) * LANES)
            top, bottom = obj_ref[piece, part, low, cols], obj_ref[piece, part, high, cols]
            rowa_ref[2 * part + block] = pick(spot_ref, 0, bottom, top)
            rowb_ref[2 * part + block] = pick(spot_ref, 0, top, bottom)
    for place, east in ((4, False), (5, True)):
        even, odd = (cola_ref, colb_ref) if east else (colb_ref, cola_ref)
        top = pick(spot_ref, 1, even[low], odd[low])
        bottom = pick(spot_ref, 1, even[high], odd[high])
        rowa_ref[place] = pick(spot_ref, 0, bottom, top)
        rowb_ref[place] = pick(spot_ref, 0, top, bottom)


def grow(ext, spot_ref, piece_ref, cola_ref, colb_ref, rowa_ref, rowb_ref):
    half = LANES // 2
    tile = piece_ref.shape[1]
    for part in range(2):
        for block in range(4):
            place = 2 * part + block - 1 if block in (1, 2) else 4 + block // 3
            top = pick(spot_ref, 0, rowb_ref[place], rowa_ref[place])
            bottom = pick(spot_ref, 0, rowa_ref[place], rowb_ref[place])
            if block in (1, 2):
                middle = piece_ref[part, :, (block - 1) * LANES : block * LANES]
            elif block == 0:
                middle = pick(spot_ref, 1, colb_ref[...], cola_ref[...])
            else:
                middle = pick(spot_ref, 1, cola_ref[...], colb_ref[...])
            for strip, start in ((top, 0), (middle, half), (bottom, half + tile)):
                if (block == 0 and part == 0) or (block == 3 and part == 1):
                    strip = pltpu.roll(strip, half, 1)
                ext[part, block, start : start + strip.shape[0]] = strip


def place_window(row_ref, col_ref, slot):
    col = col_ref[0, slot] + LANES // 2
    return row_ref[0, slot], col // LANES, lax.rem(col, LANES)


def window(ext, row_ref, col_ref, slot, width):
    row, block, shift = place_window(row_ref, col_ref, slot)
    back = lax.rem(LANES - shift, LANES)
    keep = lax.broadcasted_iota(jnp.int32, (width, LANES), 1) < LANES - shift
    parts = []
    for part in range(2):
        near = pltpu.roll(ext[part, block, pl.ds(row, width), :], back, 1)
        far = pltpu.roll(ext[part, block + 1, pl.ds(row, width), :], back, 1)
        parts.append(jnp.where(keep, near, far))
    return parts


def windows(ext, row_ref, col_ref, slots, width):
    got = [window(ext, row_ref, col_ref, slot, width) for slot in slots]
    return tuple(jnp.concatenate([g[part] for g in got], axis=0) for part in range(2))


def stacked(ref, slots, part):
    return jnp.concatenate([ref[slot, part] for slot in slots], axis=0)


def store(ref, slots, values):
    width = ref.shape[2]
    for place, slot in enumerate(slots):
        for part in range(2):
            ref[slot, part] = values[part][place * width : (place + 1) * width]


def first_kernel(
    row_ref, col_ref, spot_ref, obj_ref, cola_ref, colb_ref, rowa_ref, rowb_ref, probe_ref, tabs_ref,
    win_ref, mid_ref, ext,
):
    width = probe_ref.shape[1]
    grow(ext, spot_ref, obj_ref.at[0], cola_ref, colb_ref, rowa_ref, rowb_ref)

    def pair(index, _):
        slots = (2 * index, 2 * index + 1)
        first_re, first_im = windows(ext, row_ref, col_ref, slots, width)
        probe_re, probe_im = (jnp.concatenate([probe_ref[p]] * 2, axis=0) for p in range(2))
        wave_re = probe_re * first_re - probe_im * first_im
        wave_im = probe_re * first_im + probe_im * first_re
        store(win_ref, slots, (first_re, first_im))
        store(mid_ref, slots, two_sided(tabs_ref, 0, 1, wave_re, wave_im))
        return 0

    lax.fori_loop(0, row_ref.shape[1] // 2, pair, 0)


def second_kernel(
    row_ref, col_ref, spot_ref, live_ref, obj_ref, cola_ref, colb_ref, rowa_ref, rowb_ref,
    win_ref, mid_ref, measured_ref, tabs_ref,
    grad_ref, down_ref, keep_ref, send_ref,
    ext, sum_ref,
):
    width = win_ref.shape[2]
    grow(ext, spot_ref, obj_ref.at[1], cola_ref, colb_ref, rowa_ref, rowb_ref)
    sum_ref[...] = jnp.zeros_like(sum_ref)

    def pair(index, _):
        slots = (2 * index, 2 * index + 1)
        second_re, second_im = windows(ext, row_ref, col_ref, slots, width)
        mid_re, mid_im = (stacked(mid_ref, slots, part) for part in range(2))
        exit_re = mid_re * second_re - mid_im * second_im
        exit_im = mid_re * second_im + mid_im * second_re
        far_re, far_im = two_sided(tabs_ref, 2, 3, exit_re, exit_im)
        weights = []
        for place, slot in enumerate(slots):
            rows = slice(place * width, (place + 1) * width)
            active = jnp.where(slot < live_ref[0, 0], 2.0, 0.0)
            power = far_re[rows] * far_re[rows] + far_im[rows] * far_im[rows]
            weights.append((power - measured_ref[slot]) * active)
        weight = jnp.concatenate(weights, axis=0)
        chi_re, chi_im = two_sided(tabs_ref, 3, 2, weight * far_re, weight * far_im)
        grad_re = mid_re * chi_re + mid_im * chi_im
        grad_im = mid_re * chi_im - mid_im * chi_re
        store(grad_ref, slots, (grad_re, grad_im))
        back_re = second_re * chi_re + second_im * chi_im
        back_im = second_re * chi_im - second_im * chi_re
        down_re, down_im = two_sided(tabs_ref, 1, 0, back_re, back_im)
        store(down_ref, slots, (down_re, down_im))
        first_re, first_im = (stacked(win_ref, slots, part) for part in range(2))
        sum_re = first_re * down_re + first_im * down_im
        sum_im = first_re * down_im - first_im * down_re
        sum_ref[0] += sum_re[:width] + sum_re[width:]
        sum_ref[1] += sum_im[:width] + sum_im[width:]
        return 0

    lax.fori_loop(0, row_ref.shape[1] // 2, pair, 0)
    keep_ref[...] = pick(spot_ref, 1, sum_ref[0], sum_ref[1])
    send_ref[...] = pick(spot_ref, 1, sum_ref[1], sum_ref[0])


def place_kernel(
    row_ref, col_ref, spot_ref, obj_ref, probe_ref, down_ref, second_ref,
    new_ref, rowa_ref, rowb_ref, left_ref, right_ref,
    grad,
):
    width = probe_ref.shape[1]
    tile = obj_ref.shape[2]
    half = width // 2
    grad[...] = jnp.zeros_like(grad)
    lane = lax.broadcasted_iota(jnp.int32, (width, LANES), 1)

    def deposit(slot, _):
        row, block, shift = place_window(row_ref, col_ref, slot)
        keep = lane >= shift
        probe_re, probe_im = probe_ref[0], probe_ref[1]
        down_re, down_im = down_ref[slot, 0], down_ref[slot, 1]
        values = (
            (probe_re * down_re + probe_im * down_im, probe_re * down_im - probe_im * down_re),
            (second_ref[slot, 0], second_ref[slot, 1]),
        )
        for piece in range(2):
            for part in range(2):
                value = pltpu.roll(values[piece][part], shift, 1)
                grad[piece, part, block, pl.ds(row, width), :] += jnp.where(keep, value, 0.0)
                grad[piece, part, block + 1, pl.ds(row, width), :] += jnp.where(keep, 0.0, value)
        return 0

    lax.fori_loop(0, row_ref.shape[1], deposit, 0)
    first = lax.broadcasted_iota(jnp.int32, (tile + width, LANES), 1) < half
    for piece in range(2):
        for part in range(2):
            for block in range(2):
                cols = slice(block * LANES, (block + 1) * LANES)
                top = grad[piece, part, 1 + block, :half]
                bottom = grad[piece, part, 1 + block, half + tile :]
                rowa_ref[piece, 2 * part + block] = pick(spot_ref, 0, bottom, top)
                rowb_ref[piece, 2 * part + block] = pick(spot_ref, 0, top, bottom)
                new_ref[piece, part, :, cols] = (
                    obj_ref[piece, part, :, cols]
                    - STEP_OBJECT * grad[piece, part, 1 + block, half : half + tile]
                )
        left = jnp.where(first, pltpu.roll(grad[piece, 0, 0], half, 1), grad[piece, 1, 0])
        right = jnp.where(first, grad[piece, 0, 3], pltpu.roll(grad[piece, 1, 3], half, 1))
        for place, strip, ref in ((4, left, left_ref), (5, right, right_ref)):
            top, bottom = strip[:half], strip[half + tile :]
            rowa_ref[piece, place] = pick(spot_ref, 0, bottom, top)
            rowb_ref[piece, place] = pick(spot_ref, 0, top, bottom)
            ref[piece] = strip[half : half + tile]


def fold_kernel(spot_ref, left_ref, right_ref, rowa_ref, rowb_ref, cola_ref, colb_ref):
    half = LANES // 2
    tile = left_ref.shape[1]
    for piece in range(2):
        sides = []
        for ref, place in ((left_ref, 4), (right_ref, 5)):
            a, b = rowa_ref[piece, place], rowb_ref[piece, place]
            sides.append(
                (
                    ref[piece, :half] + pick(spot_ref, 0, b, a),
                    ref[piece, half : tile - half],
                    ref[piece, tile - half :] + pick(spot_ref, 0, a, b),
                )
            )
        for left, right, rows in zip(*sides, (slice(0, half), slice(half, tile - half), slice(tile - half, tile))):
            cola_ref[piece, rows] = pick(spot_ref, 1, right, left)
            colb_ref[piece, rows] = pick(spot_ref, 1, left, right)


def finish_kernel(
    spot_ref, part_ref, rowa_ref, rowb_ref, cola_ref, colb_ref, probe_ref, mine_ref, other_ref,
    new_ref, newp_ref, *, scale,
):
    tile = part_ref.shape[2]
    half = LANES // 2
    first = lax.broadcasted_iota(jnp.int32, (half, LANES), 1) < half
    newp_ref[0] = probe_ref[0] - scale * pick(spot_ref, 1, mine_ref[...], other_ref[...])
    newp_ref[1] = probe_ref[1] - scale * pick(spot_ref, 1, other_ref[...], mine_ref[...])
    for piece in range(2):
        for start in range(0, tile, half):
            rows = slice(start, start + half)
            cola, colb = cola_ref[piece, rows], colb_ref[piece, rows]
            sides = (pick(spot_ref, 1, colb, cola), pick(spot_ref, 1, cola, colb))
            for part in range(2):
                for block in range(2):
                    cols = slice(block * LANES, (block + 1) * LANES)
                    total = sides[block]
                    if block != part:
                        total = pltpu.roll(total, half, 1)
                    total = jnp.where(first == (block == 0), total, 0.0)
                    a, b = rowa_ref[piece, 2 * part + block], rowb_ref[piece, 2 * part + block]
                    if start == 0:
                        total += pick(spot_ref, 0, b, a)
                    if start == tile - half:
                        total += pick(spot_ref, 0, a, b)
                    new_ref[piece, part, rows, cols] = (
                        part_ref[piece, part, rows, cols] - STEP_OBJECT * total
                    )


def vmem(count):
    return [pl.BlockSpec(memory_space=pltpu.VMEM)] * count


def smem(count):
    return [pl.BlockSpec(memory_space=pltpu.SMEM)] * count


def array(*shape):
    return jax.ShapeDtypeStruct(shape, jnp.float32)


def meet(strips, axis):
    rows, cols = lax.axis_size("row"), lax.axis_size("col")
    got = []
    for odd, strip in enumerate(strips):
        pairs = []
        for a in range(rows):
            for b in range(cols):
                c, d = (a, b) if axis else (((a + odd) ^ 1) - odd, b)
                if axis:
                    d = ((b + odd) ^ 1) - odd
                if 0 <= c < rows and 0 <= d < cols:
                    pairs.append((a * cols + b, c * cols + d))
        got.append(lax.ppermute(strip, BOTH, pairs))
    return got


def swap(value, mask):
    count = lax.axis_size("row") * lax.axis_size("col")
    return lax.ppermute(value, BOTH, [(i, i ^ mask) for i in range(count)])


def call(kernel, out_shape, scalars, arrays, scratch=()):
    return pl.pallas_call(
        kernel, out_shape=tuple(out_shape), in_specs=smem(len(scalars)) + vmem(len(arrays)),
        out_specs=tuple(vmem(len(out_shape))), scratch_shapes=list(scratch),
        compiler_params=pltpu.CompilerParams(vmem_limit_bytes=GRANT),
    )(*scalars, *arrays)


def on_device(object_field, probe, intensity, offset_row, offset_col, live):
    tile = object_field.shape[2]
    width = probe.shape[1]
    half = width // 2
    count = offset_row.shape[1]
    side, edge, plane = (tile, LANES), (6, half, LANES), (width, width)
    field, fields = array(2, 2, tile, tile), array(count, 2, width, width)
    spot = jnp.stack([lax.axis_index("row"), lax.axis_index("col")]).astype(jnp.int32) % 2
    spot = spot.reshape(1, 2)
    tabs = jnp.asarray(make_tables(width))
    grown = pltpu.VMEM((2, 4, tile + width, LANES), jnp.float32)
    packed = call(pack_kernel, [array(*side)] * 4, (spot,), (object_field,))
    halos = []
    cols = [meet(packed[2 * piece : 2 * piece + 2], 1) for piece in range(2)]
    for piece in range(2):
        strips = call(
            functools.partial(rows_kernel, piece=piece), [array(*edge)] * 2,
            (spot,), (object_field, *cols[piece]),
        )
        halos.append((*cols[piece], *meet(strips, 0)))
    win, mid = call(
        first_kernel, [fields] * 2, (offset_row, offset_col, spot),
        (object_field, *halos[0], probe, tabs), (grown,),
    )
    grad, down, mine, send = call(
        second_kernel, [fields] * 2 + [array(*plane)] * 2, (offset_row, offset_col, spot, live),
        (object_field, *halos[1], win, mid, intensity[0], tabs),
        (grown, pltpu.VMEM((2, *plane), jnp.float32)),
    )
    part, *strips, left, right = call(
        place_kernel, [field] + [array(2, *edge)] * 2 + [array(2, *side)] * 2,
        (offset_row, offset_col, spot), (object_field, probe, down, grad),
        (pltpu.VMEM((2, 2, 4, tile + width, LANES), jnp.float32),),
    )
    mine = mine + swap(send, 1)
    mine = mine + swap(mine, MASKS[0])
    mine, *strips = lax.optimization_barrier((mine, *strips))
    rows = meet(strips, 0)
    for mask in MASKS[1:4]:
        mine = mine + swap(mine, mask)
    strips = call(fold_kernel, [array(2, *side)] * 2, (spot,), (left, right, *rows))
    mine, *strips = lax.optimization_barrier((mine, *strips))
    cols = meet(strips, 1)
    for mask in MASKS[4:]:
        mine = mine + swap(mine, mask)
    other = swap(mine, 1)
    count_all = count * lax.axis_size("row") * lax.axis_size("col")
    return call(
        functools.partial(finish_kernel, scale=STEP_PROBE / count_all),
        (field, array(2, *plane)),
        (spot,),
        (part, *rows, *cols, probe, mine, other),
    )


def solution(mesh):
    placed = (
        P(None, None, "row", "col"),
        P(),
        P("row", "col", None, None),
        P("row", "col"),
        P("row", "col"),
        P("row", "col"),
    )
    return jax.shard_map(
        on_device,
        mesh=mesh,
        in_specs=placed,
        out_specs=(P(None, None, "row", "col"), P()),
        check_vma=False,
    )
```

```python
import functools
import math

import jax
import jax.numpy as jnp
import ml_dtypes
import numpy as np
from jax import lax
from jax.experimental import pallas as pl
from jax.experimental.pallas import tpu as pltpu
from jax.sharding import PartitionSpec as P

STEP_OBJECT = 0.03
STEP_PROBE = 2.0
FRESNEL_PHASE = 60.0
LANES = 128
BOTH = ("row", "col")
GRANT = 16 * 1024 * 1024
MASKS = (4, 12, 128, 130, 16, 32, 96)


def split_table(table):
    high = table.astype(ml_dtypes.bfloat16)
    low = (table - high.astype(np.float64)).astype(ml_dtypes.bfloat16)
    return high, low


def make_tables(width):
    index = np.arange(width)
    four = np.exp(-2j * math.pi * (np.outer(index, index) % width) / width) / math.sqrt(width)
    freq = np.where(index < width // 2, index, index - width) / width
    hop = np.conj(four) @ np.diag(np.exp(-1j * FRESNEL_PHASE * freq**2)) @ four
    forms = []
    for table in (hop, four):
        forms.append(np.block([[table.real, table.imag], [-table.imag, table.real]]))
        forms.append(np.block([[table.real, -table.imag], [table.imag, table.real]]))
    pairs = [split_table(form) for form in forms]
    return np.stack([np.stack(pair) for pair in pairs])


def split(value):
    high = value.astype(jnp.bfloat16)
    low = (value - high.astype(jnp.float32)).astype(jnp.bfloat16)
    return high, low


def mul3(left, right):
    dot = functools.partial(jnp.dot, preferred_element_type=jnp.float32)
    return dot(left[0], right[0]) + (dot(left[1], right[0]) + dot(left[0], right[1]))


def two_sided(tabs_ref, right, left, real, imag):
    width = real.shape[1]
    field = split(jnp.concatenate([real, imag], axis=1))
    half = mul3(field, (tabs_ref[right, 0], tabs_ref[right, 1]))
    real, imag = half[:, :width], half[:, width:]
    field = jnp.concatenate(
        [
            jnp.concatenate([real[:width], real[width:]], axis=1),
            jnp.concatenate([imag[:width], imag[width:]], axis=1),
        ],
        axis=0,
    )
    full = mul3((tabs_ref[left, 0], tabs_ref[left, 1]), split(field))
    real = jnp.concatenate([full[:width, :width], full[:width, width:]], axis=0)
    imag = jnp.concatenate([full[width:, :width], full[width:, width:]], axis=0)
    return real, imag


def columns(piece_ref, first):
    half = LANES // 2
    left = jnp.where(first, piece_ref[0, :, :LANES], pltpu.roll(piece_ref[1, :, :LANES], half, 1))
    right = jnp.where(first, pltpu.roll(piece_ref[0, :, LANES:], half, 1), piece_ref[1, :, LANES:])
    return left, right


def pick(spot_ref, axis, even, odd):
    return jnp.where(lax.rem(spot_ref[0, axis], 2) == 0, even, odd)


def beside(spot_ref, axis, a, b):
    place = spot_ref[0, axis]
    before = jnp.where(place == 0, 0.0, pick(spot_ref, axis, b, a))
    after = jnp.where(place == spot_ref[0, 2 + axis] - 1, 0.0, pick(spot_ref, axis, a, b))
    return before, after


def pack_kernel(spot_ref, obj_ref, *outs):
    first = lax.broadcasted_iota(jnp.int32, (obj_ref.shape[2], LANES), 1) < LANES // 2
    for piece in range(2):
        left, right = columns(obj_ref.at[piece], first)
        outs[2 * piece][...] = pick(spot_ref, 1, right, left)
        outs[2 * piece + 1][...] = pick(spot_ref, 1, left, right)


def rows_kernel(spot_ref, obj_ref, cola_ref, colb_ref, rowa_ref, rowb_ref, *, piece):
    half = LANES // 2
    low, high = slice(0, half), slice(obj_ref.shape[2] - half, obj_ref.shape[2])
    for part in range(2):
        for block in range(2):
            cols = slice(block * LANES, (block + 1) * LANES)
            top, bottom = obj_ref[piece, part, low, cols], obj_ref[piece, part, high, cols]
            rowa_ref[2 * part + block] = pick(spot_ref, 0, bottom, top)
            rowb_ref[2 * part + block] = pick(spot_ref, 0, top, bottom)
    tops = beside(spot_ref, 1, cola_ref[low], colb_ref[low])
    bottoms = beside(spot_ref, 1, cola_ref[high], colb_ref[high])
    for place, top, bottom in zip((4, 5), tops, bottoms):
        rowa_ref[place] = pick(spot_ref, 0, bottom, top)
        rowb_ref[place] = pick(spot_ref, 0, top, bottom)


def grow(ext, spot_ref, piece_ref, cola_ref, colb_ref, rowa_ref, rowb_ref):
    half = LANES // 2
    tile = piece_ref.shape[1]
    sides = beside(spot_ref, 1, cola_ref[...], colb_ref[...])
    for part in range(2):
        for block in range(4):
            place = 2 * part + block - 1 if block in (1, 2) else 4 + block // 3
            top, bottom = beside(spot_ref, 0, rowa_ref[place], rowb_ref[place])
            if block in (1, 2):
                middle = piece_ref[part, :, (block - 1) * LANES : block * LANES]
            else:
                middle = sides[block // 3]
            for strip, start in ((top, 0), (middle, half), (bottom, half + tile)):
                if (block == 0 and part == 0) or (block == 3 and part == 1):
                    strip = pltpu.roll(strip, half, 1)
                ext[part, block, start : start + strip.shape[0]] = strip


def place_window(row_ref, col_ref, slot):
    col = col_ref[0, slot] + LANES // 2
    return row_ref[0, slot], col // LANES, lax.rem(col, LANES)


def window(ext, row_ref, col_ref, slot, width):
    row, block, shift = place_window(row_ref, col_ref, slot)
    back = lax.rem(LANES - shift, LANES)
    keep = lax.broadcasted_iota(jnp.int32, (width, LANES), 1) < LANES - shift
    parts = []
    for part in range(2):
        near = pltpu.roll(ext[part, block, pl.ds(row, width), :], back, 1)
        far = pltpu.roll(ext[part, block + 1, pl.ds(row, width), :], back, 1)
        parts.append(jnp.where(keep, near, far))
    return parts


def windows(ext, row_ref, col_ref, slots, width):
    got = [window(ext, row_ref, col_ref, slot, width) for slot in slots]
    return tuple(jnp.concatenate([g[part] for g in got], axis=0) for part in range(2))


def stacked(ref, slots, part):
    return jnp.concatenate([ref[slot, part] for slot in slots], axis=0)


def store(ref, slots, values):
    width = ref.shape[2]
    for place, slot in enumerate(slots):
        for part in range(2):
            ref[slot, part] = values[part][place * width : (place + 1) * width]


def first_kernel(
    row_ref, col_ref, spot_ref, obj_ref, cola_ref, colb_ref, rowa_ref, rowb_ref, probe_ref, tabs_ref,
    win_ref, mid_ref, ext,
):
    width = probe_ref.shape[1]
    grow(ext, spot_ref, obj_ref.at[0], cola_ref, colb_ref, rowa_ref, rowb_ref)

    def pair(index, _):
        slots = (2 * index, 2 * index + 1)
        first_re, first_im = windows(ext, row_ref, col_ref, slots, width)
        probe_re, probe_im = (jnp.concatenate([probe_ref[p]] * 2, axis=0) for p in range(2))
        wave_re = probe_re * first_re - probe_im * first_im
        wave_im = probe_re * first_im + probe_im * first_re
        store(win_ref, slots, (first_re, first_im))
        store(mid_ref, slots, two_sided(tabs_ref, 0, 1, wave_re, wave_im))
        return 0

    lax.fori_loop(0, row_ref.shape[1] // 2, pair, 0)


def second_kernel(
    row_ref, col_ref, spot_ref, live_ref, obj_ref, cola_ref, colb_ref, rowa_ref, rowb_ref,
    win_ref, mid_ref, measured_ref, tabs_ref,
    grad_ref, down_ref, keep_ref, send_ref,
    ext, sum_ref,
):
    width = win_ref.shape[2]
    grow(ext, spot_ref, obj_ref.at[1], cola_ref, colb_ref, rowa_ref, rowb_ref)
    sum_ref[...] = jnp.zeros_like(sum_ref)

    def pair(index, _):
        slots = (2 * index, 2 * index + 1)
        second_re, second_im = windows(ext, row_ref, col_ref, slots, width)
        mid_re, mid_im = (stacked(mid_ref, slots, part) for part in range(2))
        exit_re = mid_re * second_re - mid_im * second_im
        exit_im = mid_re * second_im + mid_im * second_re
        far_re, far_im = two_sided(tabs_ref, 2, 3, exit_re, exit_im)
        weights = []
        for place, slot in enumerate(slots):
            rows = slice(place * width, (place + 1) * width)
            active = jnp.where(slot < live_ref[0, 0], 2.0, 0.0)
            power = far_re[rows] * far_re[rows] + far_im[rows] * far_im[rows]
            weights.append((power - measured_ref[slot]) * active)
        weight = jnp.concatenate(weights, axis=0)
        chi_re, chi_im = two_sided(tabs_ref, 3, 2, weight * far_re, weight * far_im)
        grad_re = mid_re * chi_re + mid_im * chi_im
        grad_im = mid_re * chi_im - mid_im * chi_re
        store(grad_ref, slots, (grad_re, grad_im))
        back_re = second_re * chi_re + second_im * chi_im
        back_im = second_re * chi_im - second_im * chi_re
        down_re, down_im = two_sided(tabs_ref, 1, 0, back_re, back_im)
        store(down_ref, slots, (down_re, down_im))
        first_re, first_im = (stacked(win_ref, slots, part) for part in range(2))
        sum_re = first_re * down_re + first_im * down_im
        sum_im = first_re * down_im - first_im * down_re
        sum_ref[0] += sum_re[:width] + sum_re[width:]
        sum_ref[1] += sum_im[:width] + sum_im[width:]
        return 0

    lax.fori_loop(0, row_ref.shape[1] // 2, pair, 0)
    keep_ref[...] = pick(spot_ref, 1, sum_ref[0], sum_ref[1])
    send_ref[...] = pick(spot_ref, 1, sum_ref[1], sum_ref[0])


def place_kernel(
    row_ref, col_ref, spot_ref, obj_ref, probe_ref, down_ref, second_ref,
    new_ref, rowa_ref, rowb_ref, left_ref, right_ref,
    grad,
):
    width = probe_ref.shape[1]
    tile = obj_ref.shape[2]
    half = width // 2
    grad[...] = jnp.zeros_like(grad)
    lane = lax.broadcasted_iota(jnp.int32, (width, LANES), 1)

    def deposit(slot, _):
        row, block, shift = place_window(row_ref, col_ref, slot)
        keep = lane >= shift
        probe_re, probe_im = probe_ref[0], probe_ref[1]
        down_re, down_im = down_ref[slot, 0], down_ref[slot, 1]
        values = (
            (probe_re * down_re + probe_im * down_im, probe_re * down_im - probe_im * down_re),
            (second_ref[slot, 0], second_ref[slot, 1]),
        )
        for piece in range(2):
            for part in range(2):
                value = pltpu.roll(values[piece][part], shift, 1)
                grad[piece, part, block, pl.ds(row, width), :] += jnp.where(keep, value, 0.0)
                grad[piece, part, block + 1, pl.ds(row, width), :] += jnp.where(keep, 0.0, value)
        return 0

    lax.fori_loop(0, row_ref.shape[1], deposit, 0)
    first = lax.broadcasted_iota(jnp.int32, (tile + width, LANES), 1) < half
    for piece in range(2):
        for part in range(2):
            for block in range(2):
                cols = slice(block * LANES, (block + 1) * LANES)
                top = grad[piece, part, 1 + block, :half]
                bottom = grad[piece, part, 1 + block, half + tile :]
                rowa_ref[piece, 2 * part + block] = pick(spot_ref, 0, bottom, top)
                rowb_ref[piece, 2 * part + block] = pick(spot_ref, 0, top, bottom)
                new_ref[piece, part, :, cols] = (
                    obj_ref[piece, part, :, cols]
                    - STEP_OBJECT * grad[piece, part, 1 + block, half : half + tile]
                )
        left = jnp.where(first, pltpu.roll(grad[piece, 0, 0], half, 1), grad[piece, 1, 0])
        right = jnp.where(first, grad[piece, 0, 3], pltpu.roll(grad[piece, 1, 3], half, 1))
        for place, strip, ref in ((4, left, left_ref), (5, right, right_ref)):
            top, bottom = strip[:half], strip[half + tile :]
            rowa_ref[piece, place] = pick(spot_ref, 0, bottom, top)
            rowb_ref[piece, place] = pick(spot_ref, 0, top, bottom)
            ref[piece] = strip[half : half + tile]


def fold_kernel(spot_ref, left_ref, right_ref, rowa_ref, rowb_ref, cola_ref, colb_ref):
    half = LANES // 2
    tile = left_ref.shape[1]
    for piece in range(2):
        sides = []
        for ref, place in ((left_ref, 4), (right_ref, 5)):
            top, bottom = beside(spot_ref, 0, rowa_ref[piece, place], rowb_ref[piece, place])
            sides.append(
                (
                    ref[piece, :half] + top,
                    ref[piece, half : tile - half],
                    ref[piece, tile - half :] + bottom,
                )
            )
        for left, right, rows in zip(*sides, (slice(0, half), slice(half, tile - half), slice(tile - half, tile))):
            cola_ref[piece, rows] = pick(spot_ref, 1, right, left)
            colb_ref[piece, rows] = pick(spot_ref, 1, left, right)


def finish_kernel(
    spot_ref, part_ref, rowa_ref, rowb_ref, cola_ref, colb_ref, probe_ref, mine_ref, other_ref,
    new_ref, newp_ref, *, scale,
):
    tile = part_ref.shape[2]
    half = LANES // 2
    first = lax.broadcasted_iota(jnp.int32, (half, LANES), 1) < half
    newp_ref[0] = probe_ref[0] - scale * pick(spot_ref, 1, mine_ref[...], other_ref[...])
    newp_ref[1] = probe_ref[1] - scale * pick(spot_ref, 1, other_ref[...], mine_ref[...])
    for piece in range(2):
        for start in range(0, tile, half):
            rows = slice(start, start + half)
            sides = beside(spot_ref, 1, cola_ref[piece, rows], colb_ref[piece, rows])
            for part in range(2):
                for block in range(2):
                    cols = slice(block * LANES, (block + 1) * LANES)
                    total = sides[block]
                    if block != part:
                        total = pltpu.roll(total, half, 1)
                    total = jnp.where(first == (block == 0), total, 0.0)
                    place = 2 * part + block
                    ends = beside(spot_ref, 0, rowa_ref[piece, place], rowb_ref[piece, place])
                    if start == 0:
                        total += ends[0]
                    if start == tile - half:
                        total += ends[1]
                    new_ref[piece, part, rows, cols] = (
                        part_ref[piece, part, rows, cols] - STEP_OBJECT * total
                    )


def vmem(count):
    return [pl.BlockSpec(memory_space=pltpu.VMEM)] * count


def smem(count):
    return [pl.BlockSpec(memory_space=pltpu.SMEM)] * count


def array(*shape):
    return jax.ShapeDtypeStruct(shape, jnp.float32)


def meet(strips, axis):
    sizes = (lax.axis_size("row"), lax.axis_size("col"))
    got = []
    for odd, strip in enumerate(strips):
        pairs = []
        for spot in np.ndindex(*sizes):
            other = list(spot)
            other[axis] = (((spot[axis] + odd) ^ 1) - odd) % sizes[axis]
            pairs.append((spot[0] * sizes[1] + spot[1], other[0] * sizes[1] + other[1]))
        got.append(lax.ppermute(strip, BOTH, pairs))
    return got


def swap(value, mask):
    count = lax.axis_size("row") * lax.axis_size("col")
    return lax.ppermute(value, BOTH, [(i, i ^ mask) for i in range(count)])


def call(kernel, out_shape, scalars, arrays, scratch=()):
    return pl.pallas_call(
        kernel, out_shape=tuple(out_shape), in_specs=smem(len(scalars)) + vmem(len(arrays)),
        out_specs=tuple(vmem(len(out_shape))), scratch_shapes=list(scratch),
        compiler_params=pltpu.CompilerParams(vmem_limit_bytes=GRANT),
    )(*scalars, *arrays)


def on_device(object_field, probe, intensity, offset_row, offset_col, live):
    tile = object_field.shape[2]
    width = probe.shape[1]
    half = width // 2
    count = offset_row.shape[1]
    side, edge, plane = (tile, LANES), (6, half, LANES), (width, width)
    field, fields = array(2, 2, tile, tile), array(count, 2, width, width)
    place = [lax.axis_index(axis) for axis in BOTH] + [lax.axis_size(axis) for axis in BOTH]
    spot = jnp.stack([jnp.asarray(entry, jnp.int32) for entry in place]).reshape(1, 4)
    tabs = jnp.asarray(make_tables(width))
    grown = pltpu.VMEM((2, 4, tile + width, LANES), jnp.float32)
    packed = call(pack_kernel, [array(*side)] * 4, (spot,), (object_field,))
    halos = []
    cols = [meet(packed[2 * piece : 2 * piece + 2], 1) for piece in range(2)]
    for piece in range(2):
        strips = call(
            functools.partial(rows_kernel, piece=piece), [array(*edge)] * 2,
            (spot,), (object_field, *cols[piece]),
        )
        halos.append((*cols[piece], *meet(strips, 0)))
    win, mid = call(
        first_kernel, [fields] * 2, (offset_row, offset_col, spot),
        (object_field, *halos[0], probe, tabs), (grown,),
    )
    grad, down, mine, send = call(
        second_kernel, [fields] * 2 + [array(*plane)] * 2, (offset_row, offset_col, spot, live),
        (object_field, *halos[1], win, mid, intensity[0], tabs),
        (grown, pltpu.VMEM((2, *plane), jnp.float32)),
    )
    part, *strips, left, right = call(
        place_kernel, [field] + [array(2, *edge)] * 2 + [array(2, *side)] * 2,
        (offset_row, offset_col, spot), (object_field, probe, down, grad),
        (pltpu.VMEM((2, 2, 4, tile + width, LANES), jnp.float32),),
    )
    mine = mine + swap(send, 1)
    mine = mine + swap(mine, MASKS[0])
    mine, *strips = lax.optimization_barrier((mine, *strips))
    rows = meet(strips, 0)
    for mask in MASKS[1:4]:
        mine = mine + swap(mine, mask)
    strips = call(fold_kernel, [array(2, *side)] * 2, (spot,), (left, right, *rows))
    mine, *strips = lax.optimization_barrier((mine, *strips))
    cols = meet(strips, 1)
    for mask in MASKS[4:]:
        mine = mine + swap(mine, mask)
    other = swap(mine, 1)
    count_all = count * lax.axis_size("row") * lax.axis_size("col")
    return call(
        functools.partial(finish_kernel, scale=STEP_PROBE / count_all),
        (field, array(2, *plane)),
        (spot,),
        (part, *rows, *cols, probe, mine, other),
    )


def solution(mesh):
    placed = (
        P(None, None, "row", "col"),
        P(),
        P("row", "col", None, None),
        P("row", "col"),
        P("row", "col"),
        P("row", "col"),
    )
    return jax.shard_map(
        on_device,
        mesh=mesh,
        in_specs=placed,
        out_specs=(P(None, None, "row", "col"), P()),
        check_vma=False,
    )
```

```python
import functools
import math

import jax
import jax.numpy as jnp
import ml_dtypes
import numpy as np
from jax import lax
from jax.experimental import pallas as pl
from jax.experimental.pallas import tpu as pltpu
from jax.sharding import PartitionSpec as P

STEP_OBJECT = 0.03
STEP_PROBE = 2.0
FRESNEL_PHASE = 60.0
LANES = 128
BOTH = ("row", "col")
GRANT = 16 * 1024 * 1024
MASKS = ((4, 16), (12, 32), (128, 96), (130, 128), (16, 130), (32, 4), (96, 12))


def split_table(table):
    high = table.astype(ml_dtypes.bfloat16)
    low = (table - high.astype(np.float64)).astype(ml_dtypes.bfloat16)
    return high, low


def make_tables(width):
    index = np.arange(width)
    four = np.exp(-2j * math.pi * (np.outer(index, index) % width) / width) / math.sqrt(width)
    freq = np.where(index < width // 2, index, index - width) / width
    hop = np.conj(four) @ np.diag(np.exp(-1j * FRESNEL_PHASE * freq**2)) @ four
    forms = []
    for table in (hop, four):
        forms.append(np.block([[table.real, table.imag], [-table.imag, table.real]]))
        forms.append(np.block([[table.real, -table.imag], [table.imag, table.real]]))
    pairs = [split_table(form) for form in forms]
    return np.stack([np.stack(pair) for pair in pairs])


def split(value):
    high = value.astype(jnp.bfloat16)
    low = (value - high.astype(jnp.float32)).astype(jnp.bfloat16)
    return high, low


def mul3(left, right):
    dot = functools.partial(jnp.dot, preferred_element_type=jnp.float32)
    return dot(left[0], right[0]) + (dot(left[1], right[0]) + dot(left[0], right[1]))


def two_sided(tabs_ref, right, left, real, imag):
    width = real.shape[1]
    field = split(jnp.concatenate([real, imag], axis=1))
    half = mul3(field, (tabs_ref[right, 0], tabs_ref[right, 1]))
    real, imag = half[:, :width], half[:, width:]
    field = jnp.concatenate(
        [
            jnp.concatenate([real[:width], real[width:]], axis=1),
            jnp.concatenate([imag[:width], imag[width:]], axis=1),
        ],
        axis=0,
    )
    full = mul3((tabs_ref[left, 0], tabs_ref[left, 1]), split(field))
    real = jnp.concatenate([full[:width, :width], full[:width, width:]], axis=0)
    imag = jnp.concatenate([full[width:, :width], full[width:, width:]], axis=0)
    return real, imag


def columns(piece_ref, first):
    half = LANES // 2
    left = jnp.where(first, piece_ref[0, :, :LANES], pltpu.roll(piece_ref[1, :, :LANES], half, 1))
    right = jnp.where(first, pltpu.roll(piece_ref[0, :, LANES:], half, 1), piece_ref[1, :, LANES:])
    return left, right


def pick(spot_ref, axis, even, odd):
    return jnp.where(lax.rem(spot_ref[0, axis], 2) == 0, even, odd)


def beside(spot_ref, axis, a, b):
    place = spot_ref[0, axis]
    before = jnp.where(place == 0, 0.0, pick(spot_ref, axis, b, a))
    after = jnp.where(place == spot_ref[0, 2 + axis] - 1, 0.0, pick(spot_ref, axis, a, b))
    return before, after


def pack_kernel(spot_ref, obj_ref, *refs):
    *outs, held, sems = refs
    first = lax.broadcasted_iota(jnp.int32, (held.shape[2], LANES), 1) < LANES // 2
    copies = [pltpu.make_async_copy(obj_ref.at[p], held.at[p], sems.at[p]) for p in range(2)]
    for copy in copies:
        copy.start()
    for piece in range(2):
        copies[piece].wait()
        left, right = columns(held.at[piece], first)
        outs[2 * piece][...] = pick(spot_ref, 1, right, left)
        outs[2 * piece + 1][...] = pick(spot_ref, 1, left, right)


def rows_kernel(spot_ref, obj_ref, cola_ref, colb_ref, rowa_ref, rowb_ref, *, piece):
    half = LANES // 2
    low, high = slice(0, half), slice(obj_ref.shape[2] - half, obj_ref.shape[2])
    for part in range(2):
        for block in range(2):
            cols = slice(block * LANES, (block + 1) * LANES)
            top, bottom = obj_ref[piece, part, low, cols], obj_ref[piece, part, high, cols]
            rowa_ref[2 * part + block] = pick(spot_ref, 0, bottom, top)
            rowb_ref[2 * part + block] = pick(spot_ref, 0, top, bottom)
    tops = beside(spot_ref, 1, cola_ref[low], colb_ref[low])
    bottoms = beside(spot_ref, 1, cola_ref[high], colb_ref[high])
    for place, top, bottom in zip((4, 5), tops, bottoms):
        rowa_ref[place] = pick(spot_ref, 0, bottom, top)
        rowb_ref[place] = pick(spot_ref, 0, top, bottom)


def grow(ext, spot_ref, piece_ref, cola_ref, colb_ref, rowa_ref, rowb_ref):
    half = LANES // 2
    tile = piece_ref.shape[1]
    sides = beside(spot_ref, 1, cola_ref[...], colb_ref[...])
    for part in range(2):
        for block in range(4):
            place = 2 * part + block - 1 if block in (1, 2) else 4 + block // 3
            top, bottom = beside(spot_ref, 0, rowa_ref[place], rowb_ref[place])
            if block in (1, 2):
                middle = piece_ref[part, :, (block - 1) * LANES : block * LANES]
            else:
                middle = sides[block // 3]
            for strip, start in ((top, 0), (middle, half), (bottom, half + tile)):
                if (block == 0 and part == 0) or (block == 3 and part == 1):
                    strip = pltpu.roll(strip, half, 1)
                ext[part, block, start : start + strip.shape[0]] = strip


def place_window(row_ref, col_ref, slot):
    col = col_ref[0, slot] + LANES // 2
    return row_ref[0, slot], col // LANES, lax.rem(col, LANES)


def window(ext, row_ref, col_ref, slot, width):
    row, block, shift = place_window(row_ref, col_ref, slot)
    back = lax.rem(LANES - shift, LANES)
    keep = lax.broadcasted_iota(jnp.int32, (width, LANES), 1) < LANES - shift
    parts = []
    for part in range(2):
        near = pltpu.roll(ext[part, block, pl.ds(row, width), :], back, 1)
        far = pltpu.roll(ext[part, block + 1, pl.ds(row, width), :], back, 1)
        parts.append(jnp.where(keep, near, far))
    return parts


def windows(ext, row_ref, col_ref, slots, width):
    got = [window(ext, row_ref, col_ref, slot, width) for slot in slots]
    return tuple(jnp.concatenate([g[part] for g in got], axis=0) for part in range(2))


def stacked(ref, slots, part):
    return jnp.concatenate([ref[slot, part] for slot in slots], axis=0)


def store(ref, slots, values):
    width = ref.shape[2]
    for place, slot in enumerate(slots):
        for part in range(2):
            ref[slot, part] = values[part][place * width : (place + 1) * width]


def first_kernel(
    row_ref, col_ref, spot_ref, obj_ref, cola_ref, colb_ref, rowa_ref, rowb_ref, probe_ref, tabs_ref,
    win_ref, mid_ref, ext,
):
    width = probe_ref.shape[1]
    grow(ext, spot_ref, obj_ref.at[0], cola_ref, colb_ref, rowa_ref, rowb_ref)

    def pair(index, _):
        slots = (2 * index, 2 * index + 1)
        first_re, first_im = windows(ext, row_ref, col_ref, slots, width)
        probe_re, probe_im = (jnp.concatenate([probe_ref[p]] * 2, axis=0) for p in range(2))
        wave_re = probe_re * first_re - probe_im * first_im
        wave_im = probe_re * first_im + probe_im * first_re
        store(win_ref, slots, (first_re, first_im))
        store(mid_ref, slots, two_sided(tabs_ref, 0, 1, wave_re, wave_im))
        return 0

    lax.fori_loop(0, row_ref.shape[1] // 2, pair, 0)


def second_kernel(
    row_ref, col_ref, spot_ref, live_ref, obj_ref, cola_ref, colb_ref, rowa_ref, rowb_ref,
    win_ref, mid_ref, measured_ref, tabs_ref,
    grad_ref, down_ref, keep_ref, send_ref,
    ext, sum_ref,
):
    width = win_ref.shape[2]
    grow(ext, spot_ref, obj_ref.at[1], cola_ref, colb_ref, rowa_ref, rowb_ref)
    sum_ref[...] = jnp.zeros_like(sum_ref)

    def pair(index, _):
        slots = (2 * index, 2 * index + 1)
        second_re, second_im = windows(ext, row_ref, col_ref, slots, width)
        mid_re, mid_im = (stacked(mid_ref, slots, part) for part in range(2))
        exit_re = mid_re * second_re - mid_im * second_im
        exit_im = mid_re * second_im + mid_im * second_re
        far_re, far_im = two_sided(tabs_ref, 2, 3, exit_re, exit_im)
        weights = []
        for place, slot in enumerate(slots):
            rows = slice(place * width, (place + 1) * width)
            active = jnp.where(slot < live_ref[0, 0], 2.0, 0.0)
            power = far_re[rows] * far_re[rows] + far_im[rows] * far_im[rows]
            weights.append((power - measured_ref[slot]) * active)
        weight = jnp.concatenate(weights, axis=0)
        chi_re, chi_im = two_sided(tabs_ref, 3, 2, weight * far_re, weight * far_im)
        grad_re = mid_re * chi_re + mid_im * chi_im
        grad_im = mid_re * chi_im - mid_im * chi_re
        store(grad_ref, slots, (grad_re, grad_im))
        back_re = second_re * chi_re + second_im * chi_im
        back_im = second_re * chi_im - second_im * chi_re
        down_re, down_im = two_sided(tabs_ref, 1, 0, back_re, back_im)
        store(down_ref, slots, (down_re, down_im))
        first_re, first_im = (stacked(win_ref, slots, part) for part in range(2))
        sum_re = first_re * down_re + first_im * down_im
        sum_im = first_re * down_im - first_im * down_re
        sum_ref[0] += sum_re[:width] + sum_re[width:]
        sum_ref[1] += sum_im[:width] + sum_im[width:]
        return 0

    lax.fori_loop(0, row_ref.shape[1] // 2, pair, 0)
    keep_ref[...] = pick(spot_ref, 1, sum_ref[0], sum_ref[1])
    send_ref[...] = pick(spot_ref, 1, sum_ref[1], sum_ref[0])


def place_kernel(
    row_ref, col_ref, spot_ref, obj_ref, probe_ref, down_ref, second_ref,
    new_ref, rowa_ref, rowb_ref, left_ref, right_ref,
    grad,
):
    width = probe_ref.shape[1]
    tile = obj_ref.shape[2]
    half = width // 2
    grad[...] = jnp.zeros_like(grad)
    lane = lax.broadcasted_iota(jnp.int32, (width, LANES), 1)

    def deposit(slot, _):
        row, block, shift = place_window(row_ref, col_ref, slot)
        keep = lane >= shift
        probe_re, probe_im = probe_ref[0], probe_ref[1]
        down_re, down_im = down_ref[slot, 0], down_ref[slot, 1]
        values = (
            (probe_re * down_re + probe_im * down_im, probe_re * down_im - probe_im * down_re),
            (second_ref[slot, 0], second_ref[slot, 1]),
        )
        for piece in range(2):
            for part in range(2):
                value = pltpu.roll(values[piece][part], shift, 1)
                grad[piece, part, block, pl.ds(row, width), :] += jnp.where(keep, value, 0.0)
                grad[piece, part, block + 1, pl.ds(row, width), :] += jnp.where(keep, 0.0, value)
        return 0

    lax.fori_loop(0, row_ref.shape[1], deposit, 0)
    first = lax.broadcasted_iota(jnp.int32, (tile + width, LANES), 1) < half
    for piece in range(2):
        for part in range(2):
            for block in range(2):
                cols = slice(block * LANES, (block + 1) * LANES)
                top = grad[piece, part, 1 + block, :half]
                bottom = grad[piece, part, 1 + block, half + tile :]
                rowa_ref[piece, 2 * part + block] = pick(spot_ref, 0, bottom, top)
                rowb_ref[piece, 2 * part + block] = pick(spot_ref, 0, top, bottom)
                new_ref[piece, part, :, cols] = (
                    obj_ref[piece, part, :, cols]
                    - STEP_OBJECT * grad[piece, part, 1 + block, half : half + tile]
                )
        left = jnp.where(first, pltpu.roll(grad[piece, 0, 0], half, 1), grad[piece, 1, 0])
        right = jnp.where(first, grad[piece, 0, 3], pltpu.roll(grad[piece, 1, 3], half, 1))
        for place, strip, ref in ((4, left, left_ref), (5, right, right_ref)):
            top, bottom = strip[:half], strip[half + tile :]
            rowa_ref[piece, place] = pick(spot_ref, 0, bottom, top)
            rowb_ref[piece, place] = pick(spot_ref, 0, top, bottom)
            ref[piece] = strip[half : half + tile]


def fold_kernel(spot_ref, left_ref, right_ref, rowa_ref, rowb_ref, cola_ref, colb_ref):
    half = LANES // 2
    tile = left_ref.shape[1]
    for piece in range(2):
        sides = []
        for ref, place in ((left_ref, 4), (right_ref, 5)):
            top, bottom = beside(spot_ref, 0, rowa_ref[piece, place], rowb_ref[piece, place])
            sides.append(
                (
                    ref[piece, :half] + top,
                    ref[piece, half : tile - half],
                    ref[piece, tile - half :] + bottom,
                )
            )
        for left, right, rows in zip(*sides, (slice(0, half), slice(half, tile - half), slice(tile - half, tile))):
            cola_ref[piece, rows] = pick(spot_ref, 1, right, left)
            colb_ref[piece, rows] = pick(spot_ref, 1, left, right)


def finish_kernel(
    spot_ref, part_ref, rowa_ref, rowb_ref, cola_ref, colb_ref, new_ref,
):
    tile = part_ref.shape[2]
    half = LANES // 2
    first = lax.broadcasted_iota(jnp.int32, (half, LANES), 1) < half
    for piece in range(2):
        for start in range(0, tile, half):
            rows = slice(start, start + half)
            sides = beside(spot_ref, 1, cola_ref[piece, rows], colb_ref[piece, rows])
            for part in range(2):
                for block in range(2):
                    cols = slice(block * LANES, (block + 1) * LANES)
                    total = sides[block]
                    if block != part:
                        total = pltpu.roll(total, half, 1)
                    total = jnp.where(first == (block == 0), total, 0.0)
                    place = 2 * part + block
                    ends = beside(spot_ref, 0, rowa_ref[piece, place], rowb_ref[piece, place])
                    if start == 0:
                        total += ends[0]
                    if start == tile - half:
                        total += ends[1]
                    new_ref[piece, part, rows, cols] = (
                        part_ref[piece, part, rows, cols] - STEP_OBJECT * total
                    )


def probe_kernel(spot_ref, probe_ref, mine_ref, other_ref, newp_ref, *, scale):
    newp_ref[0] = probe_ref[0] - scale * pick(spot_ref, 1, mine_ref[...], other_ref[...])
    newp_ref[1] = probe_ref[1] - scale * pick(spot_ref, 1, other_ref[...], mine_ref[...])


def vmem(count):
    return [pl.BlockSpec(memory_space=pltpu.VMEM)] * count


def smem(count):
    return [pl.BlockSpec(memory_space=pltpu.SMEM)] * count


def array(*shape):
    return jax.ShapeDtypeStruct(shape, jnp.float32)


def meet(strips, axis):
    sizes = (lax.axis_size("row"), lax.axis_size("col"))
    got = []
    for odd, strip in enumerate(strips):
        pairs = []
        for spot in np.ndindex(*sizes):
            other = list(spot)
            other[axis] = (((spot[axis] + odd) ^ 1) - odd) % sizes[axis]
            pairs.append((spot[0] * sizes[1] + spot[1], other[0] * sizes[1] + other[1]))
        got.append(lax.ppermute(strip, BOTH, pairs))
    return got


def swap(value, masks):
    count = lax.axis_size("row") * lax.axis_size("col")
    return lax.ppermute(value, BOTH, [(i, i ^ masks[i % 2]) for i in range(count)])


def call(kernel, out_shape, scalars, arrays, scratch=()):
    return pl.pallas_call(
        kernel, out_shape=tuple(out_shape), in_specs=smem(len(scalars)) + vmem(len(arrays)),
        out_specs=tuple(vmem(len(out_shape))), scratch_shapes=list(scratch),
        compiler_params=pltpu.CompilerParams(vmem_limit_bytes=GRANT),
    )(*scalars, *arrays)


def on_device(object_field, probe, intensity, offset_row, offset_col, live):
    tile = object_field.shape[2]
    width = probe.shape[1]
    half = width // 2
    count = offset_row.shape[1]
    side, edge, plane = (tile, LANES), (6, half, LANES), (width, width)
    field, fields = array(2, 2, tile, tile), array(count, 2, width, width)
    place = [lax.axis_index(axis) for axis in BOTH] + [lax.axis_size(axis) for axis in BOTH]
    spot = jnp.stack([jnp.asarray(entry, jnp.int32) for entry in place]).reshape(1, 4)
    tabs = jnp.asarray(make_tables(width))
    grown = pltpu.VMEM((2, 4, tile + width, LANES), jnp.float32)
    packed = pl.pallas_call(
        pack_kernel, out_shape=tuple([array(*side)] * 4),
        in_specs=smem(1) + [pl.BlockSpec(memory_space=pltpu.HBM)], out_specs=tuple(vmem(4)),
        scratch_shapes=[pltpu.VMEM(object_field.shape, jnp.float32), pltpu.SemaphoreType.DMA((2,))],
        compiler_params=pltpu.CompilerParams(vmem_limit_bytes=GRANT),
    )(spot, pltpu.with_memory_space_constraint(object_field, pltpu.HBM))
    halos = []
    cols = [meet(packed[2 * piece : 2 * piece + 2], 1) for piece in range(2)]
    for piece in range(2):
        strips = call(
            functools.partial(rows_kernel, piece=piece), [array(*edge)] * 2,
            (spot,), (object_field, *cols[piece]),
        )
        halos.append((*cols[piece], *meet(strips, 0)))
    win, mid = call(
        first_kernel, [fields] * 2, (offset_row, offset_col, spot),
        (object_field, *halos[0], probe, tabs), (grown,),
    )
    grad, down, mine, send = call(
        second_kernel, [fields] * 2 + [array(*plane)] * 2, (offset_row, offset_col, spot, live),
        (object_field, *halos[1], win, mid, intensity[0], tabs),
        (grown, pltpu.VMEM((2, *plane), jnp.float32)),
    )
    part, *strips, left, right = call(
        place_kernel, [field] + [array(2, *edge)] * 2 + [array(2, *side)] * 2,
        (offset_row, offset_col, spot), (object_field, probe, down, grad),
        (pltpu.VMEM((2, 2, 4, tile + width, LANES), jnp.float32),),
    )
    mine = mine + swap(send, (1, 1))
    mine = mine + swap(mine, MASKS[0])
    mine, *strips = lax.optimization_barrier((mine, *strips))
    rows = meet(strips, 0)
    for mask in MASKS[1:4]:
        mine = mine + swap(mine, mask)
    strips = call(fold_kernel, [array(2, *side)] * 2, (spot,), (left, right, *rows))
    mine, *strips = lax.optimization_barrier((mine, *strips))
    cols = meet(strips, 1)
    for mask in MASKS[4:]:
        mine = mine + swap(mine, mask)
    (new,) = call(finish_kernel, (field,), (spot,), (part, *rows, *cols))
    other = swap(mine, (1, 1))
    count_all = count * lax.axis_size("row") * lax.axis_size("col")
    (new_probe,) = call(
        functools.partial(probe_kernel, scale=STEP_PROBE / count_all), (array(2, *plane),),
        (spot,), (probe, mine, other),
    )
    return new, new_probe


def solution(mesh):
    placed = (
        P(None, None, "row", "col"),
        P(),
        P("row", "col", None, None),
        P("row", "col"),
        P("row", "col"),
        P("row", "col"),
    )
    return jax.shard_map(
        on_device,
        mesh=mesh,
        in_specs=placed,
        out_specs=(P(None, None, "row", "col"), P()),
        check_vma=False,
    )
```

```python
import functools
import math

import jax
import jax.numpy as jnp
import ml_dtypes
import numpy as np
from jax import lax
from jax.experimental import pallas as pl
from jax.experimental.pallas import tpu as pltpu
from jax.sharding import PartitionSpec as P

STEP_OBJECT = 0.03
STEP_PROBE = 2.0
FRESNEL_PHASE = 60.0
LANES = 128
BOTH = ("row", "col")
GRANT = 16 * 1024 * 1024
MASKS = ((4, 32), (12, 128), (128, 130), (130, 96), (16, 4), (32, 12), (96, 16))


def split_table(table):
    high = table.astype(ml_dtypes.bfloat16)
    low = (table - high.astype(np.float64)).astype(ml_dtypes.bfloat16)
    return high, low


def make_tables(width):
    index = np.arange(width)
    four = np.exp(-2j * math.pi * (np.outer(index, index) % width) / width) / math.sqrt(width)
    freq = np.where(index < width // 2, index, index - width) / width
    hop = np.conj(four) @ np.diag(np.exp(-1j * FRESNEL_PHASE * freq**2)) @ four
    forms = []
    for table in (hop, four):
        forms.append(np.block([[table.real, table.imag], [-table.imag, table.real]]))
        forms.append(np.block([[table.real, -table.imag], [table.imag, table.real]]))
    pairs = [split_table(form) for form in forms]
    return np.stack([np.stack(pair) for pair in pairs])


def split(value):
    high = value.astype(jnp.bfloat16)
    low = (value - high.astype(jnp.float32)).astype(jnp.bfloat16)
    return high, low


def mul3(left, right):
    dot = functools.partial(jnp.dot, preferred_element_type=jnp.float32)
    return dot(left[0], right[0]) + (dot(left[1], right[0]) + dot(left[0], right[1]))


def two_sided(tabs_ref, right, left, real, imag):
    width = real.shape[1]
    starts = range(0, real.shape[0], width)
    field = split(jnp.concatenate([real, imag], axis=1))
    half = mul3(field, (tabs_ref[right, 0], tabs_ref[right, 1]))
    field = jnp.concatenate(
        [
            jnp.concatenate([half[s : s + width, :width] for s in starts], axis=1),
            jnp.concatenate([half[s : s + width, width:] for s in starts], axis=1),
        ],
        axis=0,
    )
    full = mul3((tabs_ref[left, 0], tabs_ref[left, 1]), split(field))
    return tuple(
        jnp.concatenate([full[part * width : (part + 1) * width, s : s + width] for s in starts], axis=0)
        for part in range(2)
    )


def columns(piece_ref, first):
    half = LANES // 2
    left = jnp.where(first, piece_ref[0, :, :LANES], pltpu.roll(piece_ref[1, :, :LANES], half, 1))
    right = jnp.where(first, pltpu.roll(piece_ref[0, :, LANES:], half, 1), piece_ref[1, :, LANES:])
    return left, right


def pick(spot_ref, axis, even, odd):
    return jnp.where(lax.rem(spot_ref[0, axis], 2) == 0, even, odd)


def beside(spot_ref, axis, a, b):
    place = spot_ref[0, axis]
    before = jnp.where(place == 0, 0.0, pick(spot_ref, axis, b, a))
    after = jnp.where(place == spot_ref[0, 2 + axis] - 1, 0.0, pick(spot_ref, axis, a, b))
    return before, after


def pack_piece(spot_ref, piece_ref, cola_ref, colb_ref, rowa_ref, rowb_ref):
    half = LANES // 2
    tile = piece_ref.shape[1]
    first = lax.broadcasted_iota(jnp.int32, (tile, LANES), 1) < half
    left, right = columns(piece_ref, first)
    cola_ref[...] = pick(spot_ref, 1, right, left)
    colb_ref[...] = pick(spot_ref, 1, left, right)
    for part in range(2):
        for block in range(2):
            cols = slice(block * LANES, (block + 1) * LANES)
            top, bottom = piece_ref[part, :half, cols], piece_ref[part, tile - half :, cols]
            rowa_ref[2 * part + block] = pick(spot_ref, 0, bottom, top)
            rowb_ref[2 * part + block] = pick(spot_ref, 0, top, bottom)


def pack_kernel(spot_ref, obj_ref, cola_ref, colb_ref, rowa_ref, rowb_ref, held, sem):
    copy = pltpu.make_async_copy(obj_ref.at[0], held, sem)
    copy.start()
    copy.wait()
    pack_piece(spot_ref, held, cola_ref, colb_ref, rowa_ref, rowb_ref)


def pack_next_kernel(spot_ref, obj_ref, cola_ref, colb_ref, rowa_ref, rowb_ref):
    pack_piece(spot_ref, obj_ref.at[1], cola_ref, colb_ref, rowa_ref, rowb_ref)


def corner_kernel(spot_ref, cola_ref, colb_ref, rowa_ref, rowb_ref):
    half = LANES // 2
    low, high = slice(0, half), slice(cola_ref.shape[0] - half, cola_ref.shape[0])
    tops = beside(spot_ref, 1, cola_ref[low], colb_ref[low])
    bottoms = beside(spot_ref, 1, cola_ref[high], colb_ref[high])
    for place, (top, bottom) in enumerate(zip(tops, bottoms)):
        rowa_ref[place] = pick(spot_ref, 0, bottom, top)
        rowb_ref[place] = pick(spot_ref, 0, top, bottom)


def grow(ext, spot_ref, piece_ref, cola_ref, colb_ref, rowa_ref, rowb_ref, cora_ref, corb_ref):
    half = LANES // 2
    tile = piece_ref.shape[1]
    sides = beside(spot_ref, 1, cola_ref[...], colb_ref[...])
    for part in range(2):
        for block in range(4):
            if block in (1, 2):
                place = 2 * part + block - 1
                top, bottom = beside(spot_ref, 0, rowa_ref[place], rowb_ref[place])
                middle = piece_ref[part, :, (block - 1) * LANES : block * LANES]
            else:
                place = block // 3
                top, bottom = beside(spot_ref, 0, cora_ref[place], corb_ref[place])
                middle = sides[place]
            for strip, start in ((top, 0), (middle, half), (bottom, half + tile)):
                if (block == 0 and part == 0) or (block == 3 and part == 1):
                    strip = pltpu.roll(strip, half, 1)
                ext[part, block, start : start + strip.shape[0]] = strip


def place_window(row_ref, col_ref, slot):
    col = col_ref[0, slot] + LANES // 2
    return row_ref[0, slot], col // LANES, lax.rem(col, LANES)


def window(ext, row_ref, col_ref, slot, width):
    row, block, shift = place_window(row_ref, col_ref, slot)
    back = lax.rem(LANES - shift, LANES)
    keep = lax.broadcasted_iota(jnp.int32, (width, LANES), 1) < LANES - shift
    parts = []
    for part in range(2):
        near = pltpu.roll(ext[part, block, pl.ds(row, width), :], back, 1)
        far = pltpu.roll(ext[part, block + 1, pl.ds(row, width), :], back, 1)
        parts.append(jnp.where(keep, near, far))
    return parts


def windows(ext, row_ref, col_ref, slots, width):
    got = [window(ext, row_ref, col_ref, slot, width) for slot in slots]
    return tuple(jnp.concatenate([g[part] for g in got], axis=0) for part in range(2))


def stacked(ref, slots, part):
    return jnp.concatenate([ref[slot, part] for slot in slots], axis=0)


def store(ref, slots, values):
    width = ref.shape[2]
    for place, slot in enumerate(slots):
        for part in range(2):
            ref[slot, part] = values[part][place * width : (place + 1) * width]


def first_kernel(
    row_ref, col_ref, spot_ref, obj_ref, cola_ref, colb_ref, rowa_ref, rowb_ref, cora_ref, corb_ref,
    probe_ref, tabs_ref, win_ref, mid_ref, ext, *, group,
):
    width = probe_ref.shape[1]
    grow(ext, spot_ref, obj_ref.at[0], cola_ref, colb_ref, rowa_ref, rowb_ref, cora_ref, corb_ref)

    def some(index, _):
        slots = [group * index + place for place in range(group)]
        first_re, first_im = windows(ext, row_ref, col_ref, slots, width)
        probe_re, probe_im = (jnp.concatenate([probe_ref[p]] * group, axis=0) for p in range(2))
        wave_re = probe_re * first_re - probe_im * first_im
        wave_im = probe_re * first_im + probe_im * first_re
        store(win_ref, slots, (first_re, first_im))
        store(mid_ref, slots, two_sided(tabs_ref, 0, 1, wave_re, wave_im))
        return 0

    lax.fori_loop(0, row_ref.shape[1] // group, some, 0, unroll=True)


def second_kernel(
    row_ref, col_ref, spot_ref, live_ref, obj_ref, cola_ref, colb_ref, rowa_ref, rowb_ref,
    cora_ref, corb_ref, win_ref, mid_ref, measured_ref, tabs_ref,
    grad_ref, down_ref, keep_ref, send_ref,
    ext, sum_ref, *, group,
):
    width = win_ref.shape[2]
    grow(ext, spot_ref, obj_ref.at[1], cola_ref, colb_ref, rowa_ref, rowb_ref, cora_ref, corb_ref)
    sum_ref[...] = jnp.zeros_like(sum_ref)

    def some(index, _):
        slots = [group * index + place for place in range(group)]
        second_re, second_im = windows(ext, row_ref, col_ref, slots, width)
        mid_re, mid_im = (stacked(mid_ref, slots, part) for part in range(2))
        exit_re = mid_re * second_re - mid_im * second_im
        exit_im = mid_re * second_im + mid_im * second_re
        far_re, far_im = two_sided(tabs_ref, 2, 3, exit_re, exit_im)
        weights = []
        for place, slot in enumerate(slots):
            rows = slice(place * width, (place + 1) * width)
            active = jnp.where(slot < live_ref[0, 0], 2.0, 0.0)
            power = far_re[rows] * far_re[rows] + far_im[rows] * far_im[rows]
            weights.append((power - measured_ref[slot]) * active)
        weight = jnp.concatenate(weights, axis=0)
        chi_re, chi_im = two_sided(tabs_ref, 3, 2, weight * far_re, weight * far_im)
        grad_re = mid_re * chi_re + mid_im * chi_im
        grad_im = mid_re * chi_im - mid_im * chi_re
        store(grad_ref, slots, (grad_re, grad_im))
        back_re = second_re * chi_re + second_im * chi_im
        back_im = second_re * chi_im - second_im * chi_re
        down_re, down_im = two_sided(tabs_ref, 1, 0, back_re, back_im)
        store(down_ref, slots, (down_re, down_im))
        first_re, first_im = (stacked(win_ref, slots, part) for part in range(2))
        sum_re = first_re * down_re + first_im * down_im
        sum_im = first_re * down_im - first_im * down_re
        for part, value in enumerate((sum_re, sum_im)):
            total = value[:width]
            for start in range(width, group * width, width):
                total += value[start : start + width]
            sum_ref[part] += total
        return 0

    lax.fori_loop(0, row_ref.shape[1] // group, some, 0, unroll=True)
    keep_ref[...] = pick(spot_ref, 1, sum_ref[0], sum_ref[1])
    send_ref[...] = pick(spot_ref, 1, sum_ref[1], sum_ref[0])


def place_kernel(
    row_ref, col_ref, spot_ref, obj_ref, probe_ref, down_ref, second_ref,
    new_ref, rowa_ref, rowb_ref, left_ref, right_ref,
    grad,
):
    width = probe_ref.shape[1]
    tile = obj_ref.shape[2]
    half = width // 2
    grad[...] = jnp.zeros_like(grad)
    lane = lax.broadcasted_iota(jnp.int32, (width, LANES), 1)

    def deposit(slot, _):
        row, block, shift = place_window(row_ref, col_ref, slot)
        keep = lane >= shift
        probe_re, probe_im = probe_ref[0], probe_ref[1]
        down_re, down_im = down_ref[slot, 0], down_ref[slot, 1]
        values = (
            (probe_re * down_re + probe_im * down_im, probe_re * down_im - probe_im * down_re),
            (second_ref[slot, 0], second_ref[slot, 1]),
        )
        for piece in range(2):
            for part in range(2):
                value = pltpu.roll(values[piece][part], shift, 1)
                grad[piece, part, block, pl.ds(row, width), :] += jnp.where(keep, value, 0.0)
                grad[piece, part, block + 1, pl.ds(row, width), :] += jnp.where(keep, 0.0, value)
        return 0

    lax.fori_loop(0, row_ref.shape[1], deposit, 0)
    first = lax.broadcasted_iota(jnp.int32, (tile + width, LANES), 1) < half
    for piece in range(2):
        for part in range(2):
            for block in range(2):
                cols = slice(block * LANES, (block + 1) * LANES)
                top = grad[piece, part, 1 + block, :half]
                bottom = grad[piece, part, 1 + block, half + tile :]
                rowa_ref[piece, 2 * part + block] = pick(spot_ref, 0, bottom, top)
                rowb_ref[piece, 2 * part + block] = pick(spot_ref, 0, top, bottom)
                new_ref[piece, part, :, cols] = (
                    obj_ref[piece, part, :, cols]
                    - STEP_OBJECT * grad[piece, part, 1 + block, half : half + tile]
                )
        left = jnp.where(first, pltpu.roll(grad[piece, 0, 0], half, 1), grad[piece, 1, 0])
        right = jnp.where(first, grad[piece, 0, 3], pltpu.roll(grad[piece, 1, 3], half, 1))
        for place, strip, ref in ((4, left, left_ref), (5, right, right_ref)):
            top, bottom = strip[:half], strip[half + tile :]
            rowa_ref[piece, place] = pick(spot_ref, 0, bottom, top)
            rowb_ref[piece, place] = pick(spot_ref, 0, top, bottom)
            ref[piece] = strip[half : half + tile]


def fold_kernel(spot_ref, left_ref, right_ref, rowa_ref, rowb_ref, cola_ref, colb_ref):
    half = LANES // 2
    tile = left_ref.shape[1]
    for piece in range(2):
        sides = []
        for ref, place in ((left_ref, 4), (right_ref, 5)):
            top, bottom = beside(spot_ref, 0, rowa_ref[piece, place], rowb_ref[piece, place])
            sides.append(
                (
                    ref[piece, :half] + top,
                    ref[piece, half : tile - half],
                    ref[piece, tile - half :] + bottom,
                )
            )
        for left, right, rows in zip(*sides, (slice(0, half), slice(half, tile - half), slice(tile - half, tile))):
            cola_ref[piece, rows] = pick(spot_ref, 1, right, left)
            colb_ref[piece, rows] = pick(spot_ref, 1, left, right)


def finish_kernel(
    spot_ref, part_ref, rowa_ref, rowb_ref, cola_ref, colb_ref, new_ref,
):
    tile = part_ref.shape[2]
    half = LANES // 2
    first = lax.broadcasted_iota(jnp.int32, (half, LANES), 1) < half
    for piece in range(2):
        for start in range(0, tile, half):
            rows = slice(start, start + half)
            sides = beside(spot_ref, 1, cola_ref[piece, rows], colb_ref[piece, rows])
            for part in range(2):
                for block in range(2):
                    cols = slice(block * LANES, (block + 1) * LANES)
                    total = sides[block]
                    if block != part:
                        total = pltpu.roll(total, half, 1)
                    total = jnp.where(first == (block == 0), total, 0.0)
                    place = 2 * part + block
                    ends = beside(spot_ref, 0, rowa_ref[piece, place], rowb_ref[piece, place])
                    if start == 0:
                        total += ends[0]
                    if start == tile - half:
                        total += ends[1]
                    new_ref[piece, part, rows, cols] = (
                        part_ref[piece, part, rows, cols] - STEP_OBJECT * total
                    )


def probe_kernel(spot_ref, probe_ref, mine_ref, other_ref, newp_ref, *, scale):
    newp_ref[0] = probe_ref[0] - scale * pick(spot_ref, 1, mine_ref[...], other_ref[...])
    newp_ref[1] = probe_ref[1] - scale * pick(spot_ref, 1, other_ref[...], mine_ref[...])


def vmem(count):
    return [pl.BlockSpec(memory_space=pltpu.VMEM)] * count


def smem(count):
    return [pl.BlockSpec(memory_space=pltpu.SMEM)] * count


def array(*shape):
    return jax.ShapeDtypeStruct(shape, jnp.float32)


def meet(strips, axis):
    sizes = (lax.axis_size("row"), lax.axis_size("col"))
    got = []
    for odd, strip in enumerate(strips):
        pairs = []
        for spot in np.ndindex(*sizes):
            other = list(spot)
            other[axis] = (((spot[axis] + odd) ^ 1) - odd) % sizes[axis]
            pairs.append((spot[0] * sizes[1] + spot[1], other[0] * sizes[1] + other[1]))
        got.append(lax.ppermute(strip, BOTH, pairs))
    return got


def swap(value, masks):
    count = lax.axis_size("row") * lax.axis_size("col")
    return lax.ppermute(value, BOTH, [(i, i ^ masks[i % 2]) for i in range(count)])


def call(kernel, out_shape, scalars, arrays, scratch=()):
    return pl.pallas_call(
        kernel, out_shape=tuple(out_shape), in_specs=smem(len(scalars)) + vmem(len(arrays)),
        out_specs=tuple(vmem(len(out_shape))), scratch_shapes=list(scratch),
        compiler_params=pltpu.CompilerParams(vmem_limit_bytes=GRANT),
    )(*scalars, *arrays)


def on_device(object_field, probe, intensity, offset_row, offset_col, live):
    tile = object_field.shape[2]
    width = probe.shape[1]
    half = width // 2
    count = offset_row.shape[1]
    side, edge, plane = (tile, LANES), (6, half, LANES), (width, width)
    field, fields = array(2, 2, tile, tile), array(count, 2, width, width)
    place = [lax.axis_index(axis) for axis in BOTH] + [lax.axis_size(axis) for axis in BOTH]
    spot = jnp.stack([jnp.asarray(entry, jnp.int32) for entry in place]).reshape(1, 4)
    tabs = jnp.asarray(make_tables(width))
    grown = pltpu.VMEM((2, 4, tile + width, LANES), jnp.float32)
    outer, ends = [array(*side)] * 2 + [array(4, half, LANES)] * 2, [array(2, half, LANES)] * 2
    packed = [
        pl.pallas_call(
            pack_kernel, out_shape=tuple(outer),
            in_specs=smem(1) + [pl.BlockSpec(memory_space=pltpu.HBM)], out_specs=tuple(vmem(4)),
            scratch_shapes=[pltpu.VMEM((2, tile, tile), jnp.float32), pltpu.SemaphoreType.DMA],
            compiler_params=pltpu.CompilerParams(vmem_limit_bytes=GRANT),
        )(spot, pltpu.with_memory_space_constraint(object_field, pltpu.HBM)),
        call(pack_next_kernel, outer, (spot,), (object_field,)),
    ]
    cols = [meet(strips[:2], 1) for strips in packed]
    rows = meet(packed[0][2:], 0)
    ends0 = call(corner_kernel, ends, (spot,), cols[0])
    rows[0], rows[1], *strips = lax.optimization_barrier((*rows, *packed[1][2:]))
    halos = [(*cols[0], *rows, *meet(ends0, 0))]
    rows = meet(strips, 0)
    halos.append((*cols[1], *rows, *meet(call(corner_kernel, ends, (spot,), cols[1]), 0)))
    win, mid = call(
        functools.partial(first_kernel, group=2), [fields] * 2, (offset_row, offset_col, spot),
        (object_field, *halos[0], probe, tabs), (grown,),
    )
    grad, down, mine, send = call(
        functools.partial(second_kernel, group=count), [fields] * 2 + [array(*plane)] * 2,
        (offset_row, offset_col, spot, live),
        (object_field, *halos[1], win, mid, intensity[0], tabs),
        (grown, pltpu.VMEM((2, *plane), jnp.float32)),
    )
    part, *strips, left, right = call(
        place_kernel, [field] + [array(2, *edge)] * 2 + [array(2, *side)] * 2,
        (offset_row, offset_col, spot), (object_field, probe, down, grad),
        (pltpu.VMEM((2, 2, 4, tile + width, LANES), jnp.float32),),
    )
    mine = mine + swap(send, (1, 1))
    mine = mine + swap(mine, MASKS[0])
    mine, *strips = lax.optimization_barrier((mine, *strips))
    rows = meet(strips, 0)
    for mask in MASKS[1:4]:
        mine = mine + swap(mine, mask)
    strips = call(fold_kernel, [array(2, *side)] * 2, (spot,), (left, right, *rows))
    mine, *strips = lax.optimization_barrier((mine, *strips))
    cols = meet(strips, 1)
    for mask in MASKS[4:]:
        mine = mine + swap(mine, mask)
    (new,) = call(finish_kernel, (field,), (spot,), (part, *rows, *cols))
    other = swap(mine, (1, 1))
    count_all = count * lax.axis_size("row") * lax.axis_size("col")
    (new_probe,) = call(
        functools.partial(probe_kernel, scale=STEP_PROBE / count_all), (array(2, *plane),),
        (spot,), (probe, mine, other),
    )
    return new, new_probe


def solution(mesh):
    placed = (
        P(None, None, "row", "col"),
        P(),
        P("row", "col", None, None),
        P("row", "col"),
        P("row", "col"),
        P("row", "col"),
    )
    return jax.shard_map(
        on_device,
        mesh=mesh,
        in_specs=placed,
        out_specs=(P(None, None, "row", "col"), P()),
        check_vma=False,
    )
```

```python
import functools
import math

import jax
import jax.numpy as jnp
import ml_dtypes
import numpy as np
from jax import lax
from jax.experimental import pallas as pl
from jax.experimental.pallas import tpu as pltpu
from jax.sharding import PartitionSpec as P

STEP_OBJECT = 0.03
STEP_PROBE = 2.0
FRESNEL_PHASE = 60.0
LANES = 128
BOTH = ("row", "col")
GRANT = 16 * 1024 * 1024
MASKS = ((128, 32), (4, 12), (12, 4), (130, 128), (16, 130), (32, 96), (96, 16))


def split_table(table):
    high = table.astype(ml_dtypes.bfloat16)
    low = (table - high.astype(np.float64)).astype(ml_dtypes.bfloat16)
    return high, low


def make_tables(width):
    index = np.arange(width)
    four = np.exp(-2j * math.pi * (np.outer(index, index) % width) / width) / math.sqrt(width)
    freq = np.where(index < width // 2, index, index - width) / width
    hop = np.conj(four) @ np.diag(np.exp(-1j * FRESNEL_PHASE * freq**2)) @ four
    forms = []
    for table in (hop, four):
        forms.append(np.block([[table.real, table.imag], [-table.imag, table.real]]))
        forms.append(np.block([[table.real, -table.imag], [table.imag, table.real]]))
    pairs = [split_table(form) for form in forms]
    return np.stack([np.stack(pair) for pair in pairs])


def split(value):
    high = value.astype(jnp.bfloat16)
    low = (value - high.astype(jnp.float32)).astype(jnp.bfloat16)
    return high, low


def mul3(left, right):
    dot = functools.partial(jnp.dot, preferred_element_type=jnp.float32)
    return dot(left[0], right[0]) + (dot(left[1], right[0]) + dot(left[0], right[1]))


def two_sided(tabs_ref, right, left, real, imag):
    width = real.shape[1]
    starts = range(0, real.shape[0], width)
    field = split(jnp.concatenate([real, imag], axis=1))
    half = mul3(field, (tabs_ref[right, 0], tabs_ref[right, 1]))
    field = jnp.concatenate(
        [
            jnp.concatenate([half[s : s + width, :width] for s in starts], axis=1),
            jnp.concatenate([half[s : s + width, width:] for s in starts], axis=1),
        ],
        axis=0,
    )
    full = mul3((tabs_ref[left, 0], tabs_ref[left, 1]), split(field))
    return tuple(
        jnp.concatenate([full[part * width : (part + 1) * width, s : s + width] for s in starts], axis=0)
        for part in range(2)
    )


def columns(piece_ref, first):
    half = LANES // 2
    left = jnp.where(first, piece_ref[0, :, :LANES], pltpu.roll(piece_ref[1, :, :LANES], half, 1))
    right = jnp.where(first, pltpu.roll(piece_ref[0, :, LANES:], half, 1), piece_ref[1, :, LANES:])
    return left, right


def pick(spot_ref, axis, even, odd):
    return jnp.where(lax.rem(spot_ref[0, axis], 2) == 0, even, odd)


def beside(spot_ref, axis, a, b):
    place = spot_ref[0, axis]
    before = jnp.where(place == 0, 0.0, pick(spot_ref, axis, b, a))
    after = jnp.where(place == spot_ref[0, 2 + axis] - 1, 0.0, pick(spot_ref, axis, a, b))
    return before, after


def pack_kernel(spot_ref, obj_ref, cola_ref, colb_ref, rowa_ref, rowb_ref, held, sems):
    half = LANES // 2
    tile = held.shape[2]
    first = lax.broadcasted_iota(jnp.int32, (tile, LANES), 1) < half
    copies = [pltpu.make_async_copy(obj_ref.at[p], held.at[p], sems.at[p]) for p in range(2)]
    for copy in copies:
        copy.start()
    for piece in range(2):
        copies[piece].wait()
        left, right = columns(held.at[piece], first)
        cola_ref[piece] = pick(spot_ref, 1, right, left)
        colb_ref[piece] = pick(spot_ref, 1, left, right)
        for part in range(2):
            for block in range(2):
                cols = slice(block * LANES, (block + 1) * LANES)
                top = held[piece, part, :half, cols]
                bottom = held[piece, part, tile - half :, cols]
                rowa_ref[piece, 2 * part + block] = pick(spot_ref, 0, bottom, top)
                rowb_ref[piece, 2 * part + block] = pick(spot_ref, 0, top, bottom)


def corner_kernel(spot_ref, cola_ref, colb_ref, rowa_ref, rowb_ref):
    half = LANES // 2
    low, high = slice(0, half), slice(cola_ref.shape[1] - half, cola_ref.shape[1])
    for piece in range(2):
        tops = beside(spot_ref, 1, cola_ref[piece, low], colb_ref[piece, low])
        bottoms = beside(spot_ref, 1, cola_ref[piece, high], colb_ref[piece, high])
        for place, (top, bottom) in enumerate(zip(tops, bottoms)):
            rowa_ref[piece, place] = pick(spot_ref, 0, bottom, top)
            rowb_ref[piece, place] = pick(spot_ref, 0, top, bottom)


def grow(ext, spot_ref, *refs):
    piece_ref, cola_ref, colb_ref, rowa_ref, rowb_ref, cora_ref, corb_ref = refs
    half = LANES // 2
    tile = piece_ref.shape[1]
    sides = beside(spot_ref, 1, cola_ref[...], colb_ref[...])
    for part in range(2):
        for block in range(4):
            if block in (1, 2):
                place = 2 * part + block - 1
                top, bottom = beside(spot_ref, 0, rowa_ref[place], rowb_ref[place])
                middle = piece_ref[part, :, (block - 1) * LANES : block * LANES]
            else:
                place = block // 3
                top, bottom = beside(spot_ref, 0, cora_ref[place], corb_ref[place])
                middle = sides[place]
            for strip, start in ((top, 0), (middle, half), (bottom, half + tile)):
                if (block == 0 and part == 0) or (block == 3 and part == 1):
                    strip = pltpu.roll(strip, half, 1)
                ext[part, block, start : start + strip.shape[0]] = strip


def place_window(row_ref, col_ref, slot):
    col = col_ref[0, slot] + LANES // 2
    return row_ref[0, slot], col // LANES, lax.rem(col, LANES)


def window(ext, row_ref, col_ref, slot, width):
    row, block, shift = place_window(row_ref, col_ref, slot)
    back = lax.rem(LANES - shift, LANES)
    keep = lax.broadcasted_iota(jnp.int32, (width, LANES), 1) < LANES - shift
    parts = []
    for part in range(2):
        near = pltpu.roll(ext[part, block, pl.ds(row, width), :], back, 1)
        far = pltpu.roll(ext[part, block + 1, pl.ds(row, width), :], back, 1)
        parts.append(jnp.where(keep, near, far))
    return parts


def windows(ext, row_ref, col_ref, slots, width):
    got = [window(ext, row_ref, col_ref, slot, width) for slot in slots]
    return tuple(jnp.concatenate([g[part] for g in got], axis=0) for part in range(2))


def stacked(ref, slots, part):
    return jnp.concatenate([ref[slot, part] for slot in slots], axis=0)


def store(ref, slots, values):
    width = ref.shape[2]
    for place, slot in enumerate(slots):
        for part in range(2):
            ref[slot, part] = values[part][place * width : (place + 1) * width]


def first_kernel(
    row_ref, col_ref, spot_ref, obj_ref, cola_ref, colb_ref, rowa_ref, rowb_ref, cora_ref, corb_ref,
    probe_ref, tabs_ref, win_ref, mid_ref, ext, *, group,
):
    width = probe_ref.shape[1]
    refs = (obj_ref, cola_ref, colb_ref, rowa_ref, rowb_ref, cora_ref, corb_ref)
    grow(ext, spot_ref, *[ref.at[0] for ref in refs])

    def some(index, _):
        slots = [group * index + place for place in range(group)]
        first_re, first_im = windows(ext, row_ref, col_ref, slots, width)
        probe_re, probe_im = (jnp.concatenate([probe_ref[p]] * group, axis=0) for p in range(2))
        wave_re = probe_re * first_re - probe_im * first_im
        wave_im = probe_re * first_im + probe_im * first_re
        store(win_ref, slots, (first_re, first_im))
        store(mid_ref, slots, two_sided(tabs_ref, 0, 1, wave_re, wave_im))
        return 0

    lax.fori_loop(0, row_ref.shape[1] // group, some, 0, unroll=True)


def second_kernel(
    row_ref, col_ref, spot_ref, live_ref, obj_ref, cola_ref, colb_ref, rowa_ref, rowb_ref,
    cora_ref, corb_ref, win_ref, mid_ref, measured_ref, tabs_ref,
    grad_ref, down_ref, keep_ref, send_ref,
    ext, sum_ref, *, group,
):
    width = win_ref.shape[2]
    refs = (obj_ref, cola_ref, colb_ref, rowa_ref, rowb_ref, cora_ref, corb_ref)
    grow(ext, spot_ref, *[ref.at[1] for ref in refs])
    sum_ref[...] = jnp.zeros_like(sum_ref)

    def some(index, _):
        slots = [group * index + place for place in range(group)]
        second_re, second_im = windows(ext, row_ref, col_ref, slots, width)
        mid_re, mid_im = (stacked(mid_ref, slots, part) for part in range(2))
        exit_re = mid_re * second_re - mid_im * second_im
        exit_im = mid_re * second_im + mid_im * second_re
        far_re, far_im = two_sided(tabs_ref, 2, 3, exit_re, exit_im)
        weights = []
        for place, slot in enumerate(slots):
            rows = slice(place * width, (place + 1) * width)
            active = jnp.where(slot < live_ref[0, 0], 2.0, 0.0)
            power = far_re[rows] * far_re[rows] + far_im[rows] * far_im[rows]
            weights.append((power - measured_ref[slot]) * active)
        weight = jnp.concatenate(weights, axis=0)
        chi_re, chi_im = two_sided(tabs_ref, 3, 2, weight * far_re, weight * far_im)
        grad_re = mid_re * chi_re + mid_im * chi_im
        grad_im = mid_re * chi_im - mid_im * chi_re
        store(grad_ref, slots, (grad_re, grad_im))
        back_re = second_re * chi_re + second_im * chi_im
        back_im = second_re * chi_im - second_im * chi_re
        down_re, down_im = two_sided(tabs_ref, 1, 0, back_re, back_im)
        store(down_ref, slots, (down_re, down_im))
        first_re, first_im = (stacked(win_ref, slots, part) for part in range(2))
        sum_re = first_re * down_re + first_im * down_im
        sum_im = first_re * down_im - first_im * down_re
        for part, value in enumerate((sum_re, sum_im)):
            total = value[:width]
            for start in range(width, group * width, width):
                total += value[start : start + width]
            sum_ref[part] += total
        return 0

    lax.fori_loop(0, row_ref.shape[1] // group, some, 0, unroll=True)
    keep_ref[...] = pick(spot_ref, 1, sum_ref[0], sum_ref[1])
    send_ref[...] = pick(spot_ref, 1, sum_ref[1], sum_ref[0])


def place_kernel(
    row_ref, col_ref, spot_ref, obj_ref, probe_ref, down_ref, second_ref,
    new_ref, rowa_ref, rowb_ref, left_ref, right_ref,
    grad,
):
    width = probe_ref.shape[1]
    tile = obj_ref.shape[2]
    half = width // 2
    grad[...] = jnp.zeros_like(grad)
    lane = lax.broadcasted_iota(jnp.int32, (width, LANES), 1)

    def deposit(slot, _):
        row, block, shift = place_window(row_ref, col_ref, slot)
        keep = lane >= shift
        probe_re, probe_im = probe_ref[0], probe_ref[1]
        down_re, down_im = down_ref[slot, 0], down_ref[slot, 1]
        values = (
            (probe_re * down_re + probe_im * down_im, probe_re * down_im - probe_im * down_re),
            (second_ref[slot, 0], second_ref[slot, 1]),
        )
        for piece in range(2):
            for part in range(2):
                value = pltpu.roll(values[piece][part], shift, 1)
                grad[piece, part, block, pl.ds(row, width), :] += jnp.where(keep, value, 0.0)
                grad[piece, part, block + 1, pl.ds(row, width), :] += jnp.where(keep, 0.0, value)
        return 0

    lax.fori_loop(0, row_ref.shape[1], deposit, 0)
    first = lax.broadcasted_iota(jnp.int32, (tile + width, LANES), 1) < half
    for piece in range(2):
        for part in range(2):
            for block in range(2):
                cols = slice(block * LANES, (block + 1) * LANES)
                top = grad[piece, part, 1 + block, :half]
                bottom = grad[piece, part, 1 + block, half + tile :]
                rowa_ref[piece, 2 * part + block] = pick(spot_ref, 0, bottom, top)
                rowb_ref[piece, 2 * part + block] = pick(spot_ref, 0, top, bottom)
                new_ref[piece, part, :, cols] = (
                    obj_ref[piece, part, :, cols]
                    - STEP_OBJECT * grad[piece, part, 1 + block, half : half + tile]
                )
        left = jnp.where(first, pltpu.roll(grad[piece, 0, 0], half, 1), grad[piece, 1, 0])
        right = jnp.where(first, grad[piece, 0, 3], pltpu.roll(grad[piece, 1, 3], half, 1))
        for place, strip, ref in ((4, left, left_ref), (5, right, right_ref)):
            top, bottom = strip[:half], strip[half + tile :]
            rowa_ref[piece, place] = pick(spot_ref, 0, bottom, top)
            rowb_ref[piece, place] = pick(spot_ref, 0, top, bottom)
            ref[piece] = strip[half : half + tile]


def fold_kernel(spot_ref, left_ref, right_ref, rowa_ref, rowb_ref, cola_ref, colb_ref):
    half = LANES // 2
    tile = left_ref.shape[1]
    for piece in range(2):
        sides = []
        for ref, place in ((left_ref, 4), (right_ref, 5)):
            top, bottom = beside(spot_ref, 0, rowa_ref[piece, place], rowb_ref[piece, place])
            sides.append(
                (
                    ref[piece, :half] + top,
                    ref[piece, half : tile - half],
                    ref[piece, tile - half :] + bottom,
                )
            )
        for left, right, rows in zip(*sides, (slice(0, half), slice(half, tile - half), slice(tile - half, tile))):
            cola_ref[piece, rows] = pick(spot_ref, 1, right, left)
            colb_ref[piece, rows] = pick(spot_ref, 1, left, right)


def finish_kernel(
    spot_ref, part_ref, rowa_ref, rowb_ref, cola_ref, colb_ref, new_ref,
):
    tile = part_ref.shape[2]
    half = LANES // 2
    first = lax.broadcasted_iota(jnp.int32, (half, LANES), 1) < half
    for piece in range(2):
        for start in range(0, tile, half):
            rows = slice(start, start + half)
            sides = beside(spot_ref, 1, cola_ref[piece, rows], colb_ref[piece, rows])
            for part in range(2):
                for block in range(2):
                    cols = slice(block * LANES, (block + 1) * LANES)
                    total = sides[block]
                    if block != part:
                        total = pltpu.roll(total, half, 1)
                    total = jnp.where(first == (block == 0), total, 0.0)
                    place = 2 * part + block
                    ends = beside(spot_ref, 0, rowa_ref[piece, place], rowb_ref[piece, place])
                    if start == 0:
                        total += ends[0]
                    if start == tile - half:
                        total += ends[1]
                    new_ref[piece, part, rows, cols] = (
                        part_ref[piece, part, rows, cols] - STEP_OBJECT * total
                    )


def probe_kernel(spot_ref, probe_ref, mine_ref, other_ref, newp_ref, *, scale):
    newp_ref[0] = probe_ref[0] - scale * pick(spot_ref, 1, mine_ref[...], other_ref[...])
    newp_ref[1] = probe_ref[1] - scale * pick(spot_ref, 1, other_ref[...], mine_ref[...])


def vmem(count):
    return [pl.BlockSpec(memory_space=pltpu.VMEM)] * count


def smem(count):
    return [pl.BlockSpec(memory_space=pltpu.SMEM)] * count


def array(*shape):
    return jax.ShapeDtypeStruct(shape, jnp.float32)


def meet(strips, axis):
    sizes = (lax.axis_size("row"), lax.axis_size("col"))
    got = []
    for odd, strip in enumerate(strips):
        pairs = []
        for spot in np.ndindex(*sizes):
            other = list(spot)
            other[axis] = (((spot[axis] + odd) ^ 1) - odd) % sizes[axis]
            pairs.append((spot[0] * sizes[1] + spot[1], other[0] * sizes[1] + other[1]))
        got.append(lax.ppermute(strip, BOTH, pairs))
    return got


def swap(value, masks):
    count = lax.axis_size("row") * lax.axis_size("col")
    return lax.ppermute(value, BOTH, [(i, i ^ masks[i % 2]) for i in range(count)])


def call(kernel, out_shape, scalars, arrays, scratch=()):
    return pl.pallas_call(
        kernel, out_shape=tuple(out_shape), in_specs=smem(len(scalars)) + vmem(len(arrays)),
        out_specs=tuple(vmem(len(out_shape))), scratch_shapes=list(scratch),
        compiler_params=pltpu.CompilerParams(vmem_limit_bytes=GRANT),
    )(*scalars, *arrays)


def on_device(object_field, probe, intensity, offset_row, offset_col, live):
    tile = object_field.shape[2]
    width = probe.shape[1]
    half = width // 2
    count = offset_row.shape[1]
    side, edge, plane = (tile, LANES), (6, half, LANES), (width, width)
    field, fields = array(2, 2, tile, tile), array(count, 2, width, width)
    place = [lax.axis_index(axis) for axis in BOTH] + [lax.axis_size(axis) for axis in BOTH]
    spot = jnp.stack([jnp.asarray(entry, jnp.int32) for entry in place]).reshape(1, 4)
    tabs = jnp.asarray(make_tables(width))
    grown = pltpu.VMEM((2, 4, tile + width, LANES), jnp.float32)
    packed = pl.pallas_call(
        pack_kernel, out_shape=tuple([array(2, *side)] * 2 + [array(2, 4, half, LANES)] * 2),
        in_specs=smem(1) + [pl.BlockSpec(memory_space=pltpu.HBM)], out_specs=tuple(vmem(4)),
        scratch_shapes=[pltpu.VMEM((2, 2, tile, tile), jnp.float32), pltpu.SemaphoreType.DMA((2,))],
        compiler_params=pltpu.CompilerParams(vmem_limit_bytes=GRANT),
    )(spot, pltpu.with_memory_space_constraint(object_field, pltpu.HBM))
    cols, rows = meet(packed[:2], 1), meet(packed[2:], 0)
    corners = meet(call(corner_kernel, [array(2, 2, half, LANES)] * 2, (spot,), cols), 0)
    halo = (*cols, *rows, *corners)
    win, mid = call(
        functools.partial(first_kernel, group=2), [fields] * 2, (offset_row, offset_col, spot),
        (object_field, *halo, probe, tabs), (grown,),
    )
    grad, down, mine, send = call(
        functools.partial(second_kernel, group=count), [fields] * 2 + [array(*plane)] * 2,
        (offset_row, offset_col, spot, live),
        (object_field, *halo, win, mid, intensity[0], tabs),
        (grown, pltpu.VMEM((2, *plane), jnp.float32)),
    )
    part, *strips, left, right = call(
        place_kernel, [field] + [array(2, *edge)] * 2 + [array(2, *side)] * 2,
        (offset_row, offset_col, spot), (object_field, probe, down, grad),
        (pltpu.VMEM((2, 2, 4, tile + width, LANES), jnp.float32),),
    )
    mine = mine + swap(send, (1, 1))
    mine = mine + swap(mine, MASKS[0])
    mine, strips[0] = lax.optimization_barrier((mine, strips[0]))
    mine = mine + swap(mine, MASKS[1])
    mine, strips[1] = lax.optimization_barrier((mine, strips[1]))
    rows = meet(strips, 0)
    for mask in MASKS[2:4]:
        mine = mine + swap(mine, mask)
    mine, *rows = lax.optimization_barrier((mine, *rows))
    strips = call(fold_kernel, [array(2, *side)] * 2, (spot,), (left, right, *rows))
    mine = mine + swap(mine, MASKS[4])
    mine, *strips = lax.optimization_barrier((mine, *strips))
    cols = meet(strips, 1)
    for mask in MASKS[5:]:
        mine = mine + swap(mine, mask)
    mine, *cols = lax.optimization_barrier((mine, *cols))
    (new,) = call(finish_kernel, (field,), (spot,), (part, *rows, *cols))
    other = swap(mine, (1, 1))
    count_all = count * lax.axis_size("row") * lax.axis_size("col")
    (new_probe,) = call(
        functools.partial(probe_kernel, scale=STEP_PROBE / count_all), (array(2, *plane),),
        (spot,), (probe, mine, other),
    )
    return new, new_probe


def solution(mesh):
    placed = (
        P(None, None, "row", "col"),
        P(),
        P("row", "col", None, None),
        P("row", "col"),
        P("row", "col"),
        P("row", "col"),
    )
    return jax.shard_map(
        on_device,
        mesh=mesh,
        in_specs=placed,
        out_specs=(P(None, None, "row", "col"), P()),
        check_vma=False,
    )
```

```python
import functools
import math

import jax
import jax.numpy as jnp
import ml_dtypes
import numpy as np
from jax import lax
from jax.experimental import pallas as pl
from jax.experimental.pallas import tpu as pltpu
from jax.sharding import PartitionSpec as P

STEP_OBJECT = 0.03
STEP_PROBE = 2.0
FRESNEL_PHASE = 60.0
LANES = 128
BOTH = ("row", "col")
GRANT = 16 * 1024 * 1024
MASKS = ((128, 4), (4, 12), (12, 128), (130, 130), (16, 32), (32, 96), (96, 16))


def split_table(table):
    high = table.astype(ml_dtypes.bfloat16)
    low = (table - high.astype(np.float64)).astype(ml_dtypes.bfloat16)
    return high, low


def make_tables(width):
    index = np.arange(width)
    four = np.exp(-2j * math.pi * (np.outer(index, index) % width) / width) / math.sqrt(width)
    freq = np.where(index < width // 2, index, index - width) / width
    hop = np.conj(four) @ np.diag(np.exp(-1j * FRESNEL_PHASE * freq**2)) @ four
    forms = []
    for table in (hop, four):
        forms.append(np.block([[table.real, table.imag], [-table.imag, table.real]]))
        forms.append(np.block([[table.real, -table.imag], [table.imag, table.real]]))
    pairs = [split_table(form) for form in forms]
    return np.stack([np.stack(pair) for pair in pairs])


def split(value):
    high = value.astype(jnp.bfloat16)
    low = (value - high.astype(jnp.float32)).astype(jnp.bfloat16)
    return high, low


def mul3(left, right):
    dot = functools.partial(jnp.dot, preferred_element_type=jnp.float32)
    return dot(left[0], right[0]) + (dot(left[1], right[0]) + dot(left[0], right[1]))


def two_sided(tabs_ref, right, left, real, imag):
    width = real.shape[1]
    starts = range(0, real.shape[0], width)
    field = split(jnp.concatenate([real, imag], axis=1))
    half = mul3(field, (tabs_ref[right, 0], tabs_ref[right, 1]))
    field = jnp.concatenate(
        [
            jnp.concatenate([half[s : s + width, :width] for s in starts], axis=1),
            jnp.concatenate([half[s : s + width, width:] for s in starts], axis=1),
        ],
        axis=0,
    )
    full = mul3((tabs_ref[left, 0], tabs_ref[left, 1]), split(field))
    return tuple(
        jnp.concatenate([full[part * width : (part + 1) * width, s : s + width] for s in starts], axis=0)
        for part in range(2)
    )


def columns(piece_ref, first):
    half = LANES // 2
    left = jnp.where(first, piece_ref[0, :, :LANES], pltpu.roll(piece_ref[1, :, :LANES], half, 1))
    right = jnp.where(first, pltpu.roll(piece_ref[0, :, LANES:], half, 1), piece_ref[1, :, LANES:])
    return left, right


def pick(spot_ref, axis, even, odd):
    return jnp.where(lax.rem(spot_ref[0, axis], 2) == 0, even, odd)


def beside(spot_ref, axis, a, b):
    place = spot_ref[0, axis]
    before = jnp.where(place == 0, 0.0, pick(spot_ref, axis, b, a))
    after = jnp.where(place == spot_ref[0, 2 + axis] - 1, 0.0, pick(spot_ref, axis, a, b))
    return before, after


def pack_kernel(spot_ref, obj_ref, *refs):
    *outs, held, sems = refs
    first = lax.broadcasted_iota(jnp.int32, (held.shape[2], LANES), 1) < LANES // 2
    copies = [pltpu.make_async_copy(obj_ref.at[p], held.at[p], sems.at[p]) for p in range(2)]
    for copy in copies:
        copy.start()
    for piece in range(2):
        copies[piece].wait()
        left, right = columns(held.at[piece], first)
        outs[2 * piece][...] = pick(spot_ref, 1, right, left)
        outs[2 * piece + 1][...] = pick(spot_ref, 1, left, right)


def rows_kernel(spot_ref, obj_ref, cola_ref, colb_ref, rowa_ref, rowb_ref, *, piece):
    half = LANES // 2
    low, high = slice(0, half), slice(obj_ref.shape[2] - half, obj_ref.shape[2])
    for part in range(2):
        for block in range(2):
            cols = slice(block * LANES, (block + 1) * LANES)
            top, bottom = obj_ref[piece, part, low, cols], obj_ref[piece, part, high, cols]
            rowa_ref[2 * part + block] = pick(spot_ref, 0, bottom, top)
            rowb_ref[2 * part + block] = pick(spot_ref, 0, top, bottom)
    tops = beside(spot_ref, 1, cola_ref[low], colb_ref[low])
    bottoms = beside(spot_ref, 1, cola_ref[high], colb_ref[high])
    for place, top, bottom in zip((4, 5), tops, bottoms):
        rowa_ref[place] = pick(spot_ref, 0, bottom, top)
        rowb_ref[place] = pick(spot_ref, 0, top, bottom)


def grow(ext, spot_ref, piece_ref, cola_ref, colb_ref, rowa_ref, rowb_ref):
    half = LANES // 2
    tile = piece_ref.shape[1]
    sides = beside(spot_ref, 1, cola_ref[...], colb_ref[...])
    for part in range(2):
        for block in range(4):
            place = 2 * part + block - 1 if block in (1, 2) else 4 + block // 3
            top, bottom = beside(spot_ref, 0, rowa_ref[place], rowb_ref[place])
            if block in (1, 2):
                middle = piece_ref[part, :, (block - 1) * LANES : block * LANES]
            else:
                middle = sides[block // 3]
            for strip, start in ((top, 0), (middle, half), (bottom, half + tile)):
                if (block == 0 and part == 0) or (block == 3 and part == 1):
                    strip = pltpu.roll(strip, half, 1)
                ext[part, block, start : start + strip.shape[0]] = strip


def place_window(row_ref, col_ref, slot):
    col = col_ref[0, slot] + LANES // 2
    return row_ref[0, slot], col // LANES, lax.rem(col, LANES)


def window(ext, row_ref, col_ref, slot, width):
    row, block, shift = place_window(row_ref, col_ref, slot)
    back = lax.rem(LANES - shift, LANES)
    keep = lax.broadcasted_iota(jnp.int32, (width, LANES), 1) < LANES - shift
    parts = []
    for part in range(2):
        near = pltpu.roll(ext[part, block, pl.ds(row, width), :], back, 1)
        far = pltpu.roll(ext[part, block + 1, pl.ds(row, width), :], back, 1)
        parts.append(jnp.where(keep, near, far))
    return parts


def windows(ext, row_ref, col_ref, slots, width):
    got = [window(ext, row_ref, col_ref, slot, width) for slot in slots]
    return tuple(jnp.concatenate([g[part] for g in got], axis=0) for part in range(2))


def stacked(ref, slots, part):
    return jnp.concatenate([ref[slot, part] for slot in slots], axis=0)


def store(ref, slots, values):
    width = ref.shape[2]
    for place, slot in enumerate(slots):
        for part in range(2):
            ref[slot, part] = values[part][place * width : (place + 1) * width]


def first_kernel(
    row_ref, col_ref, spot_ref, obj_ref, cola_ref, colb_ref, rowa_ref, rowb_ref, probe_ref, tabs_ref,
    win_ref, mid_ref, ext, *, group,
):
    width = probe_ref.shape[1]
    grow(ext, spot_ref, obj_ref.at[0], cola_ref, colb_ref, rowa_ref, rowb_ref)

    def some(index, _):
        slots = [group * index + place for place in range(group)]
        first_re, first_im = windows(ext, row_ref, col_ref, slots, width)
        probe_re, probe_im = (jnp.concatenate([probe_ref[p]] * group, axis=0) for p in range(2))
        wave_re = probe_re * first_re - probe_im * first_im
        wave_im = probe_re * first_im + probe_im * first_re
        store(win_ref, slots, (first_re, first_im))
        store(mid_ref, slots, two_sided(tabs_ref, 0, 1, wave_re, wave_im))
        return 0

    lax.fori_loop(0, row_ref.shape[1] // group, some, 0, unroll=True)


def second_kernel(
    row_ref, col_ref, spot_ref, live_ref, obj_ref, cola_ref, colb_ref, rowa_ref, rowb_ref,
    win_ref, mid_ref, measured_ref, tabs_ref,
    grad_ref, down_ref, keep_ref, send_ref,
    ext, sum_ref, *, group,
):
    width = win_ref.shape[2]
    grow(ext, spot_ref, obj_ref.at[1], cola_ref, colb_ref, rowa_ref, rowb_ref)
    sum_ref[...] = jnp.zeros_like(sum_ref)

    def some(index, _):
        slots = [group * index + place for place in range(group)]
        second_re, second_im = windows(ext, row_ref, col_ref, slots, width)
        mid_re, mid_im = (stacked(mid_ref, slots, part) for part in range(2))
        exit_re = mid_re * second_re - mid_im * second_im
        exit_im = mid_re * second_im + mid_im * second_re
        far_re, far_im = two_sided(tabs_ref, 2, 3, exit_re, exit_im)
        weights = []
        for place, slot in enumerate(slots):
            rows = slice(place * width, (place + 1) * width)
            active = jnp.where(slot < live_ref[0, 0], 2.0, 0.0)
            power = far_re[rows] * far_re[rows] + far_im[rows] * far_im[rows]
            weights.append((power - measured_ref[slot]) * active)
        weight = jnp.concatenate(weights, axis=0)
        chi_re, chi_im = two_sided(tabs_ref, 3, 2, weight * far_re, weight * far_im)
        grad_re = mid_re * chi_re + mid_im * chi_im
        grad_im = mid_re * chi_im - mid_im * chi_re
        store(grad_ref, slots, (grad_re, grad_im))
        back_re = second_re * chi_re + second_im * chi_im
        back_im = second_re * chi_im - second_im * chi_re
        down_re, down_im = two_sided(tabs_ref, 1, 0, back_re, back_im)
        store(down_ref, slots, (down_re, down_im))
        first_re, first_im = (stacked(win_ref, slots, part) for part in range(2))
        sum_re = first_re * down_re + first_im * down_im
        sum_im = first_re * down_im - first_im * down_re
        for part, value in enumerate((sum_re, sum_im)):
            total = value[:width]
            for start in range(width, group * width, width):
                total += value[start : start + width]
            sum_ref[part] += total
        return 0

    lax.fori_loop(0, row_ref.shape[1] // group, some, 0, unroll=True)
    keep_ref[...] = pick(spot_ref, 1, sum_ref[0], sum_ref[1])
    send_ref[...] = pick(spot_ref, 1, sum_ref[1], sum_ref[0])


def place_kernel(
    row_ref, col_ref, spot_ref, obj_ref, probe_ref, down_ref, second_ref,
    new_ref, rowa_ref, rowb_ref, left_ref, right_ref,
    grad,
):
    width = probe_ref.shape[1]
    tile = obj_ref.shape[2]
    half = width // 2
    grad[...] = jnp.zeros_like(grad)
    lane = lax.broadcasted_iota(jnp.int32, (width, LANES), 1)

    def deposit(slot, _):
        row, block, shift = place_window(row_ref, col_ref, slot)
        keep = lane >= shift
        probe_re, probe_im = probe_ref[0], probe_ref[1]
        down_re, down_im = down_ref[slot, 0], down_ref[slot, 1]
        values = (
            (probe_re * down_re + probe_im * down_im, probe_re * down_im - probe_im * down_re),
            (second_ref[slot, 0], second_ref[slot, 1]),
        )
        for piece in range(2):
            for part in range(2):
                value = pltpu.roll(values[piece][part], shift, 1)
                grad[piece, part, block, pl.ds(row, width), :] += jnp.where(keep, value, 0.0)
                grad[piece, part, block + 1, pl.ds(row, width), :] += jnp.where(keep, 0.0, value)
        return 0

    lax.fori_loop(0, row_ref.shape[1], deposit, 0)
    first = lax.broadcasted_iota(jnp.int32, (tile + width, LANES), 1) < half
    for piece in range(2):
        for part in range(2):
            for block in range(2):
                cols = slice(block * LANES, (block + 1) * LANES)
                top = grad[piece, part, 1 + block, :half]
                bottom = grad[piece, part, 1 + block, half + tile :]
                rowa_ref[piece, 2 * part + block] = pick(spot_ref, 0, bottom, top)
                rowb_ref[piece, 2 * part + block] = pick(spot_ref, 0, top, bottom)
                new_ref[piece, part, :, cols] = (
                    obj_ref[piece, part, :, cols]
                    - STEP_OBJECT * grad[piece, part, 1 + block, half : half + tile]
                )
        left = jnp.where(first, pltpu.roll(grad[piece, 0, 0], half, 1), grad[piece, 1, 0])
        right = jnp.where(first, grad[piece, 0, 3], pltpu.roll(grad[piece, 1, 3], half, 1))
        for place, strip, ref in ((4, left, left_ref), (5, right, right_ref)):
            top, bottom = strip[:half], strip[half + tile :]
            rowa_ref[piece, place] = pick(spot_ref, 0, bottom, top)
            rowb_ref[piece, place] = pick(spot_ref, 0, top, bottom)
            ref[piece] = strip[half : half + tile]


def fold_kernel(spot_ref, left_ref, right_ref, rowa_ref, rowb_ref, cola_ref, colb_ref):
    half = LANES // 2
    tile = left_ref.shape[1]
    for piece in range(2):
        sides = []
        for ref, place in ((left_ref, 4), (right_ref, 5)):
            top, bottom = beside(spot_ref, 0, rowa_ref[piece, place], rowb_ref[piece, place])
            sides.append(
                (
                    ref[piece, :half] + top,
                    ref[piece, half : tile - half],
                    ref[piece, tile - half :] + bottom,
                )
            )
        for left, right, rows in zip(*sides, (slice(0, half), slice(half, tile - half), slice(tile - half, tile))):
            cola_ref[piece, rows] = pick(spot_ref, 1, right, left)
            colb_ref[piece, rows] = pick(spot_ref, 1, left, right)


def finish_kernel(
    spot_ref, part_ref, rowa_ref, rowb_ref, cola_ref, colb_ref, new_ref,
):
    tile = part_ref.shape[2]
    half = LANES // 2
    first = lax.broadcasted_iota(jnp.int32, (half, LANES), 1) < half
    for piece in range(2):
        for start in range(0, tile, half):
            rows = slice(start, start + half)
            sides = beside(spot_ref, 1, cola_ref[piece, rows], colb_ref[piece, rows])
            for part in range(2):
                for block in range(2):
                    cols = slice(block * LANES, (block + 1) * LANES)
                    total = sides[block]
                    if block != part:
                        total = pltpu.roll(total, half, 1)
                    total = jnp.where(first == (block == 0), total, 0.0)
                    place = 2 * part + block
                    ends = beside(spot_ref, 0, rowa_ref[piece, place], rowb_ref[piece, place])
                    if start == 0:
                        total += ends[0]
                    if start == tile - half:
                        total += ends[1]
                    new_ref[piece, part, rows, cols] = (
                        part_ref[piece, part, rows, cols] - STEP_OBJECT * total
                    )


def probe_kernel(spot_ref, probe_ref, mine_ref, other_ref, newp_ref, *, scale):
    newp_ref[0] = probe_ref[0] - scale * pick(spot_ref, 1, mine_ref[...], other_ref[...])
    newp_ref[1] = probe_ref[1] - scale * pick(spot_ref, 1, other_ref[...], mine_ref[...])


def vmem(count):
    return [pl.BlockSpec(memory_space=pltpu.VMEM)] * count


def smem(count):
    return [pl.BlockSpec(memory_space=pltpu.SMEM)] * count


def array(*shape):
    return jax.ShapeDtypeStruct(shape, jnp.float32)


def meet(strips, axis):
    sizes = (lax.axis_size("row"), lax.axis_size("col"))
    got = []
    for odd, strip in enumerate(strips):
        pairs = []
        for spot in np.ndindex(*sizes):
            other = list(spot)
            place = ((spot[axis] + odd) ^ 1) - odd
            if 0 <= place < sizes[axis]:
                other[axis] = place
            pairs.append((spot[0] * sizes[1] + spot[1], other[0] * sizes[1] + other[1]))
        got.append(lax.ppermute(strip, BOTH, pairs))
    return got


def swap(value, masks):
    count = lax.axis_size("row") * lax.axis_size("col")
    return lax.ppermute(value, BOTH, [(i, i ^ masks[i % 2]) for i in range(count)])


def call(kernel, out_shape, scalars, arrays, scratch=()):
    return pl.pallas_call(
        kernel, out_shape=tuple(out_shape), in_specs=smem(len(scalars)) + vmem(len(arrays)),
        out_specs=tuple(vmem(len(out_shape))), scratch_shapes=list(scratch),
        compiler_params=pltpu.CompilerParams(vmem_limit_bytes=GRANT),
    )(*scalars, *arrays)


def on_device(object_field, probe, intensity, offset_row, offset_col, live):
    tile = object_field.shape[2]
    width = probe.shape[1]
    half = width // 2
    count = offset_row.shape[1]
    side, edge, plane = (tile, LANES), (6, half, LANES), (width, width)
    field, fields = array(2, 2, tile, tile), array(count, 2, width, width)
    place = [lax.axis_index(axis) for axis in BOTH] + [lax.axis_size(axis) for axis in BOTH]
    spot = jnp.stack([jnp.asarray(entry, jnp.int32) for entry in place]).reshape(1, 4)
    tabs = jnp.asarray(make_tables(width))
    grown = pltpu.VMEM((2, 4, tile + width, LANES), jnp.float32)
    packed = pl.pallas_call(
        pack_kernel, out_shape=tuple([array(*side)] * 4),
        in_specs=smem(1) + [pl.BlockSpec(memory_space=pltpu.HBM)], out_specs=tuple(vmem(4)),
        scratch_shapes=[pltpu.VMEM(object_field.shape, jnp.float32), pltpu.SemaphoreType.DMA((2,))],
        compiler_params=pltpu.CompilerParams(vmem_limit_bytes=GRANT),
    )(spot, pltpu.with_memory_space_constraint(object_field, pltpu.HBM))
    halos = []
    cols = [meet(packed[2 * piece : 2 * piece + 2], 1) for piece in range(2)]
    for piece in range(2):
        strips = call(
            functools.partial(rows_kernel, piece=piece), [array(*edge)] * 2,
            (spot,), (object_field, *cols[piece]),
        )
        halos.append((*cols[piece], *meet(strips, 0)))
    win, mid = call(
        functools.partial(first_kernel, group=2), [fields] * 2, (offset_row, offset_col, spot),
        (object_field, *halos[0], probe, tabs), (grown,),
    )
    grad, down, mine, send = call(
        functools.partial(second_kernel, group=count), [fields] * 2 + [array(*plane)] * 2, (offset_row, offset_col, spot, live),
        (object_field, *halos[1], win, mid, intensity[0], tabs),
        (grown, pltpu.VMEM((2, *plane), jnp.float32)),
    )
    part, *strips, left, right = call(
        place_kernel, [field] + [array(2, *edge)] * 2 + [array(2, *side)] * 2,
        (offset_row, offset_col, spot), (object_field, probe, down, grad),
        (pltpu.VMEM((2, 2, 4, tile + width, LANES), jnp.float32),),
    )
    mine = mine + swap(send, (1, 1))
    mine = mine + swap(mine, MASKS[0])
    mine, *strips = lax.optimization_barrier((mine, *strips))
    rows = meet(strips, 0)
    for mask in MASKS[1:4]:
        mine = mine + swap(mine, mask)
    mine, *rows = lax.optimization_barrier((mine, *rows))
    strips = call(fold_kernel, [array(2, *side)] * 2, (spot,), (left, right, *rows))
    mine = mine + swap(mine, MASKS[4])
    mine, *strips = lax.optimization_barrier((mine, *strips))
    cols = meet(strips, 1)
    for mask in MASKS[5:]:
        mine = mine + swap(mine, mask)
    mine, *cols = lax.optimization_barrier((mine, *cols))
    (new,) = call(finish_kernel, (field,), (spot,), (part, *rows, *cols))
    other = swap(mine, (1, 1))
    count_all = count * lax.axis_size("row") * lax.axis_size("col")
    (new_probe,) = call(
        functools.partial(probe_kernel, scale=STEP_PROBE / count_all), (array(2, *plane),),
        (spot,), (probe, mine, other),
    )
    return new, new_probe


def solution(mesh):
    placed = (
        P(None, None, "row", "col"),
        P(),
        P("row", "col", None, None),
        P("row", "col"),
        P("row", "col"),
        P("row", "col"),
    )
    return jax.shard_map(
        on_device,
        mesh=mesh,
        in_specs=placed,
        out_specs=(P(None, None, "row", "col"), P()),
        check_vma=False,
    )
```

```python
import functools
import math

import jax
import jax.numpy as jnp
import ml_dtypes
import numpy as np
from jax import lax
from jax.experimental import pallas as pl
from jax.experimental.pallas import tpu as pltpu
from jax.sharding import PartitionSpec as P

STEP_OBJECT = 0.03
STEP_PROBE = 2.0
FRESNEL_PHASE = 60.0
LANES = 128
BOTH = ("row", "col")
GRANT = 16 * 1024 * 1024
MASKS = ((128, 4), (4, 12), (12, 128), (130, 130), (16, 32), (32, 96), (96, 16))


def split_table(table):
    high = table.astype(ml_dtypes.bfloat16)
    low = (table - high.astype(np.float64)).astype(ml_dtypes.bfloat16)
    return high, low


def make_tables(width):
    index = np.arange(width)
    four = np.exp(-2j * math.pi * (np.outer(index, index) % width) / width) / math.sqrt(width)
    freq = np.where(index < width // 2, index, index - width) / width
    hop = np.conj(four) @ np.diag(np.exp(-1j * FRESNEL_PHASE * freq**2)) @ four
    forms = []
    for table in (hop, four):
        forms.append(np.block([[table.real, table.imag], [-table.imag, table.real]]))
        forms.append(np.block([[table.real, -table.imag], [table.imag, table.real]]))
    pairs = [split_table(form) for form in forms]
    return np.stack([np.stack(pair) for pair in pairs])


def split(value):
    high = value.astype(jnp.bfloat16)
    low = (value - high.astype(jnp.float32)).astype(jnp.bfloat16)
    return high, low


def mul3(left, right):
    dot = functools.partial(jnp.dot, preferred_element_type=jnp.float32)
    return dot(left[0], right[0]) + (dot(left[1], right[0]) + dot(left[0], right[1]))


def two_sided(tabs_ref, right, left, real, imag):
    width = real.shape[1]
    starts = range(0, real.shape[0], width)
    field = split(jnp.concatenate([real, imag], axis=1))
    half = mul3(field, (tabs_ref[right, 0], tabs_ref[right, 1]))
    field = jnp.concatenate(
        [
            jnp.concatenate([half[s : s + width, :width] for s in starts], axis=1),
            jnp.concatenate([half[s : s + width, width:] for s in starts], axis=1),
        ],
        axis=0,
    )
    full = mul3((tabs_ref[left, 0], tabs_ref[left, 1]), split(field))
    return tuple(
        jnp.concatenate([full[part * width : (part + 1) * width, s : s + width] for s in starts], axis=0)
        for part in range(2)
    )


def columns(piece_ref, first):
    half = LANES // 2
    left = jnp.where(first, piece_ref[0, :, :LANES], pltpu.roll(piece_ref[1, :, :LANES], half, 1))
    right = jnp.where(first, pltpu.roll(piece_ref[0, :, LANES:], half, 1), piece_ref[1, :, LANES:])
    return left, right


def pick(spot_ref, axis, even, odd):
    return jnp.where(lax.rem(spot_ref[0, axis], 2) == 0, even, odd)


def beside(spot_ref, axis, a, b):
    place = spot_ref[0, axis]
    before = jnp.where(place == 0, 0.0, pick(spot_ref, axis, b, a))
    after = jnp.where(place == spot_ref[0, 2 + axis] - 1, 0.0, pick(spot_ref, axis, a, b))
    return before, after


def pack_kernel(spot_ref, obj_ref, *refs):
    *outs, held, sems = refs
    first = lax.broadcasted_iota(jnp.int32, (held.shape[2], LANES), 1) < LANES // 2
    copies = [pltpu.make_async_copy(obj_ref.at[p], held.at[p], sems.at[p]) for p in range(2)]
    for copy in copies:
        copy.start()
    for piece in range(2):
        copies[piece].wait()
        left, right = columns(held.at[piece], first)
        outs[2 * piece][...] = pick(spot_ref, 1, right, left)
        outs[2 * piece + 1][...] = pick(spot_ref, 1, left, right)


def rows_kernel(spot_ref, obj_ref, cola_ref, colb_ref, rowa_ref, rowb_ref, *, piece):
    half = LANES // 2
    low, high = slice(0, half), slice(obj_ref.shape[2] - half, obj_ref.shape[2])
    for part in range(2):
        for block in range(2):
            cols = slice(block * LANES, (block + 1) * LANES)
            top, bottom = obj_ref[piece, part, low, cols], obj_ref[piece, part, high, cols]
            rowa_ref[2 * part + block] = pick(spot_ref, 0, bottom, top)
            rowb_ref[2 * part + block] = pick(spot_ref, 0, top, bottom)
    tops = beside(spot_ref, 1, cola_ref[low], colb_ref[low])
    bottoms = beside(spot_ref, 1, cola_ref[high], colb_ref[high])
    for place, top, bottom in zip((4, 5), tops, bottoms):
        rowa_ref[place] = pick(spot_ref, 0, bottom, top)
        rowb_ref[place] = pick(spot_ref, 0, top, bottom)


def grow(ext, spot_ref, piece_ref, cola_ref, colb_ref, rowa_ref, rowb_ref):
    half = LANES // 2
    tile = piece_ref.shape[1]
    sides = beside(spot_ref, 1, cola_ref[...], colb_ref[...])
    for part in range(2):
        for block in range(4):
            place = 2 * part + block - 1 if block in (1, 2) else 4 + block // 3
            top, bottom = beside(spot_ref, 0, rowa_ref[place], rowb_ref[place])
            if block in (1, 2):
                middle = piece_ref[part, :, (block - 1) * LANES : block * LANES]
            else:
                middle = sides[block // 3]
            for strip, start in ((top, 0), (middle, half), (bottom, half + tile)):
                if (block == 0 and part == 0) or (block == 3 and part == 1):
                    strip = pltpu.roll(strip, half, 1)
                ext[part, block, start : start + strip.shape[0]] = strip


def place_window(row_ref, col_ref, slot):
    col = col_ref[0, slot] + LANES // 2
    return row_ref[0, slot], col // LANES, lax.rem(col, LANES)


def window(ext, row_ref, col_ref, slot, width):
    row, block, shift = place_window(row_ref, col_ref, slot)
    back = lax.rem(LANES - shift, LANES)
    keep = lax.broadcasted_iota(jnp.int32, (width, LANES), 1) < LANES - shift
    parts = []
    for part in range(2):
        near = pltpu.roll(ext[part, block, pl.ds(row, width), :], back, 1)
        far = pltpu.roll(ext[part, block + 1, pl.ds(row, width), :], back, 1)
        parts.append(jnp.where(keep, near, far))
    return parts


def windows(ext, row_ref, col_ref, slots, width):
    got = [window(ext, row_ref, col_ref, slot, width) for slot in slots]
    return tuple(jnp.concatenate([g[part] for g in got], axis=0) for part in range(2))


def stacked(ref, slots, part):
    return jnp.concatenate([ref[slot, part] for slot in slots], axis=0)


def store(ref, slots, values):
    width = ref.shape[2]
    for place, slot in enumerate(slots):
        for part in range(2):
            ref[slot, part] = values[part][place * width : (place + 1) * width]


def first_kernel(
    row_ref, col_ref, spot_ref, obj_ref, cola_ref, colb_ref, rowa_ref, rowb_ref, probe_ref, tabs_ref,
    win_ref, mid_ref, ext, *, group,
):
    width = probe_ref.shape[1]
    grow(ext, spot_ref, obj_ref.at[0], cola_ref, colb_ref, rowa_ref, rowb_ref)

    def some(index, _):
        slots = [group * index + place for place in range(group)]
        first_re, first_im = windows(ext, row_ref, col_ref, slots, width)
        probe_re, probe_im = (jnp.concatenate([probe_ref[p]] * group, axis=0) for p in range(2))
        wave_re = probe_re * first_re - probe_im * first_im
        wave_im = probe_re * first_im + probe_im * first_re
        store(win_ref, slots, (first_re, first_im))
        store(mid_ref, slots, two_sided(tabs_ref, 0, 1, wave_re, wave_im))
        return 0

    lax.fori_loop(0, row_ref.shape[1] // group, some, 0, unroll=True)


def second_kernel(
    row_ref, col_ref, spot_ref, live_ref, obj_ref, cola_ref, colb_ref, rowa_ref, rowb_ref,
    win_ref, mid_ref, measured_ref, tabs_ref,
    grad_ref, down_ref, keep_ref, send_ref,
    ext, sum_ref, *, group,
):
    width = win_ref.shape[2]
    grow(ext, spot_ref, obj_ref.at[1], cola_ref, colb_ref, rowa_ref, rowb_ref)
    sum_ref[...] = jnp.zeros_like(sum_ref)

    def some(index, _):
        slots = [group * index + place for place in range(group)]
        second_re, second_im = windows(ext, row_ref, col_ref, slots, width)
        mid_re, mid_im = (stacked(mid_ref, slots, part) for part in range(2))
        exit_re = mid_re * second_re - mid_im * second_im
        exit_im = mid_re * second_im + mid_im * second_re
        far_re, far_im = two_sided(tabs_ref, 2, 3, exit_re, exit_im)
        weights = []
        for place, slot in enumerate(slots):
            rows = slice(place * width, (place + 1) * width)
            active = jnp.where(slot < live_ref[0, 0], 2.0, 0.0)
            power = far_re[rows] * far_re[rows] + far_im[rows] * far_im[rows]
            weights.append((power - measured_ref[slot]) * active)
        weight = jnp.concatenate(weights, axis=0)
        chi_re, chi_im = two_sided(tabs_ref, 3, 2, weight * far_re, weight * far_im)
        grad_re = mid_re * chi_re + mid_im * chi_im
        grad_im = mid_re * chi_im - mid_im * chi_re
        store(grad_ref, slots, (grad_re, grad_im))
        back_re = second_re * chi_re + second_im * chi_im
        back_im = second_re * chi_im - second_im * chi_re
        down_re, down_im = two_sided(tabs_ref, 1, 0, back_re, back_im)
        store(down_ref, slots, (down_re, down_im))
        first_re, first_im = (stacked(win_ref, slots, part) for part in range(2))
        sum_re = first_re * down_re + first_im * down_im
        sum_im = first_re * down_im - first_im * down_re
        for part, value in enumerate((sum_re, sum_im)):
            total = value[:width]
            for start in range(width, group * width, width):
                total += value[start : start + width]
            sum_ref[part] += total
        return 0

    lax.fori_loop(0, row_ref.shape[1] // group, some, 0, unroll=True)
    keep_ref[...] = pick(spot_ref, 1, sum_ref[0], sum_ref[1])
    send_ref[...] = pick(spot_ref, 1, sum_ref[1], sum_ref[0])


def place_kernel(
    row_ref, col_ref, spot_ref, obj_ref, probe_ref, down_ref, second_ref,
    new_ref, rowa_ref, rowb_ref, left_ref, right_ref,
    grad,
):
    width = probe_ref.shape[1]
    tile = obj_ref.shape[2]
    half = width // 2
    grad[...] = jnp.zeros_like(grad)
    lane = lax.broadcasted_iota(jnp.int32, (width, LANES), 1)

    def deposit(slot, _):
        row, block, shift = place_window(row_ref, col_ref, slot)
        keep = lane >= shift
        probe_re, probe_im = probe_ref[0], probe_ref[1]
        down_re, down_im = down_ref[slot, 0], down_ref[slot, 1]
        values = (
            (probe_re * down_re + probe_im * down_im, probe_re * down_im - probe_im * down_re),
            (second_ref[slot, 0], second_ref[slot, 1]),
        )
        for piece in range(2):
            for part in range(2):
                value = pltpu.roll(values[piece][part], shift, 1)
                grad[piece, part, block, pl.ds(row, width), :] += jnp.where(keep, value, 0.0)
                grad[piece, part, block + 1, pl.ds(row, width), :] += jnp.where(keep, 0.0, value)
        return 0

    lax.fori_loop(0, row_ref.shape[1], deposit, 0)
    first = lax.broadcasted_iota(jnp.int32, (tile + width, LANES), 1) < half
    for piece in range(2):
        for part in range(2):
            for block in range(2):
                cols = slice(block * LANES, (block + 1) * LANES)
                top = grad[piece, part, 1 + block, :half]
                bottom = grad[piece, part, 1 + block, half + tile :]
                rowa_ref[piece, 2 * part + block] = pick(spot_ref, 0, bottom, top)
                rowb_ref[piece, 2 * part + block] = pick(spot_ref, 0, top, bottom)
                new_ref[piece, part, :, cols] = (
                    obj_ref[piece, part, :, cols]
                    - STEP_OBJECT * grad[piece, part, 1 + block, half : half + tile]
                )
        left = jnp.where(first, pltpu.roll(grad[piece, 0, 0], half, 1), grad[piece, 1, 0])
        right = jnp.where(first, grad[piece, 0, 3], pltpu.roll(grad[piece, 1, 3], half, 1))
        for place, strip, ref in ((4, left, left_ref), (5, right, right_ref)):
            top, bottom = strip[:half], strip[half + tile :]
            rowa_ref[piece, place] = pick(spot_ref, 0, bottom, top)
            rowb_ref[piece, place] = pick(spot_ref, 0, top, bottom)
            ref[piece] = strip[half : half + tile]


def fold_kernel(spot_ref, left_ref, right_ref, rowa_ref, rowb_ref, cola_ref, colb_ref):
    half = LANES // 2
    tile = left_ref.shape[1]
    for piece in range(2):
        sides = []
        for ref, place in ((left_ref, 4), (right_ref, 5)):
            top, bottom = beside(spot_ref, 0, rowa_ref[piece, place], rowb_ref[piece, place])
            sides.append(
                (
                    ref[piece, :half] + top,
                    ref[piece, half : tile - half],
                    ref[piece, tile - half :] + bottom,
                )
            )
        for left, right, rows in zip(*sides, (slice(0, half), slice(half, tile - half), slice(tile - half, tile))):
            cola_ref[piece, rows] = pick(spot_ref, 1, right, left)
            colb_ref[piece, rows] = pick(spot_ref, 1, left, right)


def finish_kernel(
    spot_ref, part_ref, rowa_ref, rowb_ref, cola_ref, colb_ref, new_ref,
):
    tile = part_ref.shape[2]
    half = LANES // 2
    first = lax.broadcasted_iota(jnp.int32, (half, LANES), 1) < half
    for piece in range(2):
        for start in range(0, tile, half):
            rows = slice(start, start + half)
            sides = beside(spot_ref, 1, cola_ref[piece, rows], colb_ref[piece, rows])
            for part in range(2):
                for block in range(2):
                    cols = slice(block * LANES, (block + 1) * LANES)
                    total = sides[block]
                    if block != part:
                        total = pltpu.roll(total, half, 1)
                    total = jnp.where(first == (block == 0), total, 0.0)
                    place = 2 * part + block
                    ends = beside(spot_ref, 0, rowa_ref[piece, place], rowb_ref[piece, place])
                    if start == 0:
                        total += ends[0]
                    if start == tile - half:
                        total += ends[1]
                    new_ref[piece, part, rows, cols] = (
                        part_ref[piece, part, rows, cols] - STEP_OBJECT * total
                    )


def probe_kernel(spot_ref, probe_ref, mine_ref, other_ref, newp_ref, *, scale):
    newp_ref[0] = probe_ref[0] - scale * pick(spot_ref, 1, mine_ref[...], other_ref[...])
    newp_ref[1] = probe_ref[1] - scale * pick(spot_ref, 1, other_ref[...], mine_ref[...])


def vmem(count):
    return [pl.BlockSpec(memory_space=pltpu.VMEM)] * count


def smem(count):
    return [pl.BlockSpec(memory_space=pltpu.SMEM)] * count


def array(*shape):
    return jax.ShapeDtypeStruct(shape, jnp.float32)


def meet(strips, axis):
    sizes = (lax.axis_size("row"), lax.axis_size("col"))
    got = []
    for odd, strip in enumerate(strips):
        pairs = []
        for spot in np.ndindex(*sizes):
            other = list(spot)
            place = ((spot[axis] + odd) ^ 1) - odd
            if 0 <= place < sizes[axis]:
                other[axis] = place
            else:
                other[1 - axis] ^= 1
            pairs.append((spot[0] * sizes[1] + spot[1], other[0] * sizes[1] + other[1]))
        got.append(lax.ppermute(strip, BOTH, pairs))
    return got


def swap(value, masks):
    count = lax.axis_size("row") * lax.axis_size("col")
    return lax.ppermute(value, BOTH, [(i, i ^ masks[i % 2]) for i in range(count)])


def call(kernel, out_shape, scalars, arrays, scratch=()):
    return pl.pallas_call(
        kernel, out_shape=tuple(out_shape), in_specs=smem(len(scalars)) + vmem(len(arrays)),
        out_specs=tuple(vmem(len(out_shape))), scratch_shapes=list(scratch),
        compiler_params=pltpu.CompilerParams(vmem_limit_bytes=GRANT),
    )(*scalars, *arrays)


def on_device(object_field, probe, intensity, offset_row, offset_col, live):
    tile = object_field.shape[2]
    width = probe.shape[1]
    half = width // 2
    count = offset_row.shape[1]
    side, edge, plane = (tile, LANES), (6, half, LANES), (width, width)
    field, fields = array(2, 2, tile, tile), array(count, 2, width, width)
    place = [lax.axis_index(axis) for axis in BOTH] + [lax.axis_size(axis) for axis in BOTH]
    spot = jnp.stack([jnp.asarray(entry, jnp.int32) for entry in place]).reshape(1, 4)
    tabs = jnp.asarray(make_tables(width))
    grown = pltpu.VMEM((2, 4, tile + width, LANES), jnp.float32)
    packed = pl.pallas_call(
        pack_kernel, out_shape=tuple([array(*side)] * 4),
        in_specs=smem(1) + [pl.BlockSpec(memory_space=pltpu.HBM)], out_specs=tuple(vmem(4)),
        scratch_shapes=[pltpu.VMEM(object_field.shape, jnp.float32), pltpu.SemaphoreType.DMA((2,))],
        compiler_params=pltpu.CompilerParams(vmem_limit_bytes=GRANT),
    )(spot, pltpu.with_memory_space_constraint(object_field, pltpu.HBM))
    halos = []
    cols = [meet(packed[2 * piece : 2 * piece + 2], 1) for piece in range(2)]
    for piece in range(2):
        strips = call(
            functools.partial(rows_kernel, piece=piece), [array(*edge)] * 2,
            (spot,), (object_field, *cols[piece]),
        )
        halos.append((*cols[piece], *meet(strips, 0)))
    win, mid = call(
        functools.partial(first_kernel, group=2), [fields] * 2, (offset_row, offset_col, spot),
        (object_field, *halos[0], probe, tabs), (grown,),
    )
    grad, down, mine, send = call(
        functools.partial(second_kernel, group=count), [fields] * 2 + [array(*plane)] * 2, (offset_row, offset_col, spot, live),
        (object_field, *halos[1], win, mid, intensity[0], tabs),
        (grown, pltpu.VMEM((2, *plane), jnp.float32)),
    )
    part, *strips, left, right = call(
        place_kernel, [field] + [array(2, *edge)] * 2 + [array(2, *side)] * 2,
        (offset_row, offset_col, spot), (object_field, probe, down, grad),
        (pltpu.VMEM((2, 2, 4, tile + width, LANES), jnp.float32),),
    )
    mine = mine + swap(send, (1, 1))
    mine = mine + swap(mine, MASKS[0])
    mine, *strips = lax.optimization_barrier((mine, *strips))
    rows = meet(strips, 0)
    for mask in MASKS[1:4]:
        mine = mine + swap(mine, mask)
    mine, *rows = lax.optimization_barrier((mine, *rows))
    strips = call(fold_kernel, [array(2, *side)] * 2, (spot,), (left, right, *rows))
    mine = mine + swap(mine, MASKS[4])
    mine, *strips = lax.optimization_barrier((mine, *strips))
    cols = meet(strips, 1)
    for mask in MASKS[5:]:
        mine = mine + swap(mine, mask)
    mine, *cols = lax.optimization_barrier((mine, *cols))
    (new,) = call(finish_kernel, (field,), (spot,), (part, *rows, *cols))
    other = swap(mine, (1, 1))
    count_all = count * lax.axis_size("row") * lax.axis_size("col")
    (new_probe,) = call(
        functools.partial(probe_kernel, scale=STEP_PROBE / count_all), (array(2, *plane),),
        (spot,), (probe, mine, other),
    )
    return new, new_probe


def solution(mesh):
    placed = (
        P(None, None, "row", "col"),
        P(),
        P("row", "col", None, None),
        P("row", "col"),
        P("row", "col"),
        P("row", "col"),
    )
    return jax.shard_map(
        on_device,
        mesh=mesh,
        in_specs=placed,
        out_specs=(P(None, None, "row", "col"), P()),
        check_vma=False,
    )
```

```python
import functools
import math

import jax
import jax.numpy as jnp
import ml_dtypes
import numpy as np
from jax import lax
from jax.experimental import pallas as pl
from jax.experimental.pallas import tpu as pltpu
from jax.sharding import PartitionSpec as P

STEP_OBJECT = 0.03
STEP_PROBE = 2.0
FRESNEL_PHASE = 60.0
LANES = 128
BOTH = ("row", "col")
GRANT = 16 * 1024 * 1024
MASKS = ((128, 130), (4, 12), (12, 4), (130, 128), (16, 32), (32, 96), (96, 16))


def split_table(table):
    high = table.astype(ml_dtypes.bfloat16)
    low = (table - high.astype(np.float64)).astype(ml_dtypes.bfloat16)
    return high, low


def make_tables(width):
    index = np.arange(width)
    four = np.exp(-2j * math.pi * (np.outer(index, index) % width) / width) / math.sqrt(width)
    freq = np.where(index < width // 2, index, index - width) / width
    hop = np.conj(four) @ np.diag(np.exp(-1j * FRESNEL_PHASE * freq**2)) @ four
    forms = []
    for table in (hop, four):
        forms.append(np.block([[table.real, table.imag], [-table.imag, table.real]]))
        forms.append(np.block([[table.real, -table.imag], [table.imag, table.real]]))
    pairs = [split_table(form) for form in forms]
    return np.stack([np.stack(pair) for pair in pairs])


def split(value):
    high = value.astype(jnp.bfloat16)
    low = (value - high.astype(jnp.float32)).astype(jnp.bfloat16)
    return high, low


def mul3(left, right):
    dot = functools.partial(jnp.dot, preferred_element_type=jnp.float32)
    return dot(left[0], right[0]) + (dot(left[1], right[0]) + dot(left[0], right[1]))


def two_sided(tabs_ref, right, left, real, imag):
    width = real.shape[1]
    starts = range(0, real.shape[0], width)
    field = split(jnp.concatenate([real, imag], axis=1))
    half = mul3(field, (tabs_ref[right, 0], tabs_ref[right, 1]))
    field = jnp.concatenate(
        [
            jnp.concatenate([half[s : s + width, :width] for s in starts], axis=1),
            jnp.concatenate([half[s : s + width, width:] for s in starts], axis=1),
        ],
        axis=0,
    )
    full = mul3((tabs_ref[left, 0], tabs_ref[left, 1]), split(field))
    return tuple(
        jnp.concatenate([full[part * width : (part + 1) * width, s : s + width] for s in starts], axis=0)
        for part in range(2)
    )


def columns(piece_ref, first):
    half = LANES // 2
    left = jnp.where(first, piece_ref[0, :, :LANES], pltpu.roll(piece_ref[1, :, :LANES], half, 1))
    right = jnp.where(first, pltpu.roll(piece_ref[0, :, LANES:], half, 1), piece_ref[1, :, LANES:])
    return left, right


def pick(spot_ref, axis, even, odd):
    return jnp.where(lax.rem(spot_ref[0, axis], 2) == 0, even, odd)


def beside(spot_ref, axis, a, b):
    place = spot_ref[0, axis]
    before = jnp.where(place == 0, 0.0, pick(spot_ref, axis, b, a))
    after = jnp.where(place == spot_ref[0, 2 + axis] - 1, 0.0, pick(spot_ref, axis, a, b))
    return before, after


def pack_kernel(spot_ref, obj_ref, *refs):
    *outs, held, sems = refs
    first = lax.broadcasted_iota(jnp.int32, (held.shape[2], LANES), 1) < LANES // 2
    copies = [pltpu.make_async_copy(obj_ref.at[p], held.at[p], sems.at[p]) for p in range(2)]
    for copy in copies:
        copy.start()
    for piece in range(2):
        copies[piece].wait()
        left, right = columns(held.at[piece], first)
        outs[2 * piece][...] = pick(spot_ref, 1, right, left)
        outs[2 * piece + 1][...] = pick(spot_ref, 1, left, right)


def rows_kernel(spot_ref, obj_ref, cola_ref, colb_ref, rowa_ref, rowb_ref, *, piece):
    half = LANES // 2
    low, high = slice(0, half), slice(obj_ref.shape[2] - half, obj_ref.shape[2])
    for part in range(2):
        for block in range(2):
            cols = slice(block * LANES, (block + 1) * LANES)
            top, bottom = obj_ref[piece, part, low, cols], obj_ref[piece, part, high, cols]
            rowa_ref[2 * part + block] = pick(spot_ref, 0, bottom, top)
            rowb_ref[2 * part + block] = pick(spot_ref, 0, top, bottom)
    tops = beside(spot_ref, 1, cola_ref[low], colb_ref[low])
    bottoms = beside(spot_ref, 1, cola_ref[high], colb_ref[high])
    for place, top, bottom in zip((4, 5), tops, bottoms):
        rowa_ref[place] = pick(spot_ref, 0, bottom, top)
        rowb_ref[place] = pick(spot_ref, 0, top, bottom)


def grow(ext, spot_ref, piece_ref, cola_ref, colb_ref, rowa_ref, rowb_ref):
    half = LANES // 2
    tile = piece_ref.shape[1]
    sides = beside(spot_ref, 1, cola_ref[...], colb_ref[...])
    for part in range(2):
        for block in range(4):
            place = 2 * part + block - 1 if block in (1, 2) else 4 + block // 3
            top, bottom = beside(spot_ref, 0, rowa_ref[place], rowb_ref[place])
            if block in (1, 2):
                middle = piece_ref[part, :, (block - 1) * LANES : block * LANES]
            else:
                middle = sides[block // 3]
            for strip, start in ((top, 0), (middle, half), (bottom, half + tile)):
                if (block == 0 and part == 0) or (block == 3 and part == 1):
                    strip = pltpu.roll(strip, half, 1)
                ext[part, block, start : start + strip.shape[0]] = strip


def place_window(row_ref, col_ref, slot):
    col = col_ref[0, slot] + LANES // 2
    return row_ref[0, slot], col // LANES, lax.rem(col, LANES)


def window(ext, row_ref, col_ref, slot, width):
    row, block, shift = place_window(row_ref, col_ref, slot)
    back = lax.rem(LANES - shift, LANES)
    keep = lax.broadcasted_iota(jnp.int32, (width, LANES), 1) < LANES - shift
    parts = []
    for part in range(2):
        near = pltpu.roll(ext[part, block, pl.ds(row, width), :], back, 1)
        far = pltpu.roll(ext[part, block + 1, pl.ds(row, width), :], back, 1)
        parts.append(jnp.where(keep, near, far))
    return parts


def windows(ext, row_ref, col_ref, slots, width):
    got = [window(ext, row_ref, col_ref, slot, width) for slot in slots]
    return tuple(jnp.concatenate([g[part] for g in got], axis=0) for part in range(2))


def stacked(ref, slots, part):
    return jnp.concatenate([ref[slot, part] for slot in slots], axis=0)


def store(ref, slots, values):
    width = ref.shape[2]
    for place, slot in enumerate(slots):
        for part in range(2):
            ref[slot, part] = values[part][place * width : (place + 1) * width]


def first_kernel(
    row_ref, col_ref, spot_ref, obj_ref, cola_ref, colb_ref, rowa_ref, rowb_ref, probe_ref, tabs_ref,
    win_ref, mid_ref, ext, *, group,
):
    width = probe_ref.shape[1]
    grow(ext, spot_ref, obj_ref.at[0], cola_ref, colb_ref, rowa_ref, rowb_ref)

    def some(index, _):
        slots = [group * index + place for place in range(group)]
        first_re, first_im = windows(ext, row_ref, col_ref, slots, width)
        probe_re, probe_im = (jnp.concatenate([probe_ref[p]] * group, axis=0) for p in range(2))
        wave_re = probe_re * first_re - probe_im * first_im
        wave_im = probe_re * first_im + probe_im * first_re
        store(win_ref, slots, (first_re, first_im))
        store(mid_ref, slots, two_sided(tabs_ref, 0, 1, wave_re, wave_im))
        return 0

    lax.fori_loop(0, row_ref.shape[1] // group, some, 0, unroll=True)


def second_kernel(
    row_ref, col_ref, spot_ref, live_ref, obj_ref, cola_ref, colb_ref, rowa_ref, rowb_ref,
    win_ref, mid_ref, measured_ref, tabs_ref,
    grad_ref, down_ref, keep_ref, send_ref,
    ext, sum_ref, *, group,
):
    width = win_ref.shape[2]
    grow(ext, spot_ref, obj_ref.at[1], cola_ref, colb_ref, rowa_ref, rowb_ref)
    sum_ref[...] = jnp.zeros_like(sum_ref)

    def some(index, _):
        slots = [group * index + place for place in range(group)]
        second_re, second_im = windows(ext, row_ref, col_ref, slots, width)
        mid_re, mid_im = (stacked(mid_ref, slots, part) for part in range(2))
        exit_re = mid_re * second_re - mid_im * second_im
        exit_im = mid_re * second_im + mid_im * second_re
        far_re, far_im = two_sided(tabs_ref, 2, 3, exit_re, exit_im)
        weights = []
        for place, slot in enumerate(slots):
            rows = slice(place * width, (place + 1) * width)
            active = jnp.where(slot < live_ref[0, 0], 2.0, 0.0)
            power = far_re[rows] * far_re[rows] + far_im[rows] * far_im[rows]
            weights.append((power - measured_ref[slot]) * active)
        weight = jnp.concatenate(weights, axis=0)
        chi_re, chi_im = two_sided(tabs_ref, 3, 2, weight * far_re, weight * far_im)
        grad_re = mid_re * chi_re + mid_im * chi_im
        grad_im = mid_re * chi_im - mid_im * chi_re
        store(grad_ref, slots, (grad_re, grad_im))
        back_re = second_re * chi_re + second_im * chi_im
        back_im = second_re * chi_im - second_im * chi_re
        down_re, down_im = two_sided(tabs_ref, 1, 0, back_re, back_im)
        store(down_ref, slots, (down_re, down_im))
        first_re, first_im = (stacked(win_ref, slots, part) for part in range(2))
        sum_re = first_re * down_re + first_im * down_im
        sum_im = first_re * down_im - first_im * down_re
        for part, value in enumerate((sum_re, sum_im)):
            total = value[:width]
            for start in range(width, group * width, width):
                total += value[start : start + width]
            sum_ref[part] += total
        return 0

    lax.fori_loop(0, row_ref.shape[1] // group, some, 0, unroll=True)
    keep_ref[...] = pick(spot_ref, 1, sum_ref[0], sum_ref[1])
    send_ref[...] = pick(spot_ref, 1, sum_ref[1], sum_ref[0])


def place_kernel(
    row_ref, col_ref, spot_ref, obj_ref, probe_ref, down_ref, second_ref,
    new_ref, rowa_ref, rowb_ref, left_ref, right_ref,
    grad,
):
    width = probe_ref.shape[1]
    tile = obj_ref.shape[2]
    half = width // 2
    grad[...] = jnp.zeros_like(grad)
    lane = lax.broadcasted_iota(jnp.int32, (width, LANES), 1)

    def deposit(slot, _):
        row, block, shift = place_window(row_ref, col_ref, slot)
        keep = lane >= shift
        probe_re, probe_im = probe_ref[0], probe_ref[1]
        down_re, down_im = down_ref[slot, 0], down_ref[slot, 1]
        values = (
            (probe_re * down_re + probe_im * down_im, probe_re * down_im - probe_im * down_re),
            (second_ref[slot, 0], second_ref[slot, 1]),
        )
        for piece in range(2):
            for part in range(2):
                value = pltpu.roll(values[piece][part], shift, 1)
                grad[piece, part, block, pl.ds(row, width), :] += jnp.where(keep, value, 0.0)
                grad[piece, part, block + 1, pl.ds(row, width), :] += jnp.where(keep, 0.0, value)
        return 0

    lax.fori_loop(0, row_ref.shape[1], deposit, 0)
    first = lax.broadcasted_iota(jnp.int32, (tile + width, LANES), 1) < half
    for piece in range(2):
        for part in range(2):
            for block in range(2):
                cols = slice(block * LANES, (block + 1) * LANES)
                top = grad[piece, part, 1 + block, :half]
                bottom = grad[piece, part, 1 + block, half + tile :]
                rowa_ref[piece, 2 * part + block] = pick(spot_ref, 0, bottom, top)
                rowb_ref[piece, 2 * part + block] = pick(spot_ref, 0, top, bottom)
                new_ref[piece, part, :, cols] = (
                    obj_ref[piece, part, :, cols]
                    - STEP_OBJECT * grad[piece, part, 1 + block, half : half + tile]
                )
        left = jnp.where(first, pltpu.roll(grad[piece, 0, 0], half, 1), grad[piece, 1, 0])
        right = jnp.where(first, grad[piece, 0, 3], pltpu.roll(grad[piece, 1, 3], half, 1))
        for place, strip, ref in ((4, left, left_ref), (5, right, right_ref)):
            top, bottom = strip[:half], strip[half + tile :]
            rowa_ref[piece, place] = pick(spot_ref, 0, bottom, top)
            rowb_ref[piece, place] = pick(spot_ref, 0, top, bottom)
            ref[piece] = strip[half : half + tile]


def fold_kernel(spot_ref, left_ref, right_ref, rowa_ref, rowb_ref, cola_ref, colb_ref):
    half = LANES // 2
    tile = left_ref.shape[1]
    for piece in range(2):
        sides = []
        for ref, place in ((left_ref, 4), (right_ref, 5)):
            top, bottom = beside(spot_ref, 0, rowa_ref[piece, place], rowb_ref[piece, place])
            sides.append(
                (
                    ref[piece, :half] + top,
                    ref[piece, half : tile - half],
                    ref[piece, tile - half :] + bottom,
                )
            )
        for left, right, rows in zip(*sides, (slice(0, half), slice(half, tile - half), slice(tile - half, tile))):
            cola_ref[piece, rows] = pick(spot_ref, 1, right, left)
            colb_ref[piece, rows] = pick(spot_ref, 1, left, right)


def finish_kernel(
    spot_ref, part_ref, rowa_ref, rowb_ref, cola_ref, colb_ref, new_ref,
):
    tile = part_ref.shape[2]
    half = LANES // 2
    first = lax.broadcasted_iota(jnp.int32, (half, LANES), 1) < half
    for piece in range(2):
        for start in range(0, tile, half):
            rows = slice(start, start + half)
            sides = beside(spot_ref, 1, cola_ref[piece, rows], colb_ref[piece, rows])
            for part in range(2):
                for block in range(2):
                    cols = slice(block * LANES, (block + 1) * LANES)
                    total = sides[block]
                    if block != part:
                        total = pltpu.roll(total, half, 1)
                    total = jnp.where(first == (block == 0), total, 0.0)
                    place = 2 * part + block
                    ends = beside(spot_ref, 0, rowa_ref[piece, place], rowb_ref[piece, place])
                    if start == 0:
                        total += ends[0]
                    if start == tile - half:
                        total += ends[1]
                    new_ref[piece, part, rows, cols] = (
                        part_ref[piece, part, rows, cols] - STEP_OBJECT * total
                    )


def probe_kernel(spot_ref, probe_ref, mine_ref, other_ref, newp_ref, *, scale):
    newp_ref[0] = probe_ref[0] - scale * pick(spot_ref, 1, mine_ref[...], other_ref[...])
    newp_ref[1] = probe_ref[1] - scale * pick(spot_ref, 1, other_ref[...], mine_ref[...])


def vmem(count):
    return [pl.BlockSpec(memory_space=pltpu.VMEM)] * count


def smem(count):
    return [pl.BlockSpec(memory_space=pltpu.SMEM)] * count


def array(*shape):
    return jax.ShapeDtypeStruct(shape, jnp.float32)


def meet(strips, axis):
    sizes = (lax.axis_size("row"), lax.axis_size("col"))
    got = []
    for odd, strip in enumerate(strips):
        pairs = []
        for spot in np.ndindex(*sizes):
            other = list(spot)
            place = ((spot[axis] + odd) ^ 1) - odd
            if 0 <= place < sizes[axis]:
                other[axis] = place
            else:
                other[1 - axis] ^= 1
            pairs.append((spot[0] * sizes[1] + spot[1], other[0] * sizes[1] + other[1]))
        got.append(lax.ppermute(strip, BOTH, pairs))
    return got


def swap(value, masks):
    count = lax.axis_size("row") * lax.axis_size("col")
    return lax.ppermute(value, BOTH, [(i, i ^ masks[i % 2]) for i in range(count)])


def call(kernel, out_shape, scalars, arrays, scratch=()):
    return pl.pallas_call(
        kernel, out_shape=tuple(out_shape), in_specs=smem(len(scalars)) + vmem(len(arrays)),
        out_specs=tuple(vmem(len(out_shape))), scratch_shapes=list(scratch),
        compiler_params=pltpu.CompilerParams(vmem_limit_bytes=GRANT),
    )(*scalars, *arrays)


def on_device(object_field, probe, intensity, offset_row, offset_col, live):
    tile = object_field.shape[2]
    width = probe.shape[1]
    half = width // 2
    count = offset_row.shape[1]
    side, edge, plane = (tile, LANES), (6, half, LANES), (width, width)
    field, fields = array(2, 2, tile, tile), array(count, 2, width, width)
    place = [lax.axis_index(axis) for axis in BOTH] + [lax.axis_size(axis) for axis in BOTH]
    spot = jnp.stack([jnp.asarray(entry, jnp.int32) for entry in place]).reshape(1, 4)
    tabs = jnp.asarray(make_tables(width))
    grown = pltpu.VMEM((2, 4, tile + width, LANES), jnp.float32)
    packed = pl.pallas_call(
        pack_kernel, out_shape=tuple([array(*side)] * 4),
        in_specs=smem(1) + [pl.BlockSpec(memory_space=pltpu.HBM)], out_specs=tuple(vmem(4)),
        scratch_shapes=[pltpu.VMEM(object_field.shape, jnp.float32), pltpu.SemaphoreType.DMA((2,))],
        compiler_params=pltpu.CompilerParams(vmem_limit_bytes=GRANT),
    )(spot, pltpu.with_memory_space_constraint(object_field, pltpu.HBM))
    halos = []
    cols = [meet(packed[2 * piece : 2 * piece + 2], 1) for piece in range(2)]
    for piece in range(2):
        strips = call(
            functools.partial(rows_kernel, piece=piece), [array(*edge)] * 2,
            (spot,), (object_field, *cols[piece]),
        )
        halos.append((*cols[piece], *meet(strips, 0)))
    win, mid = call(
        functools.partial(first_kernel, group=2), [fields] * 2, (offset_row, offset_col, spot),
        (object_field, *halos[0], probe, tabs), (grown,),
    )
    grad, down, mine, send = call(
        functools.partial(second_kernel, group=count), [fields] * 2 + [array(*plane)] * 2, (offset_row, offset_col, spot, live),
        (object_field, *halos[1], win, mid, intensity[0], tabs),
        (grown, pltpu.VMEM((2, *plane), jnp.float32)),
    )
    part, *strips, left, right = call(
        place_kernel, [field] + [array(2, *edge)] * 2 + [array(2, *side)] * 2,
        (offset_row, offset_col, spot), (object_field, probe, down, grad),
        (pltpu.VMEM((2, 2, 4, tile + width, LANES), jnp.float32),),
    )
    mine = mine + swap(send, (1, 1))
    mine = mine + swap(mine, MASKS[0])
    mine, *strips = lax.optimization_barrier((mine, *strips))
    rows = meet(strips, 0)
    for mask in MASKS[1:4]:
        mine = mine + swap(mine, mask)
    mine, *rows = lax.optimization_barrier((mine, *rows))
    strips = call(fold_kernel, [array(2, *side)] * 2, (spot,), (left, right, *rows))
    mine = mine + swap(mine, MASKS[4])
    cols = meet(strips, 1)
    mine = mine + swap(mine, MASKS[5])
    mine, *cols = lax.optimization_barrier((mine, *cols))
    (new,) = call(finish_kernel, (field,), (spot,), (part, *rows, *cols))
    mine = mine + swap(mine, MASKS[6])
    mine, new = lax.optimization_barrier((mine, new))
    other = swap(mine, (1, 1))
    count_all = count * lax.axis_size("row") * lax.axis_size("col")
    (new_probe,) = call(
        functools.partial(probe_kernel, scale=STEP_PROBE / count_all), (array(2, *plane),),
        (spot,), (probe, mine, other),
    )
    return new, new_probe


def solution(mesh):
    placed = (
        P(None, None, "row", "col"),
        P(),
        P("row", "col", None, None),
        P("row", "col"),
        P("row", "col"),
        P("row", "col"),
    )
    return jax.shard_map(
        on_device,
        mesh=mesh,
        in_specs=placed,
        out_specs=(P(None, None, "row", "col"), P()),
        check_vma=False,
    )
```

```python
import functools
import math

import jax
import jax.numpy as jnp
import ml_dtypes
import numpy as np
from jax import lax
from jax.experimental import pallas as pl
from jax.experimental.pallas import tpu as pltpu
from jax.sharding import PartitionSpec as P

STEP_OBJECT = 0.03
STEP_PROBE = 2.0
FRESNEL_PHASE = 60.0
LANES = 128
BOTH = ("row", "col")
GRANT = 16 * 1024 * 1024
MASKS = ((128, 130), (16, 32), (32, 96), (96, 16), (4, 12), (12, 4), (130, 128))


def split_table(table):
    high = table.astype(ml_dtypes.bfloat16)
    low = (table - high.astype(np.float64)).astype(ml_dtypes.bfloat16)
    return high, low


def make_tables(width):
    index = np.arange(width)
    four = np.exp(-2j * math.pi * (np.outer(index, index) % width) / width) / math.sqrt(width)
    freq = np.where(index < width // 2, index, index - width) / width
    hop = np.conj(four) @ np.diag(np.exp(-1j * FRESNEL_PHASE * freq**2)) @ four
    forms = []
    for table in (hop, four):
        forms.append(np.block([[table.real, table.imag], [-table.imag, table.real]]))
        forms.append(np.block([[table.real, -table.imag], [table.imag, table.real]]))
    pairs = [split_table(form) for form in forms]
    return np.stack([np.stack(pair) for pair in pairs])


def split(value):
    high = value.astype(jnp.bfloat16)
    low = (value - high.astype(jnp.float32)).astype(jnp.bfloat16)
    return high, low


def mul3(left, right):
    dot = functools.partial(jnp.dot, preferred_element_type=jnp.float32)
    return dot(left[0], right[0]) + (dot(left[1], right[0]) + dot(left[0], right[1]))


def two_sided(tabs_ref, right, left, real, imag):
    width = real.shape[1]
    starts = range(0, real.shape[0], width)
    field = split(jnp.concatenate([real, imag], axis=1))
    half = mul3(field, (tabs_ref[right, 0], tabs_ref[right, 1]))
    field = jnp.concatenate(
        [
            jnp.concatenate([half[s : s + width, :width] for s in starts], axis=1),
            jnp.concatenate([half[s : s + width, width:] for s in starts], axis=1),
        ],
        axis=0,
    )
    full = mul3((tabs_ref[left, 0], tabs_ref[left, 1]), split(field))
    return tuple(
        jnp.concatenate([full[part * width : (part + 1) * width, s : s + width] for s in starts], axis=0)
        for part in range(2)
    )


def pack_sides(real, imag):
    half = LANES // 2
    first = lax.broadcasted_iota(jnp.int32, real[0].shape, 1) < half
    left = jnp.where(first, real[0], pltpu.roll(imag[0], half, 1))
    right = jnp.where(first, pltpu.roll(real[1], half, 1), imag[1])
    return left, right


def pick(spot_ref, axis, even, odd):
    return jnp.where(lax.rem(spot_ref[0, axis], 2) == 0, even, odd)


def beside(spot_ref, axis, a, b):
    place = spot_ref[0, axis]
    before = jnp.where(place == 0, 0.0, pick(spot_ref, axis, b, a))
    after = jnp.where(place == spot_ref[0, 2 + axis] - 1, 0.0, pick(spot_ref, axis, a, b))
    return before, after


def pack_kernel(spot_ref, obj_ref, *refs):
    *outs, held, sems = refs
    half = LANES // 2
    tile = obj_ref.shape[2]
    copies = []
    for piece in range(2):
        for end, start in enumerate((0, tile - half)):
            copies.append(
                pltpu.make_async_copy(
                    obj_ref.at[piece, :, pl.ds(start, half)], held.at[piece, end], sems.at[piece, end]
                )
            )
            copies[-1].start()
    for piece in range(2):
        for copy in copies[2 * piece : 2 * piece + 2]:
            copy.wait()
        for part in range(2):
            for block in range(2):
                cols = slice(block * LANES, (block + 1) * LANES)
                top, bottom = held[piece, 0, part, :, cols], held[piece, 1, part, :, cols]
                outs[2 * piece][2 * part + block] = pick(spot_ref, 0, bottom, top)
                outs[2 * piece + 1][2 * part + block] = pick(spot_ref, 0, top, bottom)


def columns_kernel(spot_ref, obj_ref, rowa_ref, rowb_ref, cola_ref, colb_ref, *, piece):
    half = LANES // 2
    tile = obj_ref.shape[2]
    ends = [beside(spot_ref, 0, rowa_ref[place], rowb_ref[place]) for place in range(4)]
    for start, size in ((0, half), (half, tile), (half + tile, half)):
        values = []
        for place in range(4):
            cols = slice((place % 2) * LANES, (place % 2 + 1) * LANES)
            if size == tile:
                values.append(obj_ref[piece, place // 2, :, cols])
            else:
                values.append(ends[place][0 if start == 0 else 1])
        left, right = pack_sides(values[:2], values[2:])
        cola_ref[start : start + size] = pick(spot_ref, 1, right, left)
        colb_ref[start : start + size] = pick(spot_ref, 1, left, right)


def grow(ext, spot_ref, piece_ref, cola_ref, colb_ref, rowa_ref, rowb_ref):
    half = LANES // 2
    tile = piece_ref.shape[1]
    sides = beside(spot_ref, 1, cola_ref[...], colb_ref[...])
    for part in range(2):
        for block in range(2):
            place = 2 * part + block
            top, bottom = beside(spot_ref, 0, rowa_ref[place], rowb_ref[place])
            ext[part, 1 + block, :half] = top
            ext[part, 1 + block, half : half + tile] = piece_ref[part, :, block * LANES : (block + 1) * LANES]
            ext[part, 1 + block, half + tile :] = bottom
        ext[part, 0] = pltpu.roll(sides[0], half, 1) if part == 0 else sides[0]
        ext[part, 3] = sides[1] if part == 0 else pltpu.roll(sides[1], half, 1)


def place_window(row_ref, col_ref, slot):
    col = col_ref[0, slot] + LANES // 2
    return row_ref[0, slot], col // LANES, lax.rem(col, LANES)


def window(ext, row_ref, col_ref, slot, width):
    row, block, shift = place_window(row_ref, col_ref, slot)
    back = lax.rem(LANES - shift, LANES)
    keep = lax.broadcasted_iota(jnp.int32, (width, LANES), 1) < LANES - shift
    parts = []
    for part in range(2):
        near = pltpu.roll(ext[part, block, pl.ds(row, width), :], back, 1)
        far = pltpu.roll(ext[part, block + 1, pl.ds(row, width), :], back, 1)
        parts.append(jnp.where(keep, near, far))
    return parts


def windows(ext, row_ref, col_ref, slots, width):
    got = [window(ext, row_ref, col_ref, slot, width) for slot in slots]
    return tuple(jnp.concatenate([g[part] for g in got], axis=0) for part in range(2))


def stacked(ref, slots, part):
    return jnp.concatenate([ref[slot, part] for slot in slots], axis=0)


def store(ref, slots, values):
    width = ref.shape[2]
    for place, slot in enumerate(slots):
        for part in range(2):
            ref[slot, part] = values[part][place * width : (place + 1) * width]


def first_kernel(
    row_ref, col_ref, spot_ref, obj_ref, cola_ref, colb_ref, rowa_ref, rowb_ref, probe_ref, tabs_ref,
    win_ref, mid_ref, ext, *, group,
):
    width = probe_ref.shape[1]
    grow(ext, spot_ref, obj_ref.at[0], cola_ref, colb_ref, rowa_ref, rowb_ref)

    def some(index, _):
        slots = [group * index + place for place in range(group)]
        first_re, first_im = windows(ext, row_ref, col_ref, slots, width)
        probe_re, probe_im = (jnp.concatenate([probe_ref[p]] * group, axis=0) for p in range(2))
        wave_re = probe_re * first_re - probe_im * first_im
        wave_im = probe_re * first_im + probe_im * first_re
        store(win_ref, slots, (first_re, first_im))
        store(mid_ref, slots, two_sided(tabs_ref, 0, 1, wave_re, wave_im))
        return 0

    lax.fori_loop(0, row_ref.shape[1] // group, some, 0, unroll=True)


def second_kernel(
    row_ref, col_ref, spot_ref, live_ref, obj_ref, cola_ref, colb_ref, rowa_ref, rowb_ref,
    win_ref, mid_ref, measured_ref, tabs_ref,
    grad_ref, down_ref, keep_ref, send_ref,
    ext, sum_ref, *, group,
):
    width = win_ref.shape[2]
    grow(ext, spot_ref, obj_ref.at[1], cola_ref, colb_ref, rowa_ref, rowb_ref)
    sum_ref[...] = jnp.zeros_like(sum_ref)

    def some(index, _):
        slots = [group * index + place for place in range(group)]
        second_re, second_im = windows(ext, row_ref, col_ref, slots, width)
        mid_re, mid_im = (stacked(mid_ref, slots, part) for part in range(2))
        exit_re = mid_re * second_re - mid_im * second_im
        exit_im = mid_re * second_im + mid_im * second_re
        far_re, far_im = two_sided(tabs_ref, 2, 3, exit_re, exit_im)
        weights = []
        for place, slot in enumerate(slots):
            rows = slice(place * width, (place + 1) * width)
            active = jnp.where(slot < live_ref[0, 0], 2.0, 0.0)
            power = far_re[rows] * far_re[rows] + far_im[rows] * far_im[rows]
            weights.append((power - measured_ref[slot]) * active)
        weight = jnp.concatenate(weights, axis=0)
        chi_re, chi_im = two_sided(tabs_ref, 3, 2, weight * far_re, weight * far_im)
        grad_re = mid_re * chi_re + mid_im * chi_im
        grad_im = mid_re * chi_im - mid_im * chi_re
        store(grad_ref, slots, (grad_re, grad_im))
        back_re = second_re * chi_re + second_im * chi_im
        back_im = second_re * chi_im - second_im * chi_re
        down_re, down_im = two_sided(tabs_ref, 1, 0, back_re, back_im)
        store(down_ref, slots, (down_re, down_im))
        first_re, first_im = (stacked(win_ref, slots, part) for part in range(2))
        sum_re = first_re * down_re + first_im * down_im
        sum_im = first_re * down_im - first_im * down_re
        for part, value in enumerate((sum_re, sum_im)):
            total = value[:width]
            for start in range(width, group * width, width):
                total += value[start : start + width]
            sum_ref[part] += total
        return 0

    lax.fori_loop(0, row_ref.shape[1] // group, some, 0, unroll=True)
    keep_ref[...] = pick(spot_ref, 1, sum_ref[0], sum_ref[1])
    send_ref[...] = pick(spot_ref, 1, sum_ref[1], sum_ref[0])


def place_kernel(
    row_ref, col_ref, spot_ref, obj_ref, probe_ref, down_ref, second_ref,
    new_ref, cola_ref, colb_ref, top_ref, bottom_ref,
    grad,
):
    width = probe_ref.shape[1]
    tile = obj_ref.shape[2]
    half = width // 2
    grad[...] = jnp.zeros_like(grad)
    lane = lax.broadcasted_iota(jnp.int32, (width, LANES), 1)

    def deposit(slot, _):
        row, block, shift = place_window(row_ref, col_ref, slot)
        keep = lane >= shift
        probe_re, probe_im = probe_ref[0], probe_ref[1]
        down_re, down_im = down_ref[slot, 0], down_ref[slot, 1]
        values = (
            (probe_re * down_re + probe_im * down_im, probe_re * down_im - probe_im * down_re),
            (second_ref[slot, 0], second_ref[slot, 1]),
        )
        for piece in range(2):
            for part in range(2):
                value = pltpu.roll(values[piece][part], shift, 1)
                grad[piece, part, block, pl.ds(row, width), :] += jnp.where(keep, value, 0.0)
                grad[piece, part, block + 1, pl.ds(row, width), :] += jnp.where(keep, 0.0, value)
        return 0

    lax.fori_loop(0, row_ref.shape[1], deposit, 0)
    for piece in range(2):
        for part in range(2):
            for block in range(2):
                cols = slice(block * LANES, (block + 1) * LANES)
                top_ref[piece, 2 * part + block] = grad[piece, part, 1 + block, :half]
                bottom_ref[piece, 2 * part + block] = grad[piece, part, 1 + block, half + tile :]
                new_ref[piece, part, :, cols] = (
                    obj_ref[piece, part, :, cols]
                    - STEP_OBJECT * grad[piece, part, 1 + block, half : half + tile]
                )
        first = lax.broadcasted_iota(jnp.int32, (tile + width, LANES), 1) < half
        left = jnp.where(first, pltpu.roll(grad[piece, 0, 0], half, 1), grad[piece, 1, 0])
        right = jnp.where(first, grad[piece, 0, 3], pltpu.roll(grad[piece, 1, 3], half, 1))
        cola_ref[piece] = pick(spot_ref, 1, right, left)
        colb_ref[piece] = pick(spot_ref, 1, left, right)


def unpack_side(strip, part, block):
    half = LANES // 2
    first = lax.broadcasted_iota(jnp.int32, strip.shape, 1) < half
    if block != part:
        strip = pltpu.roll(strip, half, 1)
    return jnp.where(first == (block == 0), strip, 0.0)


def fold_kernel(spot_ref, top_ref, bottom_ref, cola_ref, colb_ref, rowa_ref, rowb_ref):
    half = LANES // 2
    last = cola_ref.shape[1] - half
    for piece in range(2):
        uppers = beside(spot_ref, 1, cola_ref[piece, :half], colb_ref[piece, :half])
        lowers = beside(spot_ref, 1, cola_ref[piece, last:], colb_ref[piece, last:])
        for part in range(2):
            for block in range(2):
                place = 2 * part + block
                top = top_ref[piece, place] + unpack_side(uppers[block], part, block)
                bottom = bottom_ref[piece, place] + unpack_side(lowers[block], part, block)
                rowa_ref[piece, place] = pick(spot_ref, 0, bottom, top)
                rowb_ref[piece, place] = pick(spot_ref, 0, top, bottom)


def finish_kernel(
    spot_ref, part_ref, rowa_ref, rowb_ref, cola_ref, colb_ref, new_ref,
):
    tile = part_ref.shape[2]
    half = LANES // 2
    for piece in range(2):
        for start in range(0, tile, half):
            rows = slice(start, start + half)
            strips = slice(half + start, half + start + half)
            sides = beside(spot_ref, 1, cola_ref[piece, strips], colb_ref[piece, strips])
            for part in range(2):
                for block in range(2):
                    cols = slice(block * LANES, (block + 1) * LANES)
                    total = unpack_side(sides[block], part, block)
                    place = 2 * part + block
                    ends = beside(spot_ref, 0, rowa_ref[piece, place], rowb_ref[piece, place])
                    if start == 0:
                        total += ends[0]
                    if start == tile - half:
                        total += ends[1]
                    new_ref[piece, part, rows, cols] = (
                        part_ref[piece, part, rows, cols] - STEP_OBJECT * total
                    )


def probe_kernel(spot_ref, probe_ref, mine_ref, other_ref, newp_ref, *, scale):
    newp_ref[0] = probe_ref[0] - scale * pick(spot_ref, 1, mine_ref[...], other_ref[...])
    newp_ref[1] = probe_ref[1] - scale * pick(spot_ref, 1, other_ref[...], mine_ref[...])


def vmem(count):
    return [pl.BlockSpec(memory_space=pltpu.VMEM)] * count


def smem(count):
    return [pl.BlockSpec(memory_space=pltpu.SMEM)] * count


def array(*shape):
    return jax.ShapeDtypeStruct(shape, jnp.float32)


def meet(strips, axis):
    sizes = (lax.axis_size("row"), lax.axis_size("col"))
    got = []
    for odd, strip in enumerate(strips):
        pairs = []
        for spot in np.ndindex(*sizes):
            other = list(spot)
            place = ((spot[axis] + odd) ^ 1) - odd
            if 0 <= place < sizes[axis]:
                other[axis] = place
            else:
                other[1 - axis] ^= 1
            pairs.append((spot[0] * sizes[1] + spot[1], other[0] * sizes[1] + other[1]))
        got.append(lax.ppermute(strip, BOTH, pairs))
    return got


def swap(value, masks):
    count = lax.axis_size("row") * lax.axis_size("col")
    return lax.ppermute(value, BOTH, [(i, i ^ masks[i % 2]) for i in range(count)])


def call(kernel, out_shape, scalars, arrays, scratch=()):
    return pl.pallas_call(
        kernel, out_shape=tuple(out_shape), in_specs=smem(len(scalars)) + vmem(len(arrays)),
        out_specs=tuple(vmem(len(out_shape))), scratch_shapes=list(scratch),
        compiler_params=pltpu.CompilerParams(vmem_limit_bytes=GRANT),
    )(*scalars, *arrays)


def on_device(object_field, probe, intensity, offset_row, offset_col, live):
    tile = object_field.shape[2]
    width = probe.shape[1]
    half = width // 2
    count = offset_row.shape[1]
    side, edge, plane = (tile + width, LANES), (4, half, LANES), (width, width)
    field, fields = array(2, 2, tile, tile), array(count, 2, width, width)
    place = [lax.axis_index(axis) for axis in BOTH] + [lax.axis_size(axis) for axis in BOTH]
    spot = jnp.stack([jnp.asarray(entry, jnp.int32) for entry in place]).reshape(1, 4)
    tabs = jnp.asarray(make_tables(width))
    grown = pltpu.VMEM((2, 4, tile + width, LANES), jnp.float32)
    packed = pl.pallas_call(
        pack_kernel, out_shape=tuple([array(*edge)] * 4),
        in_specs=smem(1) + [pl.BlockSpec(memory_space=pltpu.HBM)], out_specs=tuple(vmem(4)),
        scratch_shapes=[pltpu.VMEM((2, 2, 2, half, tile), jnp.float32), pltpu.SemaphoreType.DMA((2, 2))],
        compiler_params=pltpu.CompilerParams(vmem_limit_bytes=GRANT),
    )(spot, pltpu.with_memory_space_constraint(object_field, pltpu.HBM))
    halos = []
    rows = [meet(packed[2 * piece : 2 * piece + 2], 0) for piece in range(2)]
    for piece in range(2):
        strips = call(
            functools.partial(columns_kernel, piece=piece), [array(*side)] * 2,
            (spot,), (object_field, *rows[piece]),
        )
        halos.append((*meet(strips, 1), *rows[piece]))
    win, mid = call(
        functools.partial(first_kernel, group=2), [fields] * 2, (offset_row, offset_col, spot),
        (object_field, *halos[0], probe, tabs), (grown,),
    )
    grad, down, mine, send = call(
        functools.partial(second_kernel, group=count), [fields] * 2 + [array(*plane)] * 2, (offset_row, offset_col, spot, live),
        (object_field, *halos[1], win, mid, intensity[0], tabs),
        (grown, pltpu.VMEM((2, *plane), jnp.float32)),
    )
    part, *strips, top, bottom = call(
        place_kernel, [field] + [array(2, *side)] * 2 + [array(2, *edge)] * 2,
        (offset_row, offset_col, spot), (object_field, probe, down, grad),
        (pltpu.VMEM((2, 2, 4, tile + width, LANES), jnp.float32),),
    )
    mine = mine + swap(send, (1, 1))
    mine = mine + swap(mine, MASKS[0])
    mine, *strips = lax.optimization_barrier((mine, *strips))
    cols = meet(strips, 1)
    for mask in MASKS[1:4]:
        mine = mine + swap(mine, mask)
    mine, *cols = lax.optimization_barrier((mine, *cols))
    strips = call(fold_kernel, [array(2, *edge)] * 2, (spot,), (top, bottom, *cols))
    mine = mine + swap(mine, MASKS[4])
    mine, *strips = lax.optimization_barrier((mine, *strips))
    rows = meet(strips, 0)
    for mask in MASKS[5:]:
        mine = mine + swap(mine, mask)
    mine, *rows = lax.optimization_barrier((mine, *rows))
    (new,) = call(finish_kernel, (field,), (spot,), (part, *rows, *cols))
    other = swap(mine, (1, 1))
    count_all = count * lax.axis_size("row") * lax.axis_size("col")
    (new_probe,) = call(
        functools.partial(probe_kernel, scale=STEP_PROBE / count_all), (array(2, *plane),),
        (spot,), (probe, mine, other),
    )
    return new, new_probe


def solution(mesh):
    placed = (
        P(None, None, "row", "col"),
        P(),
        P("row", "col", None, None),
        P("row", "col"),
        P("row", "col"),
        P("row", "col"),
    )
    return jax.shard_map(
        on_device,
        mesh=mesh,
        in_specs=placed,
        out_specs=(P(None, None, "row", "col"), P()),
        check_vma=False,
    )
```

```python
import functools
import math

import jax
import jax.numpy as jnp
import ml_dtypes
import numpy as np
from jax import lax
from jax.experimental import pallas as pl
from jax.experimental.pallas import tpu as pltpu
from jax.sharding import PartitionSpec as P

STEP_OBJECT = 0.03
STEP_PROBE = 2.0
FRESNEL_PHASE = 60.0
LANES = 128
BOTH = ("row", "col")
GRANT = 16 * 1024 * 1024
MASKS = ((128, 4), (4, 12), (12, 128), (130, 130), (16, 32), (32, 96), (96, 16))


def split_table(table):
    high = table.astype(ml_dtypes.bfloat16)
    low = (table - high.astype(np.float64)).astype(ml_dtypes.bfloat16)
    return high, low


def make_tables(width):
    index = np.arange(width)
    four = np.exp(-2j * math.pi * (np.outer(index, index) % width) / width) / math.sqrt(width)
    freq = np.where(index < width // 2, index, index - width) / width
    hop = np.conj(four) @ np.diag(np.exp(-1j * FRESNEL_PHASE * freq**2)) @ four
    forms = []
    for table in (hop, four):
        forms.append(np.block([[table.real, table.imag], [-table.imag, table.real]]))
        forms.append(np.block([[table.real, -table.imag], [table.imag, table.real]]))
    pairs = [split_table(form) for form in forms]
    return np.stack([np.stack(pair) for pair in pairs])


def split(value):
    high = value.astype(jnp.bfloat16)
    low = (value - high.astype(jnp.float32)).astype(jnp.bfloat16)
    return high, low


def mul3(left, right):
    dot = functools.partial(jnp.dot, preferred_element_type=jnp.float32)
    return dot(left[0], right[0]) + (dot(left[1], right[0]) + dot(left[0], right[1]))


def two_sided(tabs_ref, right, left, real, imag):
    width = real.shape[1]
    starts = range(0, real.shape[0], width)
    field = split(jnp.concatenate([real, imag], axis=1))
    half = mul3(field, (tabs_ref[right, 0], tabs_ref[right, 1]))
    field = jnp.concatenate(
        [
            jnp.concatenate([half[s : s + width, :width] for s in starts], axis=1),
            jnp.concatenate([half[s : s + width, width:] for s in starts], axis=1),
        ],
        axis=0,
    )
    full = mul3((tabs_ref[left, 0], tabs_ref[left, 1]), split(field))
    return tuple(
        jnp.concatenate([full[part * width : (part + 1) * width, s : s + width] for s in starts], axis=0)
        for part in range(2)
    )


def columns(piece_ref, first):
    half = LANES // 2
    left = jnp.where(first, piece_ref[0, :, :LANES], pltpu.roll(piece_ref[1, :, :LANES], half, 1))
    right = jnp.where(first, pltpu.roll(piece_ref[0, :, LANES:], half, 1), piece_ref[1, :, LANES:])
    return left, right


def pick(axis, even, odd):
    return jnp.where(lax.rem(lax.axis_index(BOTH[axis]), 2) == 0, even, odd)


def beside(axis, a, b):
    place = lax.axis_index(BOTH[axis])
    before = jnp.where(place == 0, 0.0, pick(axis, b, a))
    after = jnp.where(place == lax.axis_size(BOTH[axis]) - 1, 0.0, pick(axis, a, b))
    return before, after


def pack_kernel(obj_ref, *refs):
    *outs, held, sems = refs
    first = lax.broadcasted_iota(jnp.int32, (held.shape[2], LANES), 1) < LANES // 2
    copies = [pltpu.make_async_copy(obj_ref.at[p], held.at[p], sems.at[p]) for p in range(2)]
    for copy in copies:
        copy.start()
    for piece in range(2):
        copies[piece].wait()
        left, right = columns(held.at[piece], first)
        outs[2 * piece][...] = pick(1, right, left)
        outs[2 * piece + 1][...] = pick(1, left, right)


def rows_kernel(obj_ref, cola_ref, colb_ref, rowa_ref, rowb_ref, *, piece):
    half = LANES // 2
    low, high = slice(0, half), slice(obj_ref.shape[2] - half, obj_ref.shape[2])
    for part in range(2):
        for block in range(2):
            cols = slice(block * LANES, (block + 1) * LANES)
            top, bottom = obj_ref[piece, part, low, cols], obj_ref[piece, part, high, cols]
            rowa_ref[2 * part + block] = pick(0, bottom, top)
            rowb_ref[2 * part + block] = pick(0, top, bottom)
    tops = beside(1, cola_ref[low], colb_ref[low])
    bottoms = beside(1, cola_ref[high], colb_ref[high])
    for place, top, bottom in zip((4, 5), tops, bottoms):
        rowa_ref[place] = pick(0, bottom, top)
        rowb_ref[place] = pick(0, top, bottom)


def grow(ext, piece_ref, cola_ref, colb_ref, rowa_ref, rowb_ref):
    half = LANES // 2
    tile = piece_ref.shape[1]
    sides = beside(1, cola_ref[...], colb_ref[...])
    for part in range(2):
        for block in range(4):
            place = 2 * part + block - 1 if block in (1, 2) else 4 + block // 3
            top, bottom = beside(0, rowa_ref[place], rowb_ref[place])
            if block in (1, 2):
                middle = piece_ref[part, :, (block - 1) * LANES : block * LANES]
            else:
                middle = sides[block // 3]
            for strip, start in ((top, 0), (middle, half), (bottom, half + tile)):
                if (block == 0 and part == 0) or (block == 3 and part == 1):
                    strip = pltpu.roll(strip, half, 1)
                ext[part, block, start : start + strip.shape[0]] = strip


def place_window(row_ref, col_ref, slot):
    col = col_ref[0, slot] + LANES // 2
    return row_ref[0, slot], col // LANES, lax.rem(col, LANES)


def window(ext, row_ref, col_ref, slot, width):
    row, block, shift = place_window(row_ref, col_ref, slot)
    back = lax.rem(LANES - shift, LANES)
    keep = lax.broadcasted_iota(jnp.int32, (width, LANES), 1) < LANES - shift
    parts = []
    for part in range(2):
        near = pltpu.roll(ext[part, block, pl.ds(row, width), :], back, 1)
        far = pltpu.roll(ext[part, block + 1, pl.ds(row, width), :], back, 1)
        parts.append(jnp.where(keep, near, far))
    return parts


def windows(ext, row_ref, col_ref, slots, width):
    got = [window(ext, row_ref, col_ref, slot, width) for slot in slots]
    return tuple(jnp.concatenate([g[part] for g in got], axis=0) for part in range(2))


def stacked(ref, slots, part):
    return jnp.concatenate([ref[slot, part] for slot in slots], axis=0)


def store(ref, slots, values):
    width = ref.shape[2]
    for place, slot in enumerate(slots):
        for part in range(2):
            ref[slot, part] = values[part][place * width : (place + 1) * width]


def first_kernel(
    row_ref, col_ref, obj_ref, cola_ref, colb_ref, rowa_ref, rowb_ref, probe_ref, tabs_ref,
    win_ref, mid_ref, ext, *, group,
):
    width = probe_ref.shape[1]
    grow(ext, obj_ref.at[0], cola_ref, colb_ref, rowa_ref, rowb_ref)

    def some(index, _):
        slots = [group * index + place for place in range(group)]
        first_re, first_im = windows(ext, row_ref, col_ref, slots, width)
        probe_re, probe_im = (jnp.concatenate([probe_ref[p]] * group, axis=0) for p in range(2))
        wave_re = probe_re * first_re - probe_im * first_im
        wave_im = probe_re * first_im + probe_im * first_re
        store(win_ref, slots, (first_re, first_im))
        store(mid_ref, slots, two_sided(tabs_ref, 0, 1, wave_re, wave_im))
        return 0

    lax.fori_loop(0, row_ref.shape[1] // group, some, 0, unroll=True)


def second_kernel(
    row_ref, col_ref, live_ref, obj_ref, cola_ref, colb_ref, rowa_ref, rowb_ref,
    win_ref, mid_ref, measured_ref, tabs_ref,
    grad_ref, down_ref, keep_ref, send_ref,
    ext, sum_ref, *, group,
):
    width = win_ref.shape[2]
    grow(ext, obj_ref.at[1], cola_ref, colb_ref, rowa_ref, rowb_ref)
    sum_ref[...] = jnp.zeros_like(sum_ref)

    def some(index, _):
        slots = [group * index + place for place in range(group)]
        second_re, second_im = windows(ext, row_ref, col_ref, slots, width)
        mid_re, mid_im = (stacked(mid_ref, slots, part) for part in range(2))
        exit_re = mid_re * second_re - mid_im * second_im
        exit_im = mid_re * second_im + mid_im * second_re
        far_re, far_im = two_sided(tabs_ref, 2, 3, exit_re, exit_im)
        weights = []
        for place, slot in enumerate(slots):
            rows = slice(place * width, (place + 1) * width)
            active = jnp.where(slot < live_ref[0, 0], 2.0, 0.0)
            power = far_re[rows] * far_re[rows] + far_im[rows] * far_im[rows]
            weights.append((power - measured_ref[slot]) * active)
        weight = jnp.concatenate(weights, axis=0)
        chi_re, chi_im = two_sided(tabs_ref, 3, 2, weight * far_re, weight * far_im)
        grad_re = mid_re * chi_re + mid_im * chi_im
        grad_im = mid_re * chi_im - mid_im * chi_re
        store(grad_ref, slots, (grad_re, grad_im))
        back_re = second_re * chi_re + second_im * chi_im
        back_im = second_re * chi_im - second_im * chi_re
        down_re, down_im = two_sided(tabs_ref, 1, 0, back_re, back_im)
        store(down_ref, slots, (down_re, down_im))
        first_re, first_im = (stacked(win_ref, slots, part) for part in range(2))
        sum_re = first_re * down_re + first_im * down_im
        sum_im = first_re * down_im - first_im * down_re
        for part, value in enumerate((sum_re, sum_im)):
            total = value[:width]
            for start in range(width, group * width, width):
                total += value[start : start + width]
            sum_ref[part] += total
        return 0

    lax.fori_loop(0, row_ref.shape[1] // group, some, 0, unroll=True)
    keep_ref[...] = pick(1, sum_ref[0], sum_ref[1])
    send_ref[...] = pick(1, sum_ref[1], sum_ref[0])


def place_kernel(
    row_ref, col_ref, obj_ref, probe_ref, down_ref, second_ref,
    new_ref, rowa_ref, rowb_ref, left_ref, right_ref,
    grad,
):
    width = probe_ref.shape[1]
    tile = obj_ref.shape[2]
    half = width // 2
    grad[...] = jnp.zeros_like(grad)
    lane = lax.broadcasted_iota(jnp.int32, (width, LANES), 1)

    def deposit(slot, _):
        row, block, shift = place_window(row_ref, col_ref, slot)
        keep = lane >= shift
        probe_re, probe_im = probe_ref[0], probe_ref[1]
        down_re, down_im = down_ref[slot, 0], down_ref[slot, 1]
        values = (
            (probe_re * down_re + probe_im * down_im, probe_re * down_im - probe_im * down_re),
            (second_ref[slot, 0], second_ref[slot, 1]),
        )
        for piece in range(2):
            for part in range(2):
                value = pltpu.roll(values[piece][part], shift, 1)
                grad[piece, part, block, pl.ds(row, width), :] += jnp.where(keep, value, 0.0)
                grad[piece, part, block + 1, pl.ds(row, width), :] += jnp.where(keep, 0.0, value)
        return 0

    lax.fori_loop(0, row_ref.shape[1], deposit, 0)
    first = lax.broadcasted_iota(jnp.int32, (tile + width, LANES), 1) < half
    for piece in range(2):
        for part in range(2):
            for block in range(2):
                cols = slice(block * LANES, (block + 1) * LANES)
                top = grad[piece, part, 1 + block, :half]
                bottom = grad[piece, part, 1 + block, half + tile :]
                rowa_ref[piece, 2 * part + block] = pick(0, bottom, top)
                rowb_ref[piece, 2 * part + block] = pick(0, top, bottom)
                new_ref[piece, part, :, cols] = (
                    obj_ref[piece, part, :, cols]
                    - STEP_OBJECT * grad[piece, part, 1 + block, half : half + tile]
                )
        left = jnp.where(first, pltpu.roll(grad[piece, 0, 0], half, 1), grad[piece, 1, 0])
        right = jnp.where(first, grad[piece, 0, 3], pltpu.roll(grad[piece, 1, 3], half, 1))
        for place, strip, ref in ((4, left, left_ref), (5, right, right_ref)):
            top, bottom = strip[:half], strip[half + tile :]
            rowa_ref[piece, place] = pick(0, bottom, top)
            rowb_ref[piece, place] = pick(0, top, bottom)
            ref[piece] = strip[half : half + tile]


def fold_kernel(left_ref, right_ref, rowa_ref, rowb_ref, cola_ref, colb_ref):
    half = LANES // 2
    tile = left_ref.shape[1]
    for piece in range(2):
        sides = []
        for ref, place in ((left_ref, 4), (right_ref, 5)):
            top, bottom = beside(0, rowa_ref[piece, place], rowb_ref[piece, place])
            sides.append(
                (
                    ref[piece, :half] + top,
                    ref[piece, half : tile - half],
                    ref[piece, tile - half :] + bottom,
                )
            )
        for left, right, rows in zip(*sides, (slice(0, half), slice(half, tile - half), slice(tile - half, tile))):
            cola_ref[piece, rows] = pick(1, right, left)
            colb_ref[piece, rows] = pick(1, left, right)


def finish_kernel(
    part_ref, rowa_ref, rowb_ref, cola_ref, colb_ref, new_ref,
):
    tile = part_ref.shape[2]
    half = LANES // 2
    first = lax.broadcasted_iota(jnp.int32, (half, LANES), 1) < half
    for piece in range(2):
        for start in range(0, tile, half):
            rows = slice(start, start + half)
            sides = beside(1, cola_ref[piece, rows], colb_ref[piece, rows])
            for part in range(2):
                for block in range(2):
                    cols = slice(block * LANES, (block + 1) * LANES)
                    total = sides[block]
                    if block != part:
                        total = pltpu.roll(total, half, 1)
                    total = jnp.where(first == (block == 0), total, 0.0)
                    place = 2 * part + block
                    ends = beside(0, rowa_ref[piece, place], rowb_ref[piece, place])
                    if start == 0:
                        total += ends[0]
                    if start == tile - half:
                        total += ends[1]
                    new_ref[piece, part, rows, cols] = (
                        part_ref[piece, part, rows, cols] - STEP_OBJECT * total
                    )


def probe_kernel(probe_ref, mine_ref, other_ref, newp_ref, *, scale):
    newp_ref[0] = probe_ref[0] - scale * pick(1, mine_ref[...], other_ref[...])
    newp_ref[1] = probe_ref[1] - scale * pick(1, other_ref[...], mine_ref[...])


def vmem(count):
    return [pl.BlockSpec(memory_space=pltpu.VMEM)] * count


def smem(count):
    return [pl.BlockSpec(memory_space=pltpu.SMEM)] * count


def array(*shape):
    return jax.ShapeDtypeStruct(shape, jnp.float32)


def meet(strips, axis):
    sizes = (lax.axis_size("row"), lax.axis_size("col"))
    got = []
    for odd, strip in enumerate(strips):
        pairs = []
        for spot in np.ndindex(*sizes):
            other = list(spot)
            place = ((spot[axis] + odd) ^ 1) - odd
            if 0 <= place < sizes[axis]:
                other[axis] = place
            else:
                other[1 - axis] ^= 1
            pairs.append((spot[0] * sizes[1] + spot[1], other[0] * sizes[1] + other[1]))
        got.append(lax.ppermute(strip, BOTH, pairs))
    return got


def swap(value, masks):
    count = lax.axis_size("row") * lax.axis_size("col")
    return lax.ppermute(value, BOTH, [(i, i ^ masks[i % 2]) for i in range(count)])


def call(kernel, out_shape, scalars, arrays, scratch=()):
    return pl.pallas_call(
        kernel, out_shape=tuple(out_shape), in_specs=smem(len(scalars)) + vmem(len(arrays)),
        out_specs=tuple(vmem(len(out_shape))), scratch_shapes=list(scratch),
        compiler_params=pltpu.CompilerParams(vmem_limit_bytes=GRANT),
    )(*scalars, *arrays)


def on_device(object_field, probe, intensity, offset_row, offset_col, live):
    tile = object_field.shape[2]
    width = probe.shape[1]
    half = width // 2
    count = offset_row.shape[1]
    side, edge, plane = (tile, LANES), (6, half, LANES), (width, width)
    field, fields = array(2, 2, tile, tile), array(count, 2, width, width)
    tabs = jnp.asarray(make_tables(width))
    grown = pltpu.VMEM((2, 4, tile + width, LANES), jnp.float32)
    packed = pl.pallas_call(
        pack_kernel, out_shape=tuple([array(*side)] * 4),
        in_specs=[pl.BlockSpec(memory_space=pltpu.HBM)], out_specs=tuple(vmem(4)),
        scratch_shapes=[pltpu.VMEM(object_field.shape, jnp.float32), pltpu.SemaphoreType.DMA((2,))],
        compiler_params=pltpu.CompilerParams(vmem_limit_bytes=GRANT),
    )(pltpu.with_memory_space_constraint(object_field, pltpu.HBM))
    halos = []
    cols = [meet(packed[2 * piece : 2 * piece + 2], 1) for piece in range(2)]
    for piece in range(2):
        strips = call(
            functools.partial(rows_kernel, piece=piece), [array(*edge)] * 2,
            (), (object_field, *cols[piece]),
        )
        halos.append((*cols[piece], *meet(strips, 0)))
    win, mid = call(
        functools.partial(first_kernel, group=2), [fields] * 2, (offset_row, offset_col),
        (object_field, *halos[0], probe, tabs), (grown,),
    )
    grad, down, mine, send = call(
        functools.partial(second_kernel, group=count), [fields] * 2 + [array(*plane)] * 2, (offset_row, offset_col, live),
        (object_field, *halos[1], win, mid, intensity[0], tabs),
        (grown, pltpu.VMEM((2, *plane), jnp.float32)),
    )
    part, *strips, left, right = call(
        place_kernel, [field] + [array(2, *edge)] * 2 + [array(2, *side)] * 2,
        (offset_row, offset_col), (object_field, probe, down, grad),
        (pltpu.VMEM((2, 2, 4, tile + width, LANES), jnp.float32),),
    )
    mine = mine + swap(send, (1, 1))
    mine = mine + swap(mine, MASKS[0])
    mine, *strips = lax.optimization_barrier((mine, *strips))
    rows = meet(strips, 0)
    for mask in MASKS[1:4]:
        mine = mine + swap(mine, mask)
    mine, *rows = lax.optimization_barrier((mine, *rows))
    strips = call(fold_kernel, [array(2, *side)] * 2, (), (left, right, *rows))
    mine = mine + swap(mine, MASKS[4])
    mine, *strips = lax.optimization_barrier((mine, *strips))
    cols = meet(strips, 1)
    for mask in MASKS[5:]:
        mine = mine + swap(mine, mask)
    mine, *cols = lax.optimization_barrier((mine, *cols))
    (new,) = call(finish_kernel, (field,), (), (part, *rows, *cols))
    other = swap(mine, (1, 1))
    count_all = count * lax.axis_size("row") * lax.axis_size("col")
    (new_probe,) = call(
        functools.partial(probe_kernel, scale=STEP_PROBE / count_all), (array(2, *plane),),
        (), (probe, mine, other),
    )
    return new, new_probe


def solution(mesh):
    placed = (
        P(None, None, "row", "col"),
        P(),
        P("row", "col", None, None),
        P("row", "col"),
        P("row", "col"),
        P("row", "col"),
    )
    return jax.shard_map(
        on_device,
        mesh=mesh,
        in_specs=placed,
        out_specs=(P(None, None, "row", "col"), P()),
        check_vma=False,
    )
```

```python
import functools
import math

import jax
import jax.numpy as jnp
import ml_dtypes
import numpy as np
from jax import lax
from jax.experimental import pallas as pl
from jax.experimental.pallas import tpu as pltpu
from jax.sharding import PartitionSpec as P

STEP_OBJECT = 0.03
STEP_PROBE = 2.0
FRESNEL_PHASE = 60.0
LANES = 128
BOTH = ("row", "col")
GRANT = 16 * 1024 * 1024
MASKS = ((128, 4), (4, 12), (12, 128), (130, 130), (16, 32), (32, 96), (96, 16))


def split_table(table):
    high = table.astype(ml_dtypes.bfloat16)
    low = (table - high.astype(np.float64)).astype(ml_dtypes.bfloat16)
    return high, low


def make_tables(width):
    index = np.arange(width)
    four = np.exp(-2j * math.pi * (np.outer(index, index) % width) / width) / math.sqrt(width)
    freq = np.where(index < width // 2, index, index - width) / width
    hop = np.conj(four) @ np.diag(np.exp(-1j * FRESNEL_PHASE * freq**2)) @ four
    forms = []
    for table in (hop, four):
        forms.append(np.block([[table.real, table.imag], [-table.imag, table.real]]))
        forms.append(np.block([[table.real, -table.imag], [table.imag, table.real]]))
    pairs = [split_table(form) for form in forms]
    return np.stack([np.stack(pair) for pair in pairs])


def split(value):
    high = value.astype(jnp.bfloat16)
    low = (value - high.astype(jnp.float32)).astype(jnp.bfloat16)
    return high, low


def mul3(left, right):
    dot = functools.partial(jnp.dot, preferred_element_type=jnp.float32)
    return dot(left[0], right[0]) + (dot(left[1], right[0]) + dot(left[0], right[1]))


def two_sided(tabs_ref, right, left, real, imag):
    width = real.shape[1]
    starts = range(0, real.shape[0], width)
    field = split(jnp.concatenate([real, imag], axis=1))
    half = mul3(field, (tabs_ref[right, 0], tabs_ref[right, 1]))
    field = jnp.concatenate(
        [
            jnp.concatenate([half[s : s + width, :width] for s in starts], axis=1),
            jnp.concatenate([half[s : s + width, width:] for s in starts], axis=1),
        ],
        axis=0,
    )
    full = mul3((tabs_ref[left, 0], tabs_ref[left, 1]), split(field))
    return tuple(
        jnp.concatenate([full[part * width : (part + 1) * width, s : s + width] for s in starts], axis=0)
        for part in range(2)
    )


def columns(piece_ref, first):
    half = LANES // 2
    left = jnp.where(first, piece_ref[0, :, :LANES], pltpu.roll(piece_ref[1, :, :LANES], half, 1))
    right = jnp.where(first, pltpu.roll(piece_ref[0, :, LANES:], half, 1), piece_ref[1, :, LANES:])
    return left, right


def pick(axis, even, odd):
    return jnp.where(lax.rem(lax.axis_index(BOTH[axis]), 2) == 0, even, odd)


def beside(axis, a, b):
    place = lax.axis_index(BOTH[axis])
    before = jnp.where(place == 0, 0.0, pick(axis, b, a))
    after = jnp.where(place == lax.axis_size(BOTH[axis]) - 1, 0.0, pick(axis, a, b))
    return before, after


def pack_kernel(obj_ref, colb_ref, cola_ref, held, sem, *, piece):
    first = lax.broadcasted_iota(jnp.int32, (held.shape[1], LANES), 1) < LANES // 2
    copy = pltpu.make_async_copy(obj_ref.at[piece], held, sem)
    copy.start()
    copy.wait()
    left, right = columns(held, first)
    cola_ref[...] = pick(1, right, left)
    colb_ref[...] = pick(1, left, right)


def rows_kernel(obj_ref, colb_ref, cola_ref, rowb_ref, rowa_ref, *, piece):
    half = LANES // 2
    low, high = slice(0, half), slice(obj_ref.shape[2] - half, obj_ref.shape[2])
    for part in range(2):
        for block in range(2):
            cols = slice(block * LANES, (block + 1) * LANES)
            top, bottom = obj_ref[piece, part, low, cols], obj_ref[piece, part, high, cols]
            rowa_ref[2 * part + block] = pick(0, bottom, top)
            rowb_ref[2 * part + block] = pick(0, top, bottom)
    tops = beside(1, cola_ref[low], colb_ref[low])
    bottoms = beside(1, cola_ref[high], colb_ref[high])
    for place, top, bottom in zip((4, 5), tops, bottoms):
        rowa_ref[place] = pick(0, bottom, top)
        rowb_ref[place] = pick(0, top, bottom)


def grow(ext, piece_ref, colb_ref, cola_ref, rowb_ref, rowa_ref):
    half = LANES // 2
    tile = piece_ref.shape[1]
    sides = beside(1, cola_ref[...], colb_ref[...])
    for part in range(2):
        for block in range(4):
            place = 2 * part + block - 1 if block in (1, 2) else 4 + block // 3
            top, bottom = beside(0, rowa_ref[place], rowb_ref[place])
            if block in (1, 2):
                middle = piece_ref[part, :, (block - 1) * LANES : block * LANES]
            else:
                middle = sides[block // 3]
            for strip, start in ((top, 0), (middle, half), (bottom, half + tile)):
                if (block == 0 and part == 0) or (block == 3 and part == 1):
                    strip = pltpu.roll(strip, half, 1)
                ext[part, block, start : start + strip.shape[0]] = strip


def place_window(row_ref, col_ref, slot):
    col = col_ref[0, slot] + LANES // 2
    return row_ref[0, slot], col // LANES, lax.rem(col, LANES)


def window(ext, row_ref, col_ref, slot, width):
    row, block, shift = place_window(row_ref, col_ref, slot)
    back = lax.rem(LANES - shift, LANES)
    keep = lax.broadcasted_iota(jnp.int32, (width, LANES), 1) < LANES - shift
    parts = []
    for part in range(2):
        near = pltpu.roll(ext[part, block, pl.ds(row, width), :], back, 1)
        far = pltpu.roll(ext[part, block + 1, pl.ds(row, width), :], back, 1)
        parts.append(jnp.where(keep, near, far))
    return parts


def windows(ext, row_ref, col_ref, slots, width):
    got = [window(ext, row_ref, col_ref, slot, width) for slot in slots]
    return tuple(jnp.concatenate([g[part] for g in got], axis=0) for part in range(2))


def stacked(ref, slots, part):
    return jnp.concatenate([ref[slot, part] for slot in slots], axis=0)


def store(ref, slots, values):
    width = ref.shape[2]
    for place, slot in enumerate(slots):
        for part in range(2):
            ref[slot, part] = values[part][place * width : (place + 1) * width]


def first_kernel(
    row_ref, col_ref, obj_ref, colb_ref, cola_ref, rowb_ref, rowa_ref, probe_ref, tabs_ref,
    win_ref, mid_ref, ext, *, group,
):
    width = probe_ref.shape[1]
    grow(ext, obj_ref.at[0], colb_ref, cola_ref, rowb_ref, rowa_ref)

    def some(index, _):
        slots = [group * index + place for place in range(group)]
        first_re, first_im = windows(ext, row_ref, col_ref, slots, width)
        probe_re, probe_im = (jnp.concatenate([probe_ref[p]] * group, axis=0) for p in range(2))
        wave_re = probe_re * first_re - probe_im * first_im
        wave_im = probe_re * first_im + probe_im * first_re
        store(win_ref, slots, (first_re, first_im))
        store(mid_ref, slots, two_sided(tabs_ref, 0, 1, wave_re, wave_im))
        return 0

    lax.fori_loop(0, row_ref.shape[1] // group, some, 0, unroll=True)


def second_kernel(
    row_ref, col_ref, live_ref, obj_ref, colb_ref, cola_ref, rowb_ref, rowa_ref,
    win_ref, mid_ref, measured_ref, tabs_ref,
    grad_ref, down_ref, keep_ref, send_ref,
    ext, sum_ref, *, group,
):
    width = win_ref.shape[2]
    grow(ext, obj_ref.at[1], colb_ref, cola_ref, rowb_ref, rowa_ref)
    sum_ref[...] = jnp.zeros_like(sum_ref)

    def some(index, _):
        slots = [group * index + place for place in range(group)]
        second_re, second_im = windows(ext, row_ref, col_ref, slots, width)
        mid_re, mid_im = (stacked(mid_ref, slots, part) for part in range(2))
        exit_re = mid_re * second_re - mid_im * second_im
        exit_im = mid_re * second_im + mid_im * second_re
        far_re, far_im = two_sided(tabs_ref, 2, 3, exit_re, exit_im)
        weights = []
        for place, slot in enumerate(slots):
            rows = slice(place * width, (place + 1) * width)
            active = jnp.where(slot < live_ref[0, 0], 2.0, 0.0)
            power = far_re[rows] * far_re[rows] + far_im[rows] * far_im[rows]
            weights.append((power - measured_ref[slot]) * active)
        weight = jnp.concatenate(weights, axis=0)
        chi_re, chi_im = two_sided(tabs_ref, 3, 2, weight * far_re, weight * far_im)
        grad_re = mid_re * chi_re + mid_im * chi_im
        grad_im = mid_re * chi_im - mid_im * chi_re
        store(grad_ref, slots, (grad_re, grad_im))
        back_re = second_re * chi_re + second_im * chi_im
        back_im = second_re * chi_im - second_im * chi_re
        down_re, down_im = two_sided(tabs_ref, 1, 0, back_re, back_im)
        store(down_ref, slots, (down_re, down_im))
        first_re, first_im = (stacked(win_ref, slots, part) for part in range(2))
        sum_re = first_re * down_re + first_im * down_im
        sum_im = first_re * down_im - first_im * down_re
        for part, value in enumerate((sum_re, sum_im)):
            total = value[:width]
            for start in range(width, group * width, width):
                total += value[start : start + width]
            sum_ref[part] += total
        return 0

    lax.fori_loop(0, row_ref.shape[1] // group, some, 0, unroll=True)
    keep_ref[...] = pick(1, sum_ref[0], sum_ref[1])
    send_ref[...] = pick(1, sum_ref[1], sum_ref[0])


def place_kernel(
    row_ref, col_ref, obj_ref, probe_ref, down_ref, second_ref,
    new_ref, rowb_ref, rowa_ref, left_ref, right_ref,
    grad,
):
    width = probe_ref.shape[1]
    tile = obj_ref.shape[2]
    half = width // 2
    grad[...] = jnp.zeros_like(grad)
    lane = lax.broadcasted_iota(jnp.int32, (width, LANES), 1)

    def deposit(slot, _):
        row, block, shift = place_window(row_ref, col_ref, slot)
        keep = lane >= shift
        probe_re, probe_im = probe_ref[0], probe_ref[1]
        down_re, down_im = down_ref[slot, 0], down_ref[slot, 1]
        values = (
            (probe_re * down_re + probe_im * down_im, probe_re * down_im - probe_im * down_re),
            (second_ref[slot, 0], second_ref[slot, 1]),
        )
        for piece in range(2):
            for part in range(2):
                value = pltpu.roll(values[piece][part], shift, 1)
                grad[piece, part, block, pl.ds(row, width), :] += jnp.where(keep, value, 0.0)
                grad[piece, part, block + 1, pl.ds(row, width), :] += jnp.where(keep, 0.0, value)
        return 0

    lax.fori_loop(0, row_ref.shape[1], deposit, 0)
    first = lax.broadcasted_iota(jnp.int32, (tile + width, LANES), 1) < half
    for piece in range(2):
        for part in range(2):
            for block in range(2):
                cols = slice(block * LANES, (block + 1) * LANES)
                top = grad[piece, part, 1 + block, :half]
                bottom = grad[piece, part, 1 + block, half + tile :]
                rowa_ref[piece, 2 * part + block] = pick(0, bottom, top)
                rowb_ref[piece, 2 * part + block] = pick(0, top, bottom)
                new_ref[piece, part, :, cols] = (
                    obj_ref[piece, part, :, cols]
                    - STEP_OBJECT * grad[piece, part, 1 + block, half : half + tile]
                )
        left = jnp.where(first, pltpu.roll(grad[piece, 0, 0], half, 1), grad[piece, 1, 0])
        right = jnp.where(first, grad[piece, 0, 3], pltpu.roll(grad[piece, 1, 3], half, 1))
        for place, strip, ref in ((4, left, left_ref), (5, right, right_ref)):
            top, bottom = strip[:half], strip[half + tile :]
            rowa_ref[piece, place] = pick(0, bottom, top)
            rowb_ref[piece, place] = pick(0, top, bottom)
            ref[piece] = strip[half : half + tile]


def fold_kernel(left_ref, right_ref, rowb_ref, rowa_ref, colb_ref, cola_ref):
    half = LANES // 2
    tile = left_ref.shape[1]
    for piece in range(2):
        sides = []
        for ref, place in ((left_ref, 4), (right_ref, 5)):
            top, bottom = beside(0, rowa_ref[piece, place], rowb_ref[piece, place])
            sides.append(
                (
                    ref[piece, :half] + top,
                    ref[piece, half : tile - half],
                    ref[piece, tile - half :] + bottom,
                )
            )
        for left, right, rows in zip(*sides, (slice(0, half), slice(half, tile - half), slice(tile - half, tile))):
            cola_ref[piece, rows] = pick(1, right, left)
            colb_ref[piece, rows] = pick(1, left, right)


def finish_kernel(
    part_ref, rowb_ref, rowa_ref, colb_ref, cola_ref, new_ref,
):
    tile = part_ref.shape[2]
    half = LANES // 2
    first = lax.broadcasted_iota(jnp.int32, (half, LANES), 1) < half
    for piece in range(2):
        for start in range(0, tile, half):
            rows = slice(start, start + half)
            sides = beside(1, cola_ref[piece, rows], colb_ref[piece, rows])
            for part in range(2):
                for block in range(2):
                    cols = slice(block * LANES, (block + 1) * LANES)
                    total = sides[block]
                    if block != part:
                        total = pltpu.roll(total, half, 1)
                    total = jnp.where(first == (block == 0), total, 0.0)
                    place = 2 * part + block
                    ends = beside(0, rowa_ref[piece, place], rowb_ref[piece, place])
                    if start == 0:
                        total += ends[0]
                    if start == tile - half:
                        total += ends[1]
                    new_ref[piece, part, rows, cols] = (
                        part_ref[piece, part, rows, cols] - STEP_OBJECT * total
                    )


def probe_kernel(probe_ref, mine_ref, other_ref, newp_ref, *, scale):
    newp_ref[0] = probe_ref[0] - scale * pick(1, mine_ref[...], other_ref[...])
    newp_ref[1] = probe_ref[1] - scale * pick(1, other_ref[...], mine_ref[...])


def vmem(count):
    return [pl.BlockSpec(memory_space=pltpu.VMEM)] * count


def smem(count):
    return [pl.BlockSpec(memory_space=pltpu.SMEM)] * count


def array(*shape):
    return jax.ShapeDtypeStruct(shape, jnp.float32)


def meet(strips, axis):
    sizes = (lax.axis_size("row"), lax.axis_size("col"))
    got = []
    for odd, strip in zip((1, 0), strips):
        pairs = []
        for spot in np.ndindex(*sizes):
            other = list(spot)
            place = ((spot[axis] + odd) ^ 1) - odd
            if 0 <= place < sizes[axis]:
                other[axis] = place
            else:
                other[1 - axis] ^= 1
            pairs.append((spot[0] * sizes[1] + spot[1], other[0] * sizes[1] + other[1]))
        got.append(lax.ppermute(strip, BOTH, pairs))
    return got


def swap(value, masks):
    count = lax.axis_size("row") * lax.axis_size("col")
    return lax.ppermute(value, BOTH, [(i, i ^ masks[i % 2]) for i in range(count)])


def call(kernel, out_shape, scalars, arrays, scratch=()):
    return pl.pallas_call(
        kernel, out_shape=tuple(out_shape), in_specs=smem(len(scalars)) + vmem(len(arrays)),
        out_specs=tuple(vmem(len(out_shape))), scratch_shapes=list(scratch),
        compiler_params=pltpu.CompilerParams(vmem_limit_bytes=GRANT),
    )(*scalars, *arrays)


def on_device(object_field, probe, intensity, offset_row, offset_col, live):
    tile = object_field.shape[2]
    width = probe.shape[1]
    half = width // 2
    count = offset_row.shape[1]
    side, edge, plane = (tile, LANES), (6, half, LANES), (width, width)
    field, fields = array(2, 2, tile, tile), array(count, 2, width, width)
    tabs = jnp.asarray(make_tables(width))
    grown = pltpu.VMEM((2, 4, tile + width, LANES), jnp.float32)
    packed = [
        pl.pallas_call(
            functools.partial(pack_kernel, piece=piece), out_shape=tuple([array(*side)] * 2),
            in_specs=[pl.BlockSpec(memory_space=pltpu.HBM)], out_specs=tuple(vmem(2)),
            scratch_shapes=[pltpu.VMEM((2, tile, tile), jnp.float32), pltpu.SemaphoreType.DMA],
            compiler_params=pltpu.CompilerParams(vmem_limit_bytes=GRANT),
        )(pltpu.with_memory_space_constraint(object_field, pltpu.HBM))
        for piece in range(2)
    ]
    halos = []
    cols = [meet(packed[piece], 1) for piece in range(2)]
    for piece in range(2):
        strips = call(
            functools.partial(rows_kernel, piece=piece), [array(*edge)] * 2,
            (), (object_field, *cols[piece]),
        )
        halos.append((*cols[piece], *meet(strips, 0)))
    win, mid = call(
        functools.partial(first_kernel, group=2), [fields] * 2, (offset_row, offset_col),
        (object_field, *halos[0], probe, tabs), (grown,),
    )
    grad, down, mine, send = call(
        functools.partial(second_kernel, group=count), [fields] * 2 + [array(*plane)] * 2, (offset_row, offset_col, live),
        (object_field, *halos[1], win, mid, intensity[0], tabs),
        (grown, pltpu.VMEM((2, *plane), jnp.float32)),
    )
    part, *strips, left, right = call(
        place_kernel, [field] + [array(2, *edge)] * 2 + [array(2, *side)] * 2,
        (offset_row, offset_col), (object_field, probe, down, grad),
        (pltpu.VMEM((2, 2, 4, tile + width, LANES), jnp.float32),),
    )
    mine = mine + swap(send, (1, 1))
    mine = mine + swap(mine, MASKS[0])
    mine, *strips = lax.optimization_barrier((mine, *strips))
    rows = meet(strips, 0)
    for mask in MASKS[1:4]:
        mine = mine + swap(mine, mask)
    mine, *rows = lax.optimization_barrier((mine, *rows))
    strips = call(fold_kernel, [array(2, *side)] * 2, (), (left, right, *rows))
    mine = mine + swap(mine, MASKS[4])
    mine, *strips = lax.optimization_barrier((mine, *strips))
    cols = meet(strips, 1)
    for mask in MASKS[5:]:
        mine = mine + swap(mine, mask)
    mine, *cols = lax.optimization_barrier((mine, *cols))
    (new,) = call(finish_kernel, (field,), (), (part, *rows, *cols))
    other = swap(mine, (1, 1))
    count_all = count * lax.axis_size("row") * lax.axis_size("col")
    (new_probe,) = call(
        functools.partial(probe_kernel, scale=STEP_PROBE / count_all), (array(2, *plane),),
        (), (probe, mine, other),
    )
    return new, new_probe


def solution(mesh):
    placed = (
        P(None, None, "row", "col"),
        P(),
        P("row", "col", None, None),
        P("row", "col"),
        P("row", "col"),
        P("row", "col"),
    )
    return jax.shard_map(
        on_device,
        mesh=mesh,
        in_specs=placed,
        out_specs=(P(None, None, "row", "col"), P()),
        check_vma=False,
    )
```

```python
import functools
import math

import jax
import jax.numpy as jnp
import ml_dtypes
import numpy as np
from jax import lax
from jax.experimental import pallas as pl
from jax.experimental.pallas import tpu as pltpu
from jax.sharding import PartitionSpec as P

STEP_OBJECT = 0.03
STEP_PROBE = 2.0
FRESNEL_PHASE = 60.0
LANES = 128
BOTH = ("row", "col")
GRANT = 16 * 1024 * 1024
MASKS = ((128, 4), (4, 12), (12, 128), (130, 130), (16, 32), (32, 96), (96, 16))


def split_table(table):
    high = table.astype(ml_dtypes.bfloat16)
    low = (table - high.astype(np.float64)).astype(ml_dtypes.bfloat16)
    return high, low


def make_tables(width):
    index = np.arange(width)
    four = np.exp(-2j * math.pi * (np.outer(index, index) % width) / width) / math.sqrt(width)
    freq = np.where(index < width // 2, index, index - width) / width
    hop = np.conj(four) @ np.diag(np.exp(-1j * FRESNEL_PHASE * freq**2)) @ four
    forms = []
    for table in (hop, four):
        forms.append(np.block([[table.real, table.imag], [-table.imag, table.real]]))
        forms.append(np.block([[table.real, -table.imag], [table.imag, table.real]]))
    pairs = [split_table(form) for form in forms]
    return np.stack([np.stack(pair) for pair in pairs])


def split(value):
    high = value.astype(jnp.bfloat16)
    low = (value - high.astype(jnp.float32)).astype(jnp.bfloat16)
    return high, low


def mul3(left, right):
    dot = functools.partial(jnp.dot, preferred_element_type=jnp.float32)
    return dot(left[0], right[0]) + (dot(left[1], right[0]) + dot(left[0], right[1]))


def two_sided(tabs_ref, right, left, real, imag):
    width = real.shape[1]
    starts = range(0, real.shape[0], width)
    field = split(jnp.concatenate([real, imag], axis=1))
    half = mul3(field, (tabs_ref[right, 0], tabs_ref[right, 1]))
    field = jnp.concatenate(
        [
            jnp.concatenate([half[s : s + width, :width] for s in starts], axis=1),
            jnp.concatenate([half[s : s + width, width:] for s in starts], axis=1),
        ],
        axis=0,
    )
    full = mul3((tabs_ref[left, 0], tabs_ref[left, 1]), split(field))
    return tuple(
        jnp.concatenate([full[part * width : (part + 1) * width, s : s + width] for s in starts], axis=0)
        for part in range(2)
    )


def columns(piece_ref, first):
    half = LANES // 2
    left = jnp.where(first, piece_ref[0, :, :LANES], pltpu.roll(piece_ref[1, :, :LANES], half, 1))
    right = jnp.where(first, pltpu.roll(piece_ref[0, :, LANES:], half, 1), piece_ref[1, :, LANES:])
    return left, right


def pick(axis, even, odd):
    return jnp.where(lax.rem(lax.axis_index(BOTH[axis]), 2) == 0, even, odd)


def beside(axis, a, b):
    place = lax.axis_index(BOTH[axis])
    before = jnp.where(place == 0, 0.0, pick(axis, b, a))
    after = jnp.where(place == lax.axis_size(BOTH[axis]) - 1, 0.0, pick(axis, a, b))
    return before, after


def pack_kernel(obj_ref, colb_ref, cola_ref, held, sem, *, piece):
    first = lax.broadcasted_iota(jnp.int32, (held.shape[1], LANES), 1) < LANES // 2
    copy = pltpu.make_async_copy(obj_ref.at[piece], held, sem)
    copy.start()
    copy.wait()
    left, right = columns(held, first)
    cola_ref[...] = pick(1, right, left)
    colb_ref[...] = pick(1, left, right)


def rows_kernel(obj_ref, colb_ref, cola_ref, rowa_ref, rowb_ref, *, piece):
    half = LANES // 2
    low, high = slice(0, half), slice(obj_ref.shape[2] - half, obj_ref.shape[2])
    for part in range(2):
        for block in range(2):
            cols = slice(block * LANES, (block + 1) * LANES)
            top, bottom = obj_ref[piece, part, low, cols], obj_ref[piece, part, high, cols]
            rowa_ref[2 * part + block] = pick(0, bottom, top)
            rowb_ref[2 * part + block] = pick(0, top, bottom)
    tops = beside(1, cola_ref[low], colb_ref[low])
    bottoms = beside(1, cola_ref[high], colb_ref[high])
    for place, top, bottom in zip((4, 5), tops, bottoms):
        rowa_ref[place] = pick(0, bottom, top)
        rowb_ref[place] = pick(0, top, bottom)


def grow(ext, piece_ref, colb_ref, cola_ref, rowa_ref, rowb_ref):
    half = LANES // 2
    tile = piece_ref.shape[1]
    sides = beside(1, cola_ref[...], colb_ref[...])
    for part in range(2):
        for block in range(4):
            place = 2 * part + block - 1 if block in (1, 2) else 4 + block // 3
            top, bottom = beside(0, rowa_ref[place], rowb_ref[place])
            if block in (1, 2):
                middle = piece_ref[part, :, (block - 1) * LANES : block * LANES]
            else:
                middle = sides[block // 3]
            for strip, start in ((top, 0), (middle, half), (bottom, half + tile)):
                if (block == 0 and part == 0) or (block == 3 and part == 1):
                    strip = pltpu.roll(strip, half, 1)
                ext[part, block, start : start + strip.shape[0]] = strip


def place_window(row_ref, col_ref, slot):
    col = col_ref[0, slot] + LANES // 2
    return row_ref[0, slot], col // LANES, lax.rem(col, LANES)


def window(ext, row_ref, col_ref, slot, width):
    row, block, shift = place_window(row_ref, col_ref, slot)
    back = lax.rem(LANES - shift, LANES)
    keep = lax.broadcasted_iota(jnp.int32, (width, LANES), 1) < LANES - shift
    parts = []
    for part in range(2):
        near = pltpu.roll(ext[part, block, pl.ds(row, width), :], back, 1)
        far = pltpu.roll(ext[part, block + 1, pl.ds(row, width), :], back, 1)
        parts.append(jnp.where(keep, near, far))
    return parts


def windows(ext, row_ref, col_ref, slots, width):
    got = [window(ext, row_ref, col_ref, slot, width) for slot in slots]
    return tuple(jnp.concatenate([g[part] for g in got], axis=0) for part in range(2))


def stacked(ref, slots, part):
    return jnp.concatenate([ref[slot, part] for slot in slots], axis=0)


def store(ref, slots, values):
    width = ref.shape[2]
    for place, slot in enumerate(slots):
        for part in range(2):
            ref[slot, part] = values[part][place * width : (place + 1) * width]


def first_kernel(
    row_ref, col_ref, obj_ref, colb_ref, cola_ref, rowa_ref, rowb_ref, probe_ref, tabs_ref,
    win_ref, mid_ref, ext, *, group,
):
    width = probe_ref.shape[1]
    grow(ext, obj_ref.at[0], colb_ref, cola_ref, rowa_ref, rowb_ref)

    def some(index, _):
        slots = [group * index + place for place in range(group)]
        first_re, first_im = windows(ext, row_ref, col_ref, slots, width)
        probe_re, probe_im = (jnp.concatenate([probe_ref[p]] * group, axis=0) for p in range(2))
        wave_re = probe_re * first_re - probe_im * first_im
        wave_im = probe_re * first_im + probe_im * first_re
        store(win_ref, slots, (first_re, first_im))
        store(mid_ref, slots, two_sided(tabs_ref, 0, 1, wave_re, wave_im))
        return 0

    lax.fori_loop(0, row_ref.shape[1] // group, some, 0, unroll=True)


def second_kernel(
    row_ref, col_ref, live_ref, obj_ref, colb_ref, cola_ref, rowa_ref, rowb_ref,
    win_ref, mid_ref, measured_ref, tabs_ref,
    grad_ref, down_ref, keep_ref, send_ref,
    ext, sum_ref, *, group,
):
    width = win_ref.shape[2]
    grow(ext, obj_ref.at[1], colb_ref, cola_ref, rowa_ref, rowb_ref)
    sum_ref[...] = jnp.zeros_like(sum_ref)

    def some(index, _):
        slots = [group * index + place for place in range(group)]
        second_re, second_im = windows(ext, row_ref, col_ref, slots, width)
        mid_re, mid_im = (stacked(mid_ref, slots, part) for part in range(2))
        exit_re = mid_re * second_re - mid_im * second_im
        exit_im = mid_re * second_im + mid_im * second_re
        far_re, far_im = two_sided(tabs_ref, 2, 3, exit_re, exit_im)
        weights = []
        for place, slot in enumerate(slots):
            rows = slice(place * width, (place + 1) * width)
            active = jnp.where(slot < live_ref[0, 0], 2.0, 0.0)
            power = far_re[rows] * far_re[rows] + far_im[rows] * far_im[rows]
            weights.append((power - measured_ref[slot]) * active)
        weight = jnp.concatenate(weights, axis=0)
        chi_re, chi_im = two_sided(tabs_ref, 3, 2, weight * far_re, weight * far_im)
        grad_re = mid_re * chi_re + mid_im * chi_im
        grad_im = mid_re * chi_im - mid_im * chi_re
        store(grad_ref, slots, (grad_re, grad_im))
        back_re = second_re * chi_re + second_im * chi_im
        back_im = second_re * chi_im - second_im * chi_re
        down_re, down_im = two_sided(tabs_ref, 1, 0, back_re, back_im)
        store(down_ref, slots, (down_re, down_im))
        first_re, first_im = (stacked(win_ref, slots, part) for part in range(2))
        sum_re = first_re * down_re + first_im * down_im
        sum_im = first_re * down_im - first_im * down_re
        for part, value in enumerate((sum_re, sum_im)):
            total = value[:width]
            for start in range(width, group * width, width):
                total += value[start : start + width]
            sum_ref[part] += total
        return 0

    lax.fori_loop(0, row_ref.shape[1] // group, some, 0, unroll=True)
    keep_ref[...] = pick(1, sum_ref[0], sum_ref[1])
    send_ref[...] = pick(1, sum_ref[1], sum_ref[0])


def place_kernel(
    row_ref, col_ref, obj_ref, probe_ref, down_ref, second_ref,
    new_ref, rowa_ref, rowb_ref, left_ref, right_ref,
    grad,
):
    width = probe_ref.shape[1]
    tile = obj_ref.shape[2]
    half = width // 2
    grad[...] = jnp.zeros_like(grad)
    lane = lax.broadcasted_iota(jnp.int32, (width, LANES), 1)

    def deposit(slot, _):
        row, block, shift = place_window(row_ref, col_ref, slot)
        keep = lane >= shift
        probe_re, probe_im = probe_ref[0], probe_ref[1]
        down_re, down_im = down_ref[slot, 0], down_ref[slot, 1]
        values = (
            (probe_re * down_re + probe_im * down_im, probe_re * down_im - probe_im * down_re),
            (second_ref[slot, 0], second_ref[slot, 1]),
        )
        for piece in range(2):
            for part in range(2):
                value = pltpu.roll(values[piece][part], shift, 1)
                grad[piece, part, block, pl.ds(row, width), :] += jnp.where(keep, value, 0.0)
                grad[piece, part, block + 1, pl.ds(row, width), :] += jnp.where(keep, 0.0, value)
        return 0

    lax.fori_loop(0, row_ref.shape[1], deposit, 0)
    first = lax.broadcasted_iota(jnp.int32, (tile + width, LANES), 1) < half
    for piece in range(2):
        for part in range(2):
            for block in range(2):
                cols = slice(block * LANES, (block + 1) * LANES)
                top = grad[piece, part, 1 + block, :half]
                bottom = grad[piece, part, 1 + block, half + tile :]
                rowa_ref[piece, 2 * part + block] = pick(0, bottom, top)
                rowb_ref[piece, 2 * part + block] = pick(0, top, bottom)
                new_ref[piece, part, :, cols] = (
                    obj_ref[piece, part, :, cols]
                    - STEP_OBJECT * grad[piece, part, 1 + block, half : half + tile]
                )
        left = jnp.where(first, pltpu.roll(grad[piece, 0, 0], half, 1), grad[piece, 1, 0])
        right = jnp.where(first, grad[piece, 0, 3], pltpu.roll(grad[piece, 1, 3], half, 1))
        for place, strip, ref in ((4, left, left_ref), (5, right, right_ref)):
            top, bottom = strip[:half], strip[half + tile :]
            rowa_ref[piece, place] = pick(0, bottom, top)
            rowb_ref[piece, place] = pick(0, top, bottom)
            ref[piece] = strip[half : half + tile]


def fold_kernel(left_ref, right_ref, rowa_ref, rowb_ref, colb_ref, cola_ref):
    half = LANES // 2
    tile = left_ref.shape[1]
    for piece in range(2):
        sides = []
        for ref, place in ((left_ref, 4), (right_ref, 5)):
            top, bottom = beside(0, rowa_ref[piece, place], rowb_ref[piece, place])
            sides.append(
                (
                    ref[piece, :half] + top,
                    ref[piece, half : tile - half],
                    ref[piece, tile - half :] + bottom,
                )
            )
        for left, right, rows in zip(*sides, (slice(0, half), slice(half, tile - half), slice(tile - half, tile))):
            cola_ref[piece, rows] = pick(1, right, left)
            colb_ref[piece, rows] = pick(1, left, right)


def finish_kernel(
    part_ref, rowa_ref, rowb_ref, colb_ref, cola_ref, new_ref,
):
    tile = part_ref.shape[2]
    half = LANES // 2
    first = lax.broadcasted_iota(jnp.int32, (half, LANES), 1) < half
    for piece in range(2):
        for start in range(0, tile, half):
            rows = slice(start, start + half)
            sides = beside(1, cola_ref[piece, rows], colb_ref[piece, rows])
            for part in range(2):
                for block in range(2):
                    cols = slice(block * LANES, (block + 1) * LANES)
                    total = sides[block]
                    if block != part:
                        total = pltpu.roll(total, half, 1)
                    total = jnp.where(first == (block == 0), total, 0.0)
                    place = 2 * part + block
                    ends = beside(0, rowa_ref[piece, place], rowb_ref[piece, place])
                    if start == 0:
                        total += ends[0]
                    if start == tile - half:
                        total += ends[1]
                    new_ref[piece, part, rows, cols] = (
                        part_ref[piece, part, rows, cols] - STEP_OBJECT * total
                    )


def probe_kernel(probe_ref, mine_ref, other_ref, newp_ref, *, scale):
    newp_ref[0] = probe_ref[0] - scale * pick(1, mine_ref[...], other_ref[...])
    newp_ref[1] = probe_ref[1] - scale * pick(1, other_ref[...], mine_ref[...])


def vmem(count):
    return [pl.BlockSpec(memory_space=pltpu.VMEM)] * count


def smem(count):
    return [pl.BlockSpec(memory_space=pltpu.SMEM)] * count


def array(*shape):
    return jax.ShapeDtypeStruct(shape, jnp.float32)


def meet(strips, axis):
    sizes = (lax.axis_size("row"), lax.axis_size("col"))
    got = []
    for odd, strip in zip((axis, 1 - axis), strips):
        pairs = []
        for spot in np.ndindex(*sizes):
            other = list(spot)
            place = ((spot[axis] + odd) ^ 1) - odd
            if 0 <= place < sizes[axis]:
                other[axis] = place
            else:
                other[1 - axis] ^= 1
            pairs.append((spot[0] * sizes[1] + spot[1], other[0] * sizes[1] + other[1]))
        got.append(lax.ppermute(strip, BOTH, pairs))
    return got


def swap(value, masks):
    count = lax.axis_size("row") * lax.axis_size("col")
    return lax.ppermute(value, BOTH, [(i, i ^ masks[i % 2]) for i in range(count)])


def call(kernel, out_shape, scalars, arrays, scratch=()):
    return pl.pallas_call(
        kernel, out_shape=tuple(out_shape), in_specs=smem(len(scalars)) + vmem(len(arrays)),
        out_specs=tuple(vmem(len(out_shape))), scratch_shapes=list(scratch),
        compiler_params=pltpu.CompilerParams(vmem_limit_bytes=GRANT),
    )(*scalars, *arrays)


def on_device(object_field, probe, intensity, offset_row, offset_col, live):
    tile = object_field.shape[2]
    width = probe.shape[1]
    half = width // 2
    count = offset_row.shape[1]
    side, edge, plane = (tile, LANES), (6, half, LANES), (width, width)
    field, fields = array(2, 2, tile, tile), array(count, 2, width, width)
    tabs = jnp.asarray(make_tables(width))
    grown = pltpu.VMEM((2, 4, tile + width, LANES), jnp.float32)
    packed = [
        pl.pallas_call(
            functools.partial(pack_kernel, piece=piece), out_shape=tuple([array(*side)] * 2),
            in_specs=[pl.BlockSpec(memory_space=pltpu.HBM)], out_specs=tuple(vmem(2)),
            scratch_shapes=[pltpu.VMEM((2, tile, tile), jnp.float32), pltpu.SemaphoreType.DMA],
            compiler_params=pltpu.CompilerParams(vmem_limit_bytes=GRANT),
        )(pltpu.with_memory_space_constraint(object_field, pltpu.HBM))
        for piece in range(2)
    ]
    halos = []
    cols = [meet(packed[piece], 1) for piece in range(2)]
    for piece in range(2):
        strips = call(
            functools.partial(rows_kernel, piece=piece), [array(*edge)] * 2,
            (), (object_field, *cols[piece]),
        )
        halos.append((*cols[piece], *meet(strips, 0)))
    win, mid = call(
        functools.partial(first_kernel, group=2), [fields] * 2, (offset_row, offset_col),
        (object_field, *halos[0], probe, tabs), (grown,),
    )
    grad, down, mine, send = call(
        functools.partial(second_kernel, group=count), [fields] * 2 + [array(*plane)] * 2, (offset_row, offset_col, live),
        (object_field, *halos[1], win, mid, intensity[0], tabs),
        (grown, pltpu.VMEM((2, *plane), jnp.float32)),
    )
    part, *strips, left, right = call(
        place_kernel, [field] + [array(2, *edge)] * 2 + [array(2, *side)] * 2,
        (offset_row, offset_col), (object_field, probe, down, grad),
        (pltpu.VMEM((2, 2, 4, tile + width, LANES), jnp.float32),),
    )
    mine = mine + swap(send, (1, 1))
    mine = mine + swap(mine, MASKS[0])
    mine, *strips = lax.optimization_barrier((mine, *strips))
    rows = meet(strips, 0)
    for mask in MASKS[1:4]:
        mine = mine + swap(mine, mask)
    mine, *rows = lax.optimization_barrier((mine, *rows))
    strips = call(fold_kernel, [array(2, *side)] * 2, (), (left, right, *rows))
    mine = mine + swap(mine, MASKS[4])
    mine, *strips = lax.optimization_barrier((mine, *strips))
    cols = meet(strips, 1)
    for mask in MASKS[5:]:
        mine = mine + swap(mine, mask)
    mine, *cols = lax.optimization_barrier((mine, *cols))
    (new,) = call(finish_kernel, (field,), (), (part, *rows, *cols))
    other = swap(mine, (1, 1))
    count_all = count * lax.axis_size("row") * lax.axis_size("col")
    (new_probe,) = call(
        functools.partial(probe_kernel, scale=STEP_PROBE / count_all), (array(2, *plane),),
        (), (probe, mine, other),
    )
    return new, new_probe


def solution(mesh):
    placed = (
        P(None, None, "row", "col"),
        P(),
        P("row", "col", None, None),
        P("row", "col"),
        P("row", "col"),
        P("row", "col"),
    )
    return jax.shard_map(
        on_device,
        mesh=mesh,
        in_specs=placed,
        out_specs=(P(None, None, "row", "col"), P()),
        check_vma=False,
    )
```

```python
import functools
import math

import jax
import jax.numpy as jnp
import ml_dtypes
import numpy as np
from jax import lax
from jax.experimental import pallas as pl
from jax.experimental.pallas import tpu as pltpu
from jax.sharding import PartitionSpec as P

STEP_OBJECT = 0.03
STEP_PROBE = 2.0
FRESNEL_PHASE = 60.0
LANES = 128
BOTH = ("row", "col")
GRANT = 16 * 1024 * 1024
MASKS = ((16, 16), (4, 12), (12, 4), (128, 130), (130, 128), (32, 96), (96, 32))


def split_table(table):
    high = table.astype(ml_dtypes.bfloat16)
    low = (table - high.astype(np.float64)).astype(ml_dtypes.bfloat16)
    return high, low


def make_tables(width):
    index = np.arange(width)
    four = np.exp(-2j * math.pi * (np.outer(index, index) % width) / width) / math.sqrt(width)
    freq = np.where(index < width // 2, index, index - width) / width
    hop = np.conj(four) @ np.diag(np.exp(-1j * FRESNEL_PHASE * freq**2)) @ four
    forms = []
    for table in (hop, four):
        forms.append(np.block([[table.real, table.imag], [-table.imag, table.real]]))
        forms.append(np.block([[table.real, -table.imag], [table.imag, table.real]]))
    pairs = [split_table(form) for form in forms]
    return np.stack([np.stack(pair) for pair in pairs])


def split(value):
    high = value.astype(jnp.bfloat16)
    low = (value - high.astype(jnp.float32)).astype(jnp.bfloat16)
    return high, low


def mul3(left, right):
    dot = functools.partial(jnp.dot, preferred_element_type=jnp.float32)
    return dot(left[0], right[0]) + (dot(left[1], right[0]) + dot(left[0], right[1]))


def two_sided(tabs_ref, right, left, real, imag):
    width = real.shape[1]
    starts = range(0, real.shape[0], width)
    field = split(jnp.concatenate([real, imag], axis=1))
    half = mul3(field, (tabs_ref[right, 0], tabs_ref[right, 1]))
    field = jnp.concatenate(
        [
            jnp.concatenate([half[s : s + width, :width] for s in starts], axis=1),
            jnp.concatenate([half[s : s + width, width:] for s in starts], axis=1),
        ],
        axis=0,
    )
    full = mul3((tabs_ref[left, 0], tabs_ref[left, 1]), split(field))
    return tuple(
        jnp.concatenate([full[part * width : (part + 1) * width, s : s + width] for s in starts], axis=0)
        for part in range(2)
    )


def columns(piece_ref, first):
    half = LANES // 2
    left = jnp.where(first, piece_ref[0, :, :LANES], pltpu.roll(piece_ref[1, :, :LANES], half, 1))
    right = jnp.where(first, pltpu.roll(piece_ref[0, :, LANES:], half, 1), piece_ref[1, :, LANES:])
    return left, right


def pick(axis, even, odd):
    return jnp.where(lax.rem(lax.axis_index(BOTH[axis]), 2) == 0, even, odd)


def beside(axis, a, b):
    place = lax.axis_index(BOTH[axis])
    before = jnp.where(place == 0, 0.0, pick(axis, b, a))
    after = jnp.where(place == lax.axis_size(BOTH[axis]) - 1, 0.0, pick(axis, a, b))
    return before, after


def pack_kernel(obj_ref, colb_ref, cola_ref, held, sem, *, piece):
    first = lax.broadcasted_iota(jnp.int32, (held.shape[1], LANES), 1) < LANES // 2
    copy = pltpu.make_async_copy(obj_ref.at[piece], held, sem)
    copy.start()
    copy.wait()
    left, right = columns(held, first)
    cola_ref[...] = pick(1, right, left)
    colb_ref[...] = pick(1, left, right)


def rows_kernel(obj_ref, colb_ref, cola_ref, rowa_ref, rowb_ref, *, piece):
    half = LANES // 2
    low, high = slice(0, half), slice(obj_ref.shape[2] - half, obj_ref.shape[2])
    for part in range(2):
        for block in range(2):
            cols = slice(block * LANES, (block + 1) * LANES)
            top, bottom = obj_ref[piece, part, low, cols], obj_ref[piece, part, high, cols]
            rowa_ref[2 * part + block] = pick(0, bottom, top)
            rowb_ref[2 * part + block] = pick(0, top, bottom)
    tops = beside(1, cola_ref[low], colb_ref[low])
    bottoms = beside(1, cola_ref[high], colb_ref[high])
    for place, top, bottom in zip((4, 5), tops, bottoms):
        rowa_ref[place] = pick(0, bottom, top)
        rowb_ref[place] = pick(0, top, bottom)


def grow(ext, piece_ref, colb_ref, cola_ref, rowa_ref, rowb_ref):
    half = LANES // 2
    tile = piece_ref.shape[1]
    sides = beside(1, cola_ref[...], colb_ref[...])
    for part in range(2):
        for block in range(4):
            place = 2 * part + block - 1 if block in (1, 2) else 4 + block // 3
            top, bottom = beside(0, rowa_ref[place], rowb_ref[place])
            if block in (1, 2):
                middle = piece_ref[part, :, (block - 1) * LANES : block * LANES]
            else:
                middle = sides[block // 3]
            for strip, start in ((top, 0), (middle, half), (bottom, half + tile)):
                if (block == 0 and part == 0) or (block == 3 and part == 1):
                    strip = pltpu.roll(strip, half, 1)
                ext[part, block, start : start + strip.shape[0]] = strip


def place_window(row_ref, col_ref, slot):
    col = col_ref[0, slot] + LANES // 2
    return row_ref[0, slot], col // LANES, lax.rem(col, LANES)


def window(ext, row_ref, col_ref, slot, width):
    row, block, shift = place_window(row_ref, col_ref, slot)
    back = lax.rem(LANES - shift, LANES)
    keep = lax.broadcasted_iota(jnp.int32, (width, LANES), 1) < LANES - shift
    parts = []
    for part in range(2):
        near = pltpu.roll(ext[part, block, pl.ds(row, width), :], back, 1)
        far = pltpu.roll(ext[part, block + 1, pl.ds(row, width), :], back, 1)
        parts.append(jnp.where(keep, near, far))
    return parts


def windows(ext, row_ref, col_ref, slots, width):
    got = [window(ext, row_ref, col_ref, slot, width) for slot in slots]
    return tuple(jnp.concatenate([g[part] for g in got], axis=0) for part in range(2))


def stacked(ref, slots, part):
    return jnp.concatenate([ref[slot, part] for slot in slots], axis=0)


def store(ref, slots, values):
    width = ref.shape[2]
    for place, slot in enumerate(slots):
        for part in range(2):
            ref[slot, part] = values[part][place * width : (place + 1) * width]


def first_kernel(
    row_ref, col_ref, obj_ref, colb_ref, cola_ref, rowa_ref, rowb_ref, probe_ref, tabs_ref,
    win_ref, mid_ref, ext, *, group,
):
    width = probe_ref.shape[1]
    grow(ext, obj_ref.at[0], colb_ref, cola_ref, rowa_ref, rowb_ref)

    def some(index, _):
        slots = [group * index + place for place in range(group)]
        first_re, first_im = windows(ext, row_ref, col_ref, slots, width)
        probe_re, probe_im = (jnp.concatenate([probe_ref[p]] * group, axis=0) for p in range(2))
        wave_re = probe_re * first_re - probe_im * first_im
        wave_im = probe_re * first_im + probe_im * first_re
        store(win_ref, slots, (first_re, first_im))
        store(mid_ref, slots, two_sided(tabs_ref, 0, 1, wave_re, wave_im))
        return 0

    lax.fori_loop(0, row_ref.shape[1] // group, some, 0, unroll=True)


def second_kernel(
    row_ref, col_ref, live_ref, obj_ref, colb_ref, cola_ref, rowa_ref, rowb_ref,
    win_ref, mid_ref, measured_ref, tabs_ref,
    grad_ref, down_ref, keep_ref, send_ref,
    ext, sum_ref, *, group,
):
    width = win_ref.shape[2]
    grow(ext, obj_ref.at[1], colb_ref, cola_ref, rowa_ref, rowb_ref)
    sum_ref[...] = jnp.zeros_like(sum_ref)

    def some(index, _):
        slots = [group * index + place for place in range(group)]
        second_re, second_im = windows(ext, row_ref, col_ref, slots, width)
        mid_re, mid_im = (stacked(mid_ref, slots, part) for part in range(2))
        exit_re = mid_re * second_re - mid_im * second_im
        exit_im = mid_re * second_im + mid_im * second_re
        far_re, far_im = two_sided(tabs_ref, 2, 3, exit_re, exit_im)
        weights = []
        for place, slot in enumerate(slots):
            rows = slice(place * width, (place + 1) * width)
            active = jnp.where(slot < live_ref[0, 0], 2.0, 0.0)
            power = far_re[rows] * far_re[rows] + far_im[rows] * far_im[rows]
            weights.append((power - measured_ref[slot]) * active)
        weight = jnp.concatenate(weights, axis=0)
        chi_re, chi_im = two_sided(tabs_ref, 3, 2, weight * far_re, weight * far_im)
        grad_re = mid_re * chi_re + mid_im * chi_im
        grad_im = mid_re * chi_im - mid_im * chi_re
        store(grad_ref, slots, (grad_re, grad_im))
        back_re = second_re * chi_re + second_im * chi_im
        back_im = second_re * chi_im - second_im * chi_re
        down_re, down_im = two_sided(tabs_ref, 1, 0, back_re, back_im)
        store(down_ref, slots, (down_re, down_im))
        first_re, first_im = (stacked(win_ref, slots, part) for part in range(2))
        sum_re = first_re * down_re + first_im * down_im
        sum_im = first_re * down_im - first_im * down_re
        for part, value in enumerate((sum_re, sum_im)):
            total = value[:width]
            for start in range(width, group * width, width):
                total += value[start : start + width]
            sum_ref[part] += total
        return 0

    lax.fori_loop(0, row_ref.shape[1] // group, some, 0, unroll=True)
    keep_ref[...] = pick(1, sum_ref[0], sum_ref[1])
    send_ref[...] = pick(1, sum_ref[1], sum_ref[0])


def place_kernel(
    row_ref, col_ref, obj_ref, probe_ref, down_ref, second_ref,
    new_ref, rowa_ref, rowb_ref, left_ref, right_ref,
    grad,
):
    width = probe_ref.shape[1]
    tile = obj_ref.shape[2]
    half = width // 2
    grad[...] = jnp.zeros_like(grad)
    lane = lax.broadcasted_iota(jnp.int32, (width, LANES), 1)

    def deposit(slot, _):
        row, block, shift = place_window(row_ref, col_ref, slot)
        keep = lane >= shift
        probe_re, probe_im = probe_ref[0], probe_ref[1]
        down_re, down_im = down_ref[slot, 0], down_ref[slot, 1]
        values = (
            (probe_re * down_re + probe_im * down_im, probe_re * down_im - probe_im * down_re),
            (second_ref[slot, 0], second_ref[slot, 1]),
        )
        for piece in range(2):
            for part in range(2):
                value = pltpu.roll(values[piece][part], shift, 1)
                grad[piece, part, block, pl.ds(row, width), :] += jnp.where(keep, value, 0.0)
                grad[piece, part, block + 1, pl.ds(row, width), :] += jnp.where(keep, 0.0, value)
        return 0

    lax.fori_loop(0, row_ref.shape[1], deposit, 0)
    first = lax.broadcasted_iota(jnp.int32, (tile + width, LANES), 1) < half
    for piece in range(2):
        for part in range(2):
            for block in range(2):
                cols = slice(block * LANES, (block + 1) * LANES)
                top = grad[piece, part, 1 + block, :half]
                bottom = grad[piece, part, 1 + block, half + tile :]
                rowa_ref[piece, 2 * part + block] = pick(0, bottom, top)
                rowb_ref[piece, 2 * part + block] = pick(0, top, bottom)
                new_ref[piece, part, :, cols] = (
                    obj_ref[piece, part, :, cols]
                    - STEP_OBJECT * grad[piece, part, 1 + block, half : half + tile]
                )
        left = jnp.where(first, pltpu.roll(grad[piece, 0, 0], half, 1), grad[piece, 1, 0])
        right = jnp.where(first, grad[piece, 0, 3], pltpu.roll(grad[piece, 1, 3], half, 1))
        for place, strip, ref in ((4, left, left_ref), (5, right, right_ref)):
            top, bottom = strip[:half], strip[half + tile :]
            rowa_ref[piece, place] = pick(0, bottom, top)
            rowb_ref[piece, place] = pick(0, top, bottom)
            ref[piece] = strip[half : half + tile]


def fold_kernel(left_ref, right_ref, rowa_ref, rowb_ref, colb_ref, cola_ref):
    half = LANES // 2
    tile = left_ref.shape[1]
    for piece in range(2):
        sides = []
        for ref, place in ((left_ref, 4), (right_ref, 5)):
            top, bottom = beside(0, rowa_ref[piece, place], rowb_ref[piece, place])
            sides.append(
                (
                    ref[piece, :half] + top,
                    ref[piece, half : tile - half],
                    ref[piece, tile - half :] + bottom,
                )
            )
        for left, right, rows in zip(*sides, (slice(0, half), slice(half, tile - half), slice(tile - half, tile))):
            cola_ref[piece, rows] = pick(1, right, left)
            colb_ref[piece, rows] = pick(1, left, right)


def finish_kernel(
    part_ref, rowa_ref, rowb_ref, colb_ref, cola_ref, new_ref,
):
    tile = part_ref.shape[2]
    half = LANES // 2
    first = lax.broadcasted_iota(jnp.int32, (half, LANES), 1) < half
    for piece in range(2):
        for start in range(0, tile, half):
            rows = slice(start, start + half)
            sides = beside(1, cola_ref[piece, rows], colb_ref[piece, rows])
            for part in range(2):
                for block in range(2):
                    cols = slice(block * LANES, (block + 1) * LANES)
                    total = sides[block]
                    if block != part:
                        total = pltpu.roll(total, half, 1)
                    total = jnp.where(first == (block == 0), total, 0.0)
                    place = 2 * part + block
                    ends = beside(0, rowa_ref[piece, place], rowb_ref[piece, place])
                    if start == 0:
                        total += ends[0]
                    if start == tile - half:
                        total += ends[1]
                    new_ref[piece, part, rows, cols] = (
                        part_ref[piece, part, rows, cols] - STEP_OBJECT * total
                    )


def probe_kernel(probe_ref, mine_ref, other_ref, newp_ref, *, scale):
    newp_ref[0] = probe_ref[0] - scale * pick(1, mine_ref[...], other_ref[...])
    newp_ref[1] = probe_ref[1] - scale * pick(1, other_ref[...], mine_ref[...])


def vmem(count):
    return [pl.BlockSpec(memory_space=pltpu.VMEM)] * count


def smem(count):
    return [pl.BlockSpec(memory_space=pltpu.SMEM)] * count


def array(*shape):
    return jax.ShapeDtypeStruct(shape, jnp.float32)


def meet(strips, axis):
    sizes = (lax.axis_size("row"), lax.axis_size("col"))
    got = []
    for odd, strip in zip((axis, 1 - axis), strips):
        pairs = []
        for spot in np.ndindex(*sizes):
            other = list(spot)
            place = ((spot[axis] + odd) ^ 1) - odd
            if 0 <= place < sizes[axis]:
                other[axis] = place
            else:
                other[1 - axis] ^= 1
            pairs.append((spot[0] * sizes[1] + spot[1], other[0] * sizes[1] + other[1]))
        got.append(lax.ppermute(strip, BOTH, pairs))
    return got


def swap(value, masks):
    count = lax.axis_size("row") * lax.axis_size("col")
    return lax.ppermute(value, BOTH, [(i, i ^ masks[i % 2]) for i in range(count)])


def call(kernel, out_shape, scalars, arrays, scratch=()):
    return pl.pallas_call(
        kernel, out_shape=tuple(out_shape), in_specs=smem(len(scalars)) + vmem(len(arrays)),
        out_specs=tuple(vmem(len(out_shape))), scratch_shapes=list(scratch),
        compiler_params=pltpu.CompilerParams(vmem_limit_bytes=GRANT),
    )(*scalars, *arrays)


def on_device(object_field, probe, intensity, offset_row, offset_col, live):
    tile = object_field.shape[2]
    width = probe.shape[1]
    half = width // 2
    count = offset_row.shape[1]
    side, edge, plane = (tile, LANES), (6, half, LANES), (width, width)
    field, fields = array(2, 2, tile, tile), array(count, 2, width, width)
    tabs = jnp.asarray(make_tables(width))
    grown = pltpu.VMEM((2, 4, tile + width, LANES), jnp.float32)
    packed = [
        pl.pallas_call(
            functools.partial(pack_kernel, piece=piece), out_shape=tuple([array(*side)] * 2),
            in_specs=[pl.BlockSpec(memory_space=pltpu.HBM)], out_specs=tuple(vmem(2)),
            scratch_shapes=[pltpu.VMEM((2, tile, tile), jnp.float32), pltpu.SemaphoreType.DMA],
            compiler_params=pltpu.CompilerParams(vmem_limit_bytes=GRANT),
        )(pltpu.with_memory_space_constraint(object_field, pltpu.HBM))
        for piece in range(2)
    ]
    halos = []
    cols = [meet(packed[piece], 1) for piece in range(2)]
    for piece in range(2):
        strips = call(
            functools.partial(rows_kernel, piece=piece), [array(*edge)] * 2,
            (), (object_field, *cols[piece]),
        )
        halos.append((*cols[piece], *meet(strips, 0)))
    win, mid = call(
        functools.partial(first_kernel, group=2), [fields] * 2, (offset_row, offset_col),
        (object_field, *halos[0], probe, tabs), (grown,),
    )
    grad, down, mine, send = call(
        functools.partial(second_kernel, group=count), [fields] * 2 + [array(*plane)] * 2, (offset_row, offset_col, live),
        (object_field, *halos[1], win, mid, intensity[0], tabs),
        (grown, pltpu.VMEM((2, *plane), jnp.float32)),
    )
    part, *strips, left, right = call(
        place_kernel, [field] + [array(2, *edge)] * 2 + [array(2, *side)] * 2,
        (offset_row, offset_col), (object_field, probe, down, grad),
        (pltpu.VMEM((2, 2, 4, tile + width, LANES), jnp.float32),),
    )
    mine = mine + swap(send, (1, 1))
    mine = mine + swap(mine, MASKS[0])
    mine, *strips = lax.optimization_barrier((mine, *strips))
    rows = meet(strips, 0)
    for mask in MASKS[1:4]:
        mine = mine + swap(mine, mask)
    mine, *rows = lax.optimization_barrier((mine, *rows))
    strips = call(fold_kernel, [array(2, *side)] * 2, (), (left, right, *rows))
    mine = mine + swap(mine, MASKS[4])
    mine, *strips = lax.optimization_barrier((mine, *strips))
    cols = meet(strips, 1)
    for mask in MASKS[5:]:
        mine = mine + swap(mine, mask)
    mine, *cols = lax.optimization_barrier((mine, *cols))
    (new,) = call(finish_kernel, (field,), (), (part, *rows, *cols))
    other = swap(mine, (1, 1))
    count_all = count * lax.axis_size("row") * lax.axis_size("col")
    (new_probe,) = call(
        functools.partial(probe_kernel, scale=STEP_PROBE / count_all), (array(2, *plane),),
        (), (probe, mine, other),
    )
    return new, new_probe


def solution(mesh):
    placed = (
        P(None, None, "row", "col"),
        P(),
        P("row", "col", None, None),
        P("row", "col"),
        P("row", "col"),
        P("row", "col"),
    )
    return jax.shard_map(
        on_device,
        mesh=mesh,
        in_specs=placed,
        out_specs=(P(None, None, "row", "col"), P()),
        check_vma=False,
    )
```

```python
import functools
import math

import jax
import jax.numpy as jnp
import ml_dtypes
import numpy as np
from jax import lax
from jax.experimental import pallas as pl
from jax.experimental.pallas import tpu as pltpu
from jax.sharding import PartitionSpec as P

STEP_OBJECT = 0.03
STEP_PROBE = 2.0
FRESNEL_PHASE = 60.0
LANES = 128
BOTH = ("row", "col")
GRANT = 16 * 1024 * 1024
MASKS = ((16, 16), (4, 12), (12, 4), (128, 130), (130, 128), (32, 96), (96, 32))


def split_table(table):
    high = table.astype(ml_dtypes.bfloat16)
    low = (table - high.astype(np.float64)).astype(ml_dtypes.bfloat16)
    return high, low


def make_tables(width):
    index = np.arange(width)
    four = np.exp(-2j * math.pi * (np.outer(index, index) % width) / width) / math.sqrt(width)
    freq = np.where(index < width // 2, index, index - width) / width
    hop = np.conj(four) @ np.diag(np.exp(-1j * FRESNEL_PHASE * freq**2)) @ four
    forms = []
    for table in (hop, four):
        forms.append(np.block([[table.real, table.imag], [-table.imag, table.real]]))
        forms.append(np.block([[table.real, -table.imag], [table.imag, table.real]]))
    pairs = [split_table(form) for form in forms]
    return np.stack([np.stack(pair) for pair in pairs])


def split(value):
    high = value.astype(jnp.bfloat16)
    low = (value - high.astype(jnp.float32)).astype(jnp.bfloat16)
    return high, low


def mul3(left, right):
    dot = functools.partial(jnp.dot, preferred_element_type=jnp.float32)
    return dot(left[0], right[0]) + (dot(left[1], right[0]) + dot(left[0], right[1]))


def two_sided(tabs_ref, right, left, real, imag):
    width = real.shape[1]
    starts = range(0, real.shape[0], width)
    field = split(jnp.concatenate([real, imag], axis=1))
    half = mul3(field, (tabs_ref[right, 0], tabs_ref[right, 1]))
    field = jnp.concatenate(
        [
            jnp.concatenate([half[s : s + width, :width] for s in starts], axis=1),
            jnp.concatenate([half[s : s + width, width:] for s in starts], axis=1),
        ],
        axis=0,
    )
    full = mul3((tabs_ref[left, 0], tabs_ref[left, 1]), split(field))
    return tuple(
        jnp.concatenate([full[part * width : (part + 1) * width, s : s + width] for s in starts], axis=0)
        for part in range(2)
    )


def columns(piece_ref, first):
    half = LANES // 2
    left = jnp.where(first, piece_ref[0, :, :LANES], pltpu.roll(piece_ref[1, :, :LANES], half, 1))
    right = jnp.where(first, pltpu.roll(piece_ref[0, :, LANES:], half, 1), piece_ref[1, :, LANES:])
    return left, right


def pick(axis, even, odd):
    return jnp.where(lax.rem(lax.axis_index(BOTH[axis]), 2) == 0, even, odd)


def beside(axis, a, b):
    place = lax.axis_index(BOTH[axis])
    before = jnp.where(place == 0, 0.0, pick(axis, b, a))
    after = jnp.where(place == lax.axis_size(BOTH[axis]) - 1, 0.0, pick(axis, a, b))
    return before, after


def pack_kernel(obj_ref, colb_ref, cola_ref, held, sem, *, piece):
    first = lax.broadcasted_iota(jnp.int32, (held.shape[1], LANES), 1) < LANES // 2
    copy = pltpu.make_async_copy(obj_ref.at[piece], held, sem)
    copy.start()
    copy.wait()
    left, right = columns(held, first)
    cola_ref[...] = pick(1, right, left)
    colb_ref[...] = pick(1, left, right)


def rows_kernel(obj_ref, colb_ref, cola_ref, rowa_ref, rowb_ref, *, piece):
    half = LANES // 2
    low, high = slice(0, half), slice(obj_ref.shape[2] - half, obj_ref.shape[2])
    for part in range(2):
        for block in range(2):
            cols = slice(block * LANES, (block + 1) * LANES)
            top, bottom = obj_ref[piece, part, low, cols], obj_ref[piece, part, high, cols]
            rowa_ref[2 * part + block] = pick(0, bottom, top)
            rowb_ref[2 * part + block] = pick(0, top, bottom)
    tops = beside(1, cola_ref[low], colb_ref[low])
    bottoms = beside(1, cola_ref[high], colb_ref[high])
    for place, top, bottom in zip((4, 5), tops, bottoms):
        rowa_ref[place] = pick(0, bottom, top)
        rowb_ref[place] = pick(0, top, bottom)


def grow(ext, piece_ref, colb_ref, cola_ref, rowa_ref, rowb_ref):
    half = LANES // 2
    tile = piece_ref.shape[1]
    sides = beside(1, cola_ref[...], colb_ref[...])
    for part in range(2):
        for block in range(4):
            place = 2 * part + block - 1 if block in (1, 2) else 4 + block // 3
            top, bottom = beside(0, rowa_ref[place], rowb_ref[place])
            if block in (1, 2):
                middle = piece_ref[part, :, (block - 1) * LANES : block * LANES]
            else:
                middle = sides[block // 3]
            for strip, start in ((top, 0), (middle, half), (bottom, half + tile)):
                if (block == 0 and part == 0) or (block == 3 and part == 1):
                    strip = pltpu.roll(strip, half, 1)
                ext[part, block, start : start + strip.shape[0]] = strip


def place_window(row_ref, col_ref, slot):
    col = col_ref[0, slot] + LANES // 2
    return row_ref[0, slot], col // LANES, lax.rem(col, LANES)


def window(ext, row_ref, col_ref, slot, width):
    row, block, shift = place_window(row_ref, col_ref, slot)
    back = lax.rem(LANES - shift, LANES)
    keep = lax.broadcasted_iota(jnp.int32, (width, LANES), 1) < LANES - shift
    parts = []
    for part in range(2):
        near = pltpu.roll(ext[part, block, pl.ds(row, width), :], back, 1)
        far = pltpu.roll(ext[part, block + 1, pl.ds(row, width), :], back, 1)
        parts.append(jnp.where(keep, near, far))
    return parts


def windows(ext, row_ref, col_ref, slots, width):
    got = [window(ext, row_ref, col_ref, slot, width) for slot in slots]
    return tuple(jnp.concatenate([g[part] for g in got], axis=0) for part in range(2))


def stacked(ref, slots, part):
    return jnp.concatenate([ref[slot, part] for slot in slots], axis=0)


def store(ref, slots, values):
    width = ref.shape[2]
    for place, slot in enumerate(slots):
        for part in range(2):
            ref[slot, part] = values[part][place * width : (place + 1) * width]


def first_kernel(
    row_ref, col_ref, obj_ref, colb_ref, cola_ref, rowa_ref, rowb_ref, probe_ref, tabs_ref,
    win_ref, mid_ref, ext, *, group,
):
    width = probe_ref.shape[1]
    grow(ext, obj_ref.at[0], colb_ref, cola_ref, rowa_ref, rowb_ref)

    def some(index, _):
        slots = [group * index + place for place in range(group)]
        first_re, first_im = windows(ext, row_ref, col_ref, slots, width)
        probe_re, probe_im = (jnp.concatenate([probe_ref[p]] * group, axis=0) for p in range(2))
        wave_re = probe_re * first_re - probe_im * first_im
        wave_im = probe_re * first_im + probe_im * first_re
        store(win_ref, slots, (first_re, first_im))
        store(mid_ref, slots, two_sided(tabs_ref, 0, 1, wave_re, wave_im))
        return 0

    lax.fori_loop(0, row_ref.shape[1] // group, some, 0, unroll=True)


def second_kernel(
    row_ref, col_ref, live_ref, obj_ref, colb_ref, cola_ref, rowa_ref, rowb_ref,
    win_ref, mid_ref, measured_ref, tabs_ref,
    grad_ref, down_ref, keep_ref, send_ref,
    ext, sum_ref, *, group,
):
    width = win_ref.shape[2]
    grow(ext, obj_ref.at[1], colb_ref, cola_ref, rowa_ref, rowb_ref)
    sum_ref[...] = jnp.zeros_like(sum_ref)

    def some(index, _):
        slots = [group * index + place for place in range(group)]
        second_re, second_im = windows(ext, row_ref, col_ref, slots, width)
        mid_re, mid_im = (stacked(mid_ref, slots, part) for part in range(2))
        exit_re = mid_re * second_re - mid_im * second_im
        exit_im = mid_re * second_im + mid_im * second_re
        far_re, far_im = two_sided(tabs_ref, 2, 3, exit_re, exit_im)
        weights = []
        for place, slot in enumerate(slots):
            rows = slice(place * width, (place + 1) * width)
            active = jnp.where(slot < live_ref[0, 0], 2.0, 0.0)
            power = far_re[rows] * far_re[rows] + far_im[rows] * far_im[rows]
            weights.append((power - measured_ref[slot]) * active)
        weight = jnp.concatenate(weights, axis=0)
        chi_re, chi_im = two_sided(tabs_ref, 3, 2, weight * far_re, weight * far_im)
        grad_re = mid_re * chi_re + mid_im * chi_im
        grad_im = mid_re * chi_im - mid_im * chi_re
        store(grad_ref, slots, (grad_re, grad_im))
        back_re = second_re * chi_re + second_im * chi_im
        back_im = second_re * chi_im - second_im * chi_re
        down_re, down_im = two_sided(tabs_ref, 1, 0, back_re, back_im)
        store(down_ref, slots, (down_re, down_im))
        first_re, first_im = (stacked(win_ref, slots, part) for part in range(2))
        sum_re = first_re * down_re + first_im * down_im
        sum_im = first_re * down_im - first_im * down_re
        for part, value in enumerate((sum_re, sum_im)):
            total = value[:width]
            for start in range(width, group * width, width):
                total += value[start : start + width]
            sum_ref[part] += total
        return 0

    lax.fori_loop(0, row_ref.shape[1] // group, some, 0, unroll=True)
    keep_ref[...] = pick(1, sum_ref[0], sum_ref[1])
    send_ref[...] = pick(1, sum_ref[1], sum_ref[0])


def place_kernel(
    row_ref, col_ref, obj_ref, probe_ref, down_ref, second_ref,
    new_ref, rowa_ref, rowb_ref, left_ref, right_ref,
    grad,
):
    width = probe_ref.shape[1]
    tile = obj_ref.shape[2]
    half = width // 2
    grad[...] = jnp.zeros_like(grad)
    lane = lax.broadcasted_iota(jnp.int32, (width, LANES), 1)

    def deposit(slot, _):
        row, block, shift = place_window(row_ref, col_ref, slot)
        keep = lane >= shift
        probe_re, probe_im = probe_ref[0], probe_ref[1]
        down_re, down_im = down_ref[slot, 0], down_ref[slot, 1]
        values = (
            (probe_re * down_re + probe_im * down_im, probe_re * down_im - probe_im * down_re),
            (second_ref[slot, 0], second_ref[slot, 1]),
        )
        for piece in range(2):
            for part in range(2):
                value = pltpu.roll(values[piece][part], shift, 1)
                grad[piece, part, block, pl.ds(row, width), :] += jnp.where(keep, value, 0.0)
                grad[piece, part, block + 1, pl.ds(row, width), :] += jnp.where(keep, 0.0, value)
        return 0

    lax.fori_loop(0, row_ref.shape[1], deposit, 0)
    first = lax.broadcasted_iota(jnp.int32, (tile + width, LANES), 1) < half
    for piece in range(2):
        for part in range(2):
            for block in range(2):
                cols = slice(block * LANES, (block + 1) * LANES)
                top = grad[piece, part, 1 + block, :half]
                bottom = grad[piece, part, 1 + block, half + tile :]
                rowa_ref[piece, 2 * part + block] = pick(0, bottom, top)
                rowb_ref[piece, 2 * part + block] = pick(0, top, bottom)
                new_ref[piece, part, :, cols] = (
                    obj_ref[piece, part, :, cols]
                    - STEP_OBJECT * grad[piece, part, 1 + block, half : half + tile]
                )
        left = jnp.where(first, pltpu.roll(grad[piece, 0, 0], half, 1), grad[piece, 1, 0])
        right = jnp.where(first, grad[piece, 0, 3], pltpu.roll(grad[piece, 1, 3], half, 1))
        for place, strip, ref in ((4, left, left_ref), (5, right, right_ref)):
            top, bottom = strip[:half], strip[half + tile :]
            rowa_ref[piece, place] = pick(0, bottom, top)
            rowb_ref[piece, place] = pick(0, top, bottom)
            ref[piece] = strip[half : half + tile]


def fold_kernel(left_ref, right_ref, rowa_ref, rowb_ref, colb_ref, cola_ref):
    half = LANES // 2
    tile = left_ref.shape[1]
    for piece in range(2):
        sides = []
        for ref, place in ((left_ref, 4), (right_ref, 5)):
            top, bottom = beside(0, rowa_ref[piece, place], rowb_ref[piece, place])
            sides.append(
                (
                    ref[piece, :half] + top,
                    ref[piece, half : tile - half],
                    ref[piece, tile - half :] + bottom,
                )
            )
        for left, right, rows in zip(*sides, (slice(0, half), slice(half, tile - half), slice(tile - half, tile))):
            cola_ref[piece, rows] = pick(1, right, left)
            colb_ref[piece, rows] = pick(1, left, right)


def finish_kernel(
    part_ref, rowa_ref, rowb_ref, colb_ref, cola_ref, new_ref,
):
    tile = part_ref.shape[2]
    half = LANES // 2
    first = lax.broadcasted_iota(jnp.int32, (half, LANES), 1) < half
    for piece in range(2):
        for start in range(0, tile, half):
            rows = slice(start, start + half)
            sides = beside(1, cola_ref[piece, rows], colb_ref[piece, rows])
            for part in range(2):
                for block in range(2):
                    cols = slice(block * LANES, (block + 1) * LANES)
                    total = sides[block]
                    if block != part:
                        total = pltpu.roll(total, half, 1)
                    total = jnp.where(first == (block == 0), total, 0.0)
                    place = 2 * part + block
                    ends = beside(0, rowa_ref[piece, place], rowb_ref[piece, place])
                    if start == 0:
                        total += ends[0]
                    if start == tile - half:
                        total += ends[1]
                    new_ref[piece, part, rows, cols] = (
                        part_ref[piece, part, rows, cols] - STEP_OBJECT * total
                    )


def probe_kernel(probe_ref, mine_ref, other_ref, newp_ref, *, scale):
    newp_ref[0] = probe_ref[0] - scale * pick(1, mine_ref[...], other_ref[...])
    newp_ref[1] = probe_ref[1] - scale * pick(1, other_ref[...], mine_ref[...])


def vmem(count):
    return [pl.BlockSpec(memory_space=pltpu.VMEM)] * count


def smem(count):
    return [pl.BlockSpec(memory_space=pltpu.SMEM)] * count


def array(*shape):
    return jax.ShapeDtypeStruct(shape, jnp.float32)


def meet(strip, axis, odd):
    sizes = (lax.axis_size("row"), lax.axis_size("col"))
    pairs = []
    for spot in np.ndindex(*sizes):
        other = list(spot)
        place = ((spot[axis] + odd) ^ 1) - odd
        if 0 <= place < sizes[axis]:
            other[axis] = place
        else:
            other[1 - axis] ^= 1
        pairs.append((spot[0] * sizes[1] + spot[1], other[0] * sizes[1] + other[1]))
    return lax.ppermute(strip, BOTH, pairs)


def meet_rows(strips):
    return [meet(strips[0], 0, 0), meet(strips[1], 0, 1)]


def meet_cols(strips):
    return [meet(strips[0], 1, 1), meet(strips[1], 1, 0)]


def swap(value, masks):
    count = lax.axis_size("row") * lax.axis_size("col")
    return lax.ppermute(value, BOTH, [(i, i ^ masks[i % 2]) for i in range(count)])


def call(kernel, out_shape, scalars, arrays, scratch=()):
    return pl.pallas_call(
        kernel, out_shape=tuple(out_shape), in_specs=smem(len(scalars)) + vmem(len(arrays)),
        out_specs=tuple(vmem(len(out_shape))), scratch_shapes=list(scratch),
        compiler_params=pltpu.CompilerParams(vmem_limit_bytes=GRANT),
    )(*scalars, *arrays)


def on_device(object_field, probe, intensity, offset_row, offset_col, live):
    tile = object_field.shape[2]
    width = probe.shape[1]
    half = width // 2
    count = offset_row.shape[1]
    side, edge, plane = (tile, LANES), (6, half, LANES), (width, width)
    field, fields = array(2, 2, tile, tile), array(count, 2, width, width)
    tabs = jnp.asarray(make_tables(width))
    grown = pltpu.VMEM((2, 4, tile + width, LANES), jnp.float32)
    packed = [
        pl.pallas_call(
            functools.partial(pack_kernel, piece=piece), out_shape=tuple([array(*side)] * 2),
            in_specs=[pl.BlockSpec(memory_space=pltpu.HBM)], out_specs=tuple(vmem(2)),
            scratch_shapes=[pltpu.VMEM((2, tile, tile), jnp.float32), pltpu.SemaphoreType.DMA],
            compiler_params=pltpu.CompilerParams(vmem_limit_bytes=GRANT),
        )(pltpu.with_memory_space_constraint(object_field, pltpu.HBM))
        for piece in range(2)
    ]
    halos = []
    cols = [meet_cols(packed[piece]) for piece in range(2)]
    for piece in range(2):
        strips = call(
            functools.partial(rows_kernel, piece=piece), [array(*edge)] * 2,
            (), (object_field, *cols[piece]),
        )
        halos.append((*cols[piece], *meet_rows(strips)))
    win, mid = call(
        functools.partial(first_kernel, group=2), [fields] * 2, (offset_row, offset_col),
        (object_field, *halos[0], probe, tabs), (grown,),
    )
    grad, down, mine, send = call(
        functools.partial(second_kernel, group=count), [fields] * 2 + [array(*plane)] * 2, (offset_row, offset_col, live),
        (object_field, *halos[1], win, mid, intensity[0], tabs),
        (grown, pltpu.VMEM((2, *plane), jnp.float32)),
    )
    part, *strips, left, right = call(
        place_kernel, [field] + [array(2, *edge)] * 2 + [array(2, *side)] * 2,
        (offset_row, offset_col), (object_field, probe, down, grad),
        (pltpu.VMEM((2, 2, 4, tile + width, LANES), jnp.float32),),
    )
    mine = mine + swap(send, (1, 1))
    mine = mine + swap(mine, MASKS[0])
    rows = [None, None]
    mine, strips[1] = lax.optimization_barrier((mine, strips[1]))
    rows[1] = meet(strips[1], 0, 1)
    mine = mine + swap(mine, MASKS[1])
    mine, strips[0] = lax.optimization_barrier((mine, strips[0]))
    rows[0] = meet(strips[0], 0, 0)
    for mask in MASKS[2:4]:
        mine = mine + swap(mine, mask)
    mine, *rows = lax.optimization_barrier((mine, *rows))
    strips = call(fold_kernel, [array(2, *side)] * 2, (), (left, right, *rows))
    mine = mine + swap(mine, MASKS[4])
    cols = [None, None]
    mine, *strips = lax.optimization_barrier((mine, *strips))
    cols[0] = meet(strips[0], 1, 1)
    mine = mine + swap(mine, MASKS[5])
    mine, strips[1] = lax.optimization_barrier((mine, strips[1]))
    cols[1] = meet(strips[1], 1, 0)
    mine = mine + swap(mine, MASKS[6])
    mine, *cols = lax.optimization_barrier((mine, *cols))
    (new,) = call(finish_kernel, (field,), (), (part, *rows, *cols))
    other = swap(mine, (1, 1))
    count_all = count * lax.axis_size("row") * lax.axis_size("col")
    (new_probe,) = call(
        functools.partial(probe_kernel, scale=STEP_PROBE / count_all), (array(2, *plane),),
        (), (probe, mine, other),
    )
    return new, new_probe


def solution(mesh):
    placed = (
        P(None, None, "row", "col"),
        P(),
        P("row", "col", None, None),
        P("row", "col"),
        P("row", "col"),
        P("row", "col"),
    )
    return jax.shard_map(
        on_device,
        mesh=mesh,
        in_specs=placed,
        out_specs=(P(None, None, "row", "col"), P()),
        check_vma=False,
    )
```

```python
import functools
import math

import jax
import jax.numpy as jnp
import ml_dtypes
import numpy as np
from jax import lax
from jax.experimental import pallas as pl
from jax.experimental.pallas import tpu as pltpu
from jax.sharding import PartitionSpec as P

STEP_OBJECT = 0.03
STEP_PROBE = 2.0
FRESNEL_PHASE = 60.0
LANES = 128
BOTH = ("row", "col")
GRANT = 16 * 1024 * 1024
MASKS = ((16, 16), (4, 12), (12, 4), (128, 130), (130, 128), (32, 96), (96, 32))


def split_table(table):
    high = table.astype(ml_dtypes.bfloat16)
    low = (table - high.astype(np.float64)).astype(ml_dtypes.bfloat16)
    return high, low


def make_tables(width):
    index = np.arange(width)
    four = np.exp(-2j * math.pi * (np.outer(index, index) % width) / width) / math.sqrt(width)
    freq = np.where(index < width // 2, index, index - width) / width
    hop = np.conj(four) @ np.diag(np.exp(-1j * FRESNEL_PHASE * freq**2)) @ four
    forms = []
    for table in (hop, four):
        forms.append(np.block([[table.real, table.imag], [-table.imag, table.real]]))
        forms.append(np.block([[table.real, -table.imag], [table.imag, table.real]]))
    pairs = [split_table(form) for form in forms]
    return np.stack([np.stack(pair) for pair in pairs])


def split(value):
    high = value.astype(jnp.bfloat16)
    low = (value - high.astype(jnp.float32)).astype(jnp.bfloat16)
    return high, low


def mul3(left, right):
    dot = functools.partial(jnp.dot, preferred_element_type=jnp.float32)
    return dot(left[0], right[0]) + (dot(left[1], right[0]) + dot(left[0], right[1]))


def two_sided(tabs_ref, right, left, real, imag):
    width = real.shape[1]
    starts = range(0, real.shape[0], width)
    field = split(jnp.concatenate([real, imag], axis=1))
    half = mul3(field, (tabs_ref[right, 0], tabs_ref[right, 1]))
    field = jnp.concatenate(
        [
            jnp.concatenate([half[s : s + width, :width] for s in starts], axis=1),
            jnp.concatenate([half[s : s + width, width:] for s in starts], axis=1),
        ],
        axis=0,
    )
    full = mul3((tabs_ref[left, 0], tabs_ref[left, 1]), split(field))
    return tuple(
        jnp.concatenate([full[part * width : (part + 1) * width, s : s + width] for s in starts], axis=0)
        for part in range(2)
    )


def columns(piece_ref, first):
    half = LANES // 2
    left = jnp.where(first, piece_ref[0, :, :LANES], pltpu.roll(piece_ref[1, :, :LANES], half, 1))
    right = jnp.where(first, pltpu.roll(piece_ref[0, :, LANES:], half, 1), piece_ref[1, :, LANES:])
    return left, right


def pick(axis, even, odd):
    return jnp.where(lax.rem(lax.axis_index(BOTH[axis]), 2) == 0, even, odd)


def beside(axis, a, b):
    place = lax.axis_index(BOTH[axis])
    before = jnp.where(place == 0, 0.0, pick(axis, b, a))
    after = jnp.where(place == lax.axis_size(BOTH[axis]) - 1, 0.0, pick(axis, a, b))
    return before, after


def pack_kernel(obj_ref, colb_ref, cola_ref, held, sem, *, piece):
    first = lax.broadcasted_iota(jnp.int32, (held.shape[1], LANES), 1) < LANES // 2
    copy = pltpu.make_async_copy(obj_ref.at[piece], held, sem)
    copy.start()
    copy.wait()
    left, right = columns(held, first)
    cola_ref[...] = pick(1, right, left)
    colb_ref[...] = pick(1, left, right)


def rows_kernel(obj_ref, colb_ref, cola_ref, rowa_ref, rowb_ref, *, piece):
    half = LANES // 2
    low, high = slice(0, half), slice(obj_ref.shape[2] - half, obj_ref.shape[2])
    for part in range(2):
        for block in range(2):
            cols = slice(block * LANES, (block + 1) * LANES)
            top, bottom = obj_ref[piece, part, low, cols], obj_ref[piece, part, high, cols]
            rowa_ref[2 * part + block] = pick(0, bottom, top)
            rowb_ref[2 * part + block] = pick(0, top, bottom)
    tops = beside(1, cola_ref[low], colb_ref[low])
    bottoms = beside(1, cola_ref[high], colb_ref[high])
    for place, top, bottom in zip((4, 5), tops, bottoms):
        rowa_ref[place] = pick(0, bottom, top)
        rowb_ref[place] = pick(0, top, bottom)


def grow(ext, piece_ref, colb_ref, cola_ref, rowa_ref, rowb_ref):
    half = LANES // 2
    tile = piece_ref.shape[1]
    sides = beside(1, cola_ref[...], colb_ref[...])
    for part in range(2):
        for block in range(4):
            place = 2 * part + block - 1 if block in (1, 2) else 4 + block // 3
            top, bottom = beside(0, rowa_ref[place], rowb_ref[place])
            if block in (1, 2):
                middle = piece_ref[part, :, (block - 1) * LANES : block * LANES]
            else:
                middle = sides[block // 3]
            for strip, start in ((top, 0), (middle, half), (bottom, half + tile)):
                if (block == 0 and part == 0) or (block == 3 and part == 1):
                    strip = pltpu.roll(strip, half, 1)
                ext[part, block, start : start + strip.shape[0]] = strip


def place_window(row_ref, col_ref, slot):
    col = col_ref[0, slot] + LANES // 2
    return row_ref[0, slot], col // LANES, lax.rem(col, LANES)


def window(ext, row_ref, col_ref, slot, width):
    row, block, shift = place_window(row_ref, col_ref, slot)
    back = lax.rem(LANES - shift, LANES)
    keep = lax.broadcasted_iota(jnp.int32, (width, LANES), 1) < LANES - shift
    parts = []
    for part in range(2):
        near = pltpu.roll(ext[part, block, pl.ds(row, width), :], back, 1)
        far = pltpu.roll(ext[part, block + 1, pl.ds(row, width), :], back, 1)
        parts.append(jnp.where(keep, near, far))
    return parts


def windows(ext, row_ref, col_ref, slots, width):
    got = [window(ext, row_ref, col_ref, slot, width) for slot in slots]
    return tuple(jnp.concatenate([g[part] for g in got], axis=0) for part in range(2))


def stacked(ref, slots, part):
    return jnp.concatenate([ref[slot, part] for slot in slots], axis=0)


def store(ref, slots, values):
    width = ref.shape[2]
    for place, slot in enumerate(slots):
        for part in range(2):
            ref[slot, part] = values[part][place * width : (place + 1) * width]


def first_kernel(
    row_ref, col_ref, obj_ref, colb_ref, cola_ref, rowa_ref, rowb_ref, probe_ref, tabs_ref,
    win_ref, mid_ref, ext, *, group,
):
    width = probe_ref.shape[1]
    grow(ext, obj_ref.at[0], colb_ref, cola_ref, rowa_ref, rowb_ref)

    def some(index, _):
        slots = [group * index + place for place in range(group)]
        first_re, first_im = windows(ext, row_ref, col_ref, slots, width)
        probe_re, probe_im = (jnp.concatenate([probe_ref[p]] * group, axis=0) for p in range(2))
        wave_re = probe_re * first_re - probe_im * first_im
        wave_im = probe_re * first_im + probe_im * first_re
        store(win_ref, slots, (first_re, first_im))
        store(mid_ref, slots, two_sided(tabs_ref, 0, 1, wave_re, wave_im))
        return 0

    lax.fori_loop(0, row_ref.shape[1] // group, some, 0, unroll=True)


def second_kernel(
    row_ref, col_ref, live_ref, obj_ref, colb_ref, cola_ref, rowb_ref, rowa_ref,
    win_ref, mid_ref, measured_ref, tabs_ref,
    grad_ref, down_ref, keep_ref, send_ref,
    ext, sum_ref, *, group,
):
    width = win_ref.shape[2]
    grow(ext, obj_ref.at[1], colb_ref, cola_ref, rowa_ref, rowb_ref)
    sum_ref[...] = jnp.zeros_like(sum_ref)

    def some(index, _):
        slots = [group * index + place for place in range(group)]
        second_re, second_im = windows(ext, row_ref, col_ref, slots, width)
        mid_re, mid_im = (stacked(mid_ref, slots, part) for part in range(2))
        exit_re = mid_re * second_re - mid_im * second_im
        exit_im = mid_re * second_im + mid_im * second_re
        far_re, far_im = two_sided(tabs_ref, 2, 3, exit_re, exit_im)
        weights = []
        for place, slot in enumerate(slots):
            rows = slice(place * width, (place + 1) * width)
            active = jnp.where(slot < live_ref[0, 0], 2.0, 0.0)
            power = far_re[rows] * far_re[rows] + far_im[rows] * far_im[rows]
            weights.append((power - measured_ref[slot]) * active)
        weight = jnp.concatenate(weights, axis=0)
        chi_re, chi_im = two_sided(tabs_ref, 3, 2, weight * far_re, weight * far_im)
        grad_re = mid_re * chi_re + mid_im * chi_im
        grad_im = mid_re * chi_im - mid_im * chi_re
        store(grad_ref, slots, (grad_re, grad_im))
        back_re = second_re * chi_re + second_im * chi_im
        back_im = second_re * chi_im - second_im * chi_re
        down_re, down_im = two_sided(tabs_ref, 1, 0, back_re, back_im)
        store(down_ref, slots, (down_re, down_im))
        first_re, first_im = (stacked(win_ref, slots, part) for part in range(2))
        sum_re = first_re * down_re + first_im * down_im
        sum_im = first_re * down_im - first_im * down_re
        for part, value in enumerate((sum_re, sum_im)):
            total = value[:width]
            for start in range(width, group * width, width):
                total += value[start : start + width]
            sum_ref[part] += total
        return 0

    lax.fori_loop(0, row_ref.shape[1] // group, some, 0, unroll=True)
    keep_ref[...] = pick(1, sum_ref[0], sum_ref[1])
    send_ref[...] = pick(1, sum_ref[1], sum_ref[0])


def place_kernel(
    row_ref, col_ref, obj_ref, probe_ref, down_ref, second_ref,
    new_ref, rowa_ref, rowb_ref, left_ref, right_ref,
    grad,
):
    width = probe_ref.shape[1]
    tile = obj_ref.shape[2]
    half = width // 2
    grad[...] = jnp.zeros_like(grad)
    lane = lax.broadcasted_iota(jnp.int32, (width, LANES), 1)

    def deposit(slot, _):
        row, block, shift = place_window(row_ref, col_ref, slot)
        keep = lane >= shift
        probe_re, probe_im = probe_ref[0], probe_ref[1]
        down_re, down_im = down_ref[slot, 0], down_ref[slot, 1]
        values = (
            (probe_re * down_re + probe_im * down_im, probe_re * down_im - probe_im * down_re),
            (second_ref[slot, 0], second_ref[slot, 1]),
        )
        for piece in range(2):
            for part in range(2):
                value = pltpu.roll(values[piece][part], shift, 1)
                grad[piece, part, block, pl.ds(row, width), :] += jnp.where(keep, value, 0.0)
                grad[piece, part, block + 1, pl.ds(row, width), :] += jnp.where(keep, 0.0, value)
        return 0

    lax.fori_loop(0, row_ref.shape[1], deposit, 0)
    first = lax.broadcasted_iota(jnp.int32, (tile + width, LANES), 1) < half
    for piece in range(2):
        for part in range(2):
            for block in range(2):
                cols = slice(block * LANES, (block + 1) * LANES)
                top = grad[piece, part, 1 + block, :half]
                bottom = grad[piece, part, 1 + block, half + tile :]
                rowa_ref[piece, 2 * part + block] = pick(0, bottom, top)
                rowb_ref[piece, 2 * part + block] = pick(0, top, bottom)
                new_ref[piece, part, :, cols] = (
                    obj_ref[piece, part, :, cols]
                    - STEP_OBJECT * grad[piece, part, 1 + block, half : half + tile]
                )
        left = jnp.where(first, pltpu.roll(grad[piece, 0, 0], half, 1), grad[piece, 1, 0])
        right = jnp.where(first, grad[piece, 0, 3], pltpu.roll(grad[piece, 1, 3], half, 1))
        for place, strip, ref in ((4, left, left_ref), (5, right, right_ref)):
            top, bottom = strip[:half], strip[half + tile :]
            rowa_ref[piece, place] = pick(0, bottom, top)
            rowb_ref[piece, place] = pick(0, top, bottom)
            ref[piece] = strip[half : half + tile]


def fold_kernel(left_ref, right_ref, rowa_ref, rowb_ref, colb_ref, cola_ref):
    half = LANES // 2
    tile = left_ref.shape[1]
    for piece in range(2):
        sides = []
        for ref, place in ((left_ref, 4), (right_ref, 5)):
            top, bottom = beside(0, rowa_ref[piece, place], rowb_ref[piece, place])
            sides.append(
                (
                    ref[piece, :half] + top,
                    ref[piece, half : tile - half],
                    ref[piece, tile - half :] + bottom,
                )
            )
        for left, right, rows in zip(*sides, (slice(0, half), slice(half, tile - half), slice(tile - half, tile))):
            cola_ref[piece, rows] = pick(1, right, left)
            colb_ref[piece, rows] = pick(1, left, right)


def finish_kernel(
    part_ref, rowa_ref, rowb_ref, colb_ref, cola_ref, new_ref,
):
    tile = part_ref.shape[2]
    half = LANES // 2
    first = lax.broadcasted_iota(jnp.int32, (half, LANES), 1) < half
    for piece in range(2):
        for start in range(0, tile, half):
            rows = slice(start, start + half)
            sides = beside(1, cola_ref[piece, rows], colb_ref[piece, rows])
            for part in range(2):
                for block in range(2):
                    cols = slice(block * LANES, (block + 1) * LANES)
                    total = sides[block]
                    if block != part:
                        total = pltpu.roll(total, half, 1)
                    total = jnp.where(first == (block == 0), total, 0.0)
                    place = 2 * part + block
                    ends = beside(0, rowa_ref[piece, place], rowb_ref[piece, place])
                    if start == 0:
                        total += ends[0]
                    if start == tile - half:
                        total += ends[1]
                    new_ref[piece, part, rows, cols] = (
                        part_ref[piece, part, rows, cols] - STEP_OBJECT * total
                    )


def probe_kernel(probe_ref, mine_ref, other_ref, newp_ref, *, scale):
    newp_ref[0] = probe_ref[0] - scale * pick(1, mine_ref[...], other_ref[...])
    newp_ref[1] = probe_ref[1] - scale * pick(1, other_ref[...], mine_ref[...])


def vmem(count):
    return [pl.BlockSpec(memory_space=pltpu.VMEM)] * count


def smem(count):
    return [pl.BlockSpec(memory_space=pltpu.SMEM)] * count


def array(*shape):
    return jax.ShapeDtypeStruct(shape, jnp.float32)


def meet(strip, axis, odd):
    sizes = (lax.axis_size("row"), lax.axis_size("col"))
    pairs = []
    for spot in np.ndindex(*sizes):
        other = list(spot)
        place = ((spot[axis] + odd) ^ 1) - odd
        if 0 <= place < sizes[axis]:
            other[axis] = place
        else:
            other[1 - axis] ^= 1
        pairs.append((spot[0] * sizes[1] + spot[1], other[0] * sizes[1] + other[1]))
    return lax.ppermute(strip, BOTH, pairs)


def meet_rows(strips):
    return [meet(strips[0], 0, 0), meet(strips[1], 0, 1)]


def meet_cols(strips):
    return [meet(strips[0], 1, 1), meet(strips[1], 1, 0)]


def swap(value, masks):
    count = lax.axis_size("row") * lax.axis_size("col")
    return lax.ppermute(value, BOTH, [(i, i ^ masks[i % 2]) for i in range(count)])


def call(kernel, out_shape, scalars, arrays, scratch=()):
    return pl.pallas_call(
        kernel, out_shape=tuple(out_shape), in_specs=smem(len(scalars)) + vmem(len(arrays)),
        out_specs=tuple(vmem(len(out_shape))), scratch_shapes=list(scratch),
        compiler_params=pltpu.CompilerParams(vmem_limit_bytes=GRANT),
    )(*scalars, *arrays)


def on_device(object_field, probe, intensity, offset_row, offset_col, live):
    tile = object_field.shape[2]
    width = probe.shape[1]
    half = width // 2
    count = offset_row.shape[1]
    side, edge, plane = (tile, LANES), (6, half, LANES), (width, width)
    field, fields = array(2, 2, tile, tile), array(count, 2, width, width)
    tabs = jnp.asarray(make_tables(width))
    grown = pltpu.VMEM((2, 4, tile + width, LANES), jnp.float32)
    packed = [
        pl.pallas_call(
            functools.partial(pack_kernel, piece=piece), out_shape=tuple([array(*side)] * 2),
            in_specs=[pl.BlockSpec(memory_space=pltpu.HBM)], out_specs=tuple(vmem(2)),
            scratch_shapes=[pltpu.VMEM((2, tile, tile), jnp.float32), pltpu.SemaphoreType.DMA],
            compiler_params=pltpu.CompilerParams(vmem_limit_bytes=GRANT),
        )(pltpu.with_memory_space_constraint(object_field, pltpu.HBM))
        for piece in range(2)
    ]
    halos = []
    cols = [meet_cols(packed[piece]) for piece in range(2)]
    for piece in range(2):
        strips = call(
            functools.partial(rows_kernel, piece=piece), [array(*edge)] * 2,
            (), (object_field, *cols[piece]),
        )
        halos.append((*cols[piece], *meet_rows(strips)))
    *sides, even, odd = halos[1]
    win, mid = call(
        functools.partial(first_kernel, group=2), [fields] * 2, (offset_row, offset_col),
        (object_field, *halos[0], probe, tabs), (grown,),
    )
    grad, down, mine, send = call(
        functools.partial(second_kernel, group=count), [fields] * 2 + [array(*plane)] * 2, (offset_row, offset_col, live),
        (object_field, *sides, odd, even, win, mid, intensity[0], tabs),
        (grown, pltpu.VMEM((2, *plane), jnp.float32)),
    )
    part, *strips, left, right = call(
        place_kernel, [field] + [array(2, *edge)] * 2 + [array(2, *side)] * 2,
        (offset_row, offset_col), (object_field, probe, down, grad),
        (pltpu.VMEM((2, 2, 4, tile + width, LANES), jnp.float32),),
    )
    mine = mine + swap(send, (1, 1))
    mine = mine + swap(mine, MASKS[0])
    rows = [None, None]
    mine, strips[1] = lax.optimization_barrier((mine, strips[1]))
    rows[1] = meet(strips[1], 0, 1)
    mine = mine + swap(mine, MASKS[1])
    mine, strips[0] = lax.optimization_barrier((mine, strips[0]))
    rows[0] = meet(strips[0], 0, 0)
    for mask in MASKS[2:4]:
        mine = mine + swap(mine, mask)
    mine, *rows = lax.optimization_barrier((mine, *rows))
    strips = call(fold_kernel, [array(2, *side)] * 2, (), (left, right, *rows))
    mine = mine + swap(mine, MASKS[4])
    cols = [None, None]
    mine, *strips = lax.optimization_barrier((mine, *strips))
    cols[0] = meet(strips[0], 1, 1)
    mine = mine + swap(mine, MASKS[5])
    mine, strips[1] = lax.optimization_barrier((mine, strips[1]))
    cols[1] = meet(strips[1], 1, 0)
    mine = mine + swap(mine, MASKS[6])
    mine, *cols = lax.optimization_barrier((mine, *cols))
    (new,) = call(finish_kernel, (field,), (), (part, *rows, *cols))
    other = swap(mine, (1, 1))
    count_all = count * lax.axis_size("row") * lax.axis_size("col")
    (new_probe,) = call(
        functools.partial(probe_kernel, scale=STEP_PROBE / count_all), (array(2, *plane),),
        (), (probe, mine, other),
    )
    return new, new_probe


def solution(mesh):
    placed = (
        P(None, None, "row", "col"),
        P(),
        P("row", "col", None, None),
        P("row", "col"),
        P("row", "col"),
        P("row", "col"),
    )
    return jax.shard_map(
        on_device,
        mesh=mesh,
        in_specs=placed,
        out_specs=(P(None, None, "row", "col"), P()),
        check_vma=False,
    )
```

```python
import functools
import math

import jax
import jax.numpy as jnp
import ml_dtypes
import numpy as np
from jax import lax
from jax.experimental import pallas as pl
from jax.experimental.pallas import tpu as pltpu
from jax.sharding import PartitionSpec as P

STEP_OBJECT = 0.03
STEP_PROBE = 2.0
FRESNEL_PHASE = 60.0
LANES = 128
BOTH = ("row", "col")
GRANT = 16 * 1024 * 1024
MASKS = ((16, 16), (4, 12), (12, 4), (32, 96), (96, 32))
Y_MASKS = ((128, 130), (130, 128), (2, 2))


def split_table(table):
    high = table.astype(ml_dtypes.bfloat16)
    low = (table - high.astype(np.float64)).astype(ml_dtypes.bfloat16)
    return high, low


def make_tables(width):
    index = np.arange(width)
    four = np.exp(-2j * math.pi * (np.outer(index, index) % width) / width) / math.sqrt(width)
    freq = np.where(index < width // 2, index, index - width) / width
    hop = np.conj(four) @ np.diag(np.exp(-1j * FRESNEL_PHASE * freq**2)) @ four
    forms = []
    for table in (hop, four):
        forms.append(np.block([[table.real, table.imag], [-table.imag, table.real]]))
        forms.append(np.block([[table.real, -table.imag], [table.imag, table.real]]))
    pairs = [split_table(form) for form in forms]
    return np.stack([np.stack(pair) for pair in pairs])


def split(value):
    high = value.astype(jnp.bfloat16)
    low = (value - high.astype(jnp.float32)).astype(jnp.bfloat16)
    return high, low


def mul3(left, right):
    dot = functools.partial(jnp.dot, preferred_element_type=jnp.float32)
    return dot(left[0], right[0]) + (dot(left[1], right[0]) + dot(left[0], right[1]))


def two_sided(tabs_ref, right, left, real, imag):
    width = real.shape[1]
    starts = range(0, real.shape[0], width)
    field = split(jnp.concatenate([real, imag], axis=1))
    half = mul3(field, (tabs_ref[right, 0], tabs_ref[right, 1]))
    field = jnp.concatenate(
        [
            jnp.concatenate([half[s : s + width, :width] for s in starts], axis=1),
            jnp.concatenate([half[s : s + width, width:] for s in starts], axis=1),
        ],
        axis=0,
    )
    full = mul3((tabs_ref[left, 0], tabs_ref[left, 1]), split(field))
    return tuple(
        jnp.concatenate([full[part * width : (part + 1) * width, s : s + width] for s in starts], axis=0)
        for part in range(2)
    )


def columns(piece_ref, first):
    half = LANES // 2
    left = jnp.where(first, piece_ref[0, :, :LANES], pltpu.roll(piece_ref[1, :, :LANES], half, 1))
    right = jnp.where(first, pltpu.roll(piece_ref[0, :, LANES:], half, 1), piece_ref[1, :, LANES:])
    return left, right


def pick(axis, even, odd):
    return jnp.where(lax.rem(lax.axis_index(BOTH[axis]), 2) == 0, even, odd)


def beside(axis, a, b):
    place = lax.axis_index(BOTH[axis])
    before = jnp.where(place == 0, 0.0, pick(axis, b, a))
    after = jnp.where(place == lax.axis_size(BOTH[axis]) - 1, 0.0, pick(axis, a, b))
    return before, after


def pack_kernel(obj_ref, colb_ref, cola_ref, held, sem, *, piece):
    first = lax.broadcasted_iota(jnp.int32, (held.shape[1], LANES), 1) < LANES // 2
    copy = pltpu.make_async_copy(obj_ref.at[piece], held, sem)
    copy.start()
    copy.wait()
    left, right = columns(held, first)
    cola_ref[...] = pick(1, right, left)
    colb_ref[...] = pick(1, left, right)


def rows_kernel(obj_ref, colb_ref, cola_ref, rowa_ref, rowb_ref, *, piece):
    half = LANES // 2
    low, high = slice(0, half), slice(obj_ref.shape[2] - half, obj_ref.shape[2])
    for part in range(2):
        for block in range(2):
            cols = slice(block * LANES, (block + 1) * LANES)
            top, bottom = obj_ref[piece, part, low, cols], obj_ref[piece, part, high, cols]
            rowa_ref[2 * part + block] = pick(0, bottom, top)
            rowb_ref[2 * part + block] = pick(0, top, bottom)
    tops = beside(1, cola_ref[low], colb_ref[low])
    bottoms = beside(1, cola_ref[high], colb_ref[high])
    for place, top, bottom in zip((4, 5), tops, bottoms):
        rowa_ref[place] = pick(0, bottom, top)
        rowb_ref[place] = pick(0, top, bottom)


def grow(ext, piece_ref, colb_ref, cola_ref, rowa_ref, rowb_ref):
    half = LANES // 2
    tile = piece_ref.shape[1]
    sides = beside(1, cola_ref[...], colb_ref[...])
    for part in range(2):
        for block in range(4):
            place = 2 * part + block - 1 if block in (1, 2) else 4 + block // 3
            top, bottom = beside(0, rowa_ref[place], rowb_ref[place])
            if block in (1, 2):
                middle = piece_ref[part, :, (block - 1) * LANES : block * LANES]
            else:
                middle = sides[block // 3]
            for strip, start in ((top, 0), (middle, half), (bottom, half + tile)):
                if (block == 0 and part == 0) or (block == 3 and part == 1):
                    strip = pltpu.roll(strip, half, 1)
                ext[part, block, start : start + strip.shape[0]] = strip


def place_window(row_ref, col_ref, slot):
    col = col_ref[0, slot] + LANES // 2
    return row_ref[0, slot], col // LANES, lax.rem(col, LANES)


def window(ext, row_ref, col_ref, slot, width):
    row, block, shift = place_window(row_ref, col_ref, slot)
    back = lax.rem(LANES - shift, LANES)
    keep = lax.broadcasted_iota(jnp.int32, (width, LANES), 1) < LANES - shift
    parts = []
    for part in range(2):
        near = pltpu.roll(ext[part, block, pl.ds(row, width), :], back, 1)
        far = pltpu.roll(ext[part, block + 1, pl.ds(row, width), :], back, 1)
        parts.append(jnp.where(keep, near, far))
    return parts


def windows(ext, row_ref, col_ref, slots, width):
    got = [window(ext, row_ref, col_ref, slot, width) for slot in slots]
    return tuple(jnp.concatenate([g[part] for g in got], axis=0) for part in range(2))


def stacked(ref, slots, part):
    return jnp.concatenate([ref[slot, part] for slot in slots], axis=0)


def store(ref, slots, values):
    width = ref.shape[2]
    for place, slot in enumerate(slots):
        for part in range(2):
            ref[slot, part] = values[part][place * width : (place + 1) * width]


def first_kernel(
    row_ref, col_ref, obj_ref, colb_ref, cola_ref, rowa_ref, rowb_ref, probe_ref, tabs_ref,
    win_ref, mid_ref, ext, *, group,
):
    width = probe_ref.shape[1]
    grow(ext, obj_ref.at[0], colb_ref, cola_ref, rowa_ref, rowb_ref)

    def some(index, _):
        slots = [group * index + place for place in range(group)]
        first_re, first_im = windows(ext, row_ref, col_ref, slots, width)
        probe_re, probe_im = (jnp.concatenate([probe_ref[p]] * group, axis=0) for p in range(2))
        wave_re = probe_re * first_re - probe_im * first_im
        wave_im = probe_re * first_im + probe_im * first_re
        store(win_ref, slots, (first_re, first_im))
        store(mid_ref, slots, two_sided(tabs_ref, 0, 1, wave_re, wave_im))
        return 0

    lax.fori_loop(0, row_ref.shape[1] // group, some, 0, unroll=True)


def second_kernel(
    row_ref, col_ref, live_ref, obj_ref, colb_ref, cola_ref, rowb_ref, rowa_ref,
    win_ref, mid_ref, measured_ref, tabs_ref,
    grad_ref, down_ref, keep_ref, send_ref,
    ext, sum_ref, *, group,
):
    width = win_ref.shape[2]
    grow(ext, obj_ref.at[1], colb_ref, cola_ref, rowa_ref, rowb_ref)
    sum_ref[...] = jnp.zeros_like(sum_ref)

    def some(index, _):
        slots = [group * index + place for place in range(group)]
        second_re, second_im = windows(ext, row_ref, col_ref, slots, width)
        mid_re, mid_im = (stacked(mid_ref, slots, part) for part in range(2))
        exit_re = mid_re * second_re - mid_im * second_im
        exit_im = mid_re * second_im + mid_im * second_re
        far_re, far_im = two_sided(tabs_ref, 2, 3, exit_re, exit_im)
        weights = []
        for place, slot in enumerate(slots):
            rows = slice(place * width, (place + 1) * width)
            active = jnp.where(slot < live_ref[0, 0], 2.0, 0.0)
            power = far_re[rows] * far_re[rows] + far_im[rows] * far_im[rows]
            weights.append((power - measured_ref[slot]) * active)
        weight = jnp.concatenate(weights, axis=0)
        chi_re, chi_im = two_sided(tabs_ref, 3, 2, weight * far_re, weight * far_im)
        grad_re = mid_re * chi_re + mid_im * chi_im
        grad_im = mid_re * chi_im - mid_im * chi_re
        store(grad_ref, slots, (grad_re, grad_im))
        back_re = second_re * chi_re + second_im * chi_im
        back_im = second_re * chi_im - second_im * chi_re
        down_re, down_im = two_sided(tabs_ref, 1, 0, back_re, back_im)
        store(down_ref, slots, (down_re, down_im))
        first_re, first_im = (stacked(win_ref, slots, part) for part in range(2))
        sum_re = first_re * down_re + first_im * down_im
        sum_im = first_re * down_im - first_im * down_re
        for part, value in enumerate((sum_re, sum_im)):
            total = value[:width]
            for start in range(width, group * width, width):
                total += value[start : start + width]
            sum_ref[part] += total
        return 0

    lax.fori_loop(0, row_ref.shape[1] // group, some, 0, unroll=True)
    keep_ref[...] = pick(1, sum_ref[0], sum_ref[1])
    send_ref[...] = pick(1, sum_ref[1], sum_ref[0])


def place_kernel(
    row_ref, col_ref, obj_ref, probe_ref, down_ref, second_ref,
    new_ref, rowa_ref, rowb_ref, left_ref, right_ref,
    grad,
):
    width = probe_ref.shape[1]
    tile = obj_ref.shape[2]
    half = width // 2
    grad[...] = jnp.zeros_like(grad)
    lane = lax.broadcasted_iota(jnp.int32, (width, LANES), 1)

    def deposit(slot, _):
        row, block, shift = place_window(row_ref, col_ref, slot)
        keep = lane >= shift
        probe_re, probe_im = probe_ref[0], probe_ref[1]
        down_re, down_im = down_ref[slot, 0], down_ref[slot, 1]
        values = (
            (probe_re * down_re + probe_im * down_im, probe_re * down_im - probe_im * down_re),
            (second_ref[slot, 0], second_ref[slot, 1]),
        )
        for piece in range(2):
            for part in range(2):
                value = pltpu.roll(values[piece][part], shift, 1)
                grad[piece, part, block, pl.ds(row, width), :] += jnp.where(keep, value, 0.0)
                grad[piece, part, block + 1, pl.ds(row, width), :] += jnp.where(keep, 0.0, value)
        return 0

    lax.fori_loop(0, row_ref.shape[1], deposit, 0)
    first = lax.broadcasted_iota(jnp.int32, (tile + width, LANES), 1) < half
    for piece in range(2):
        for part in range(2):
            for block in range(2):
                cols = slice(block * LANES, (block + 1) * LANES)
                top = grad[piece, part, 1 + block, :half]
                bottom = grad[piece, part, 1 + block, half + tile :]
                rowa_ref[piece, 2 * part + block] = pick(0, bottom, top)
                rowb_ref[piece, 2 * part + block] = pick(0, top, bottom)
                new_ref[piece, part, :, cols] = (
                    obj_ref[piece, part, :, cols]
                    - STEP_OBJECT * grad[piece, part, 1 + block, half : half + tile]
                )
        left = jnp.where(first, pltpu.roll(grad[piece, 0, 0], half, 1), grad[piece, 1, 0])
        right = jnp.where(first, grad[piece, 0, 3], pltpu.roll(grad[piece, 1, 3], half, 1))
        for place, strip, ref in ((4, left, left_ref), (5, right, right_ref)):
            top, bottom = strip[:half], strip[half + tile :]
            rowa_ref[piece, place] = pick(0, bottom, top)
            rowb_ref[piece, place] = pick(0, top, bottom)
            ref[piece] = strip[half : half + tile]


def fold_kernel(left_ref, right_ref, rowa_ref, rowb_ref, colb_ref, cola_ref):
    half = LANES // 2
    tile = left_ref.shape[1]
    for piece in range(2):
        sides = []
        for ref, place in ((left_ref, 4), (right_ref, 5)):
            top, bottom = beside(0, rowa_ref[piece, place], rowb_ref[piece, place])
            sides.append(
                (
                    ref[piece, :half] + top,
                    ref[piece, half : tile - half],
                    ref[piece, tile - half :] + bottom,
                )
            )
        for left, right, rows in zip(*sides, (slice(0, half), slice(half, tile - half), slice(tile - half, tile))):
            cola_ref[piece, rows] = pick(1, right, left)
            colb_ref[piece, rows] = pick(1, left, right)


def finish_kernel(
    part_ref, rowa_ref, rowb_ref, colb_ref, cola_ref, new_ref,
):
    tile = part_ref.shape[2]
    half = LANES // 2
    first = lax.broadcasted_iota(jnp.int32, (half, LANES), 1) < half
    for piece in range(2):
        for start in range(0, tile, half):
            rows = slice(start, start + half)
            sides = beside(1, cola_ref[piece, rows], colb_ref[piece, rows])
            for part in range(2):
                for block in range(2):
                    cols = slice(block * LANES, (block + 1) * LANES)
                    total = sides[block]
                    if block != part:
                        total = pltpu.roll(total, half, 1)
                    total = jnp.where(first == (block == 0), total, 0.0)
                    place = 2 * part + block
                    ends = beside(0, rowa_ref[piece, place], rowb_ref[piece, place])
                    if start == 0:
                        total += ends[0]
                    if start == tile - half:
                        total += ends[1]
                    new_ref[piece, part, rows, cols] = (
                        part_ref[piece, part, rows, cols] - STEP_OBJECT * total
                    )


def probe_kernel(probe_ref, mine_ref, other_ref, newp_ref, *, scale):
    newp_ref[0] = probe_ref[0] - scale * pick(1, mine_ref[...], other_ref[...])
    newp_ref[1] = probe_ref[1] - scale * pick(1, other_ref[...], mine_ref[...])


def vmem(count):
    return [pl.BlockSpec(memory_space=pltpu.VMEM)] * count


def smem(count):
    return [pl.BlockSpec(memory_space=pltpu.SMEM)] * count


def array(*shape):
    return jax.ShapeDtypeStruct(shape, jnp.float32)


def meet(strip, axis, odd):
    sizes = (lax.axis_size("row"), lax.axis_size("col"))
    pairs = []
    for spot in np.ndindex(*sizes):
        other = list(spot)
        place = ((spot[axis] + odd) ^ 1) - odd
        if 0 <= place < sizes[axis]:
            other[axis] = place
        else:
            other[1 - axis] ^= 1
        pairs.append((spot[0] * sizes[1] + spot[1], other[0] * sizes[1] + other[1]))
    return lax.ppermute(strip, BOTH, pairs)


def meet_rows(strips):
    return [meet(strips[0], 0, 0), meet(strips[1], 0, 1)]


def meet_cols(strips):
    return [meet(strips[0], 1, 1), meet(strips[1], 1, 0)]


def swap(value, masks):
    count = lax.axis_size("row") * lax.axis_size("col")
    return lax.ppermute(value, BOTH, [(i, i ^ masks[i % 2]) for i in range(count)])


def call(kernel, out_shape, scalars, arrays, scratch=()):
    return pl.pallas_call(
        kernel, out_shape=tuple(out_shape), in_specs=smem(len(scalars)) + vmem(len(arrays)),
        out_specs=tuple(vmem(len(out_shape))), scratch_shapes=list(scratch),
        compiler_params=pltpu.CompilerParams(vmem_limit_bytes=GRANT),
    )(*scalars, *arrays)


def on_device(object_field, probe, intensity, offset_row, offset_col, live):
    tile = object_field.shape[2]
    width = probe.shape[1]
    half = width // 2
    count = offset_row.shape[1]
    side, edge, plane = (tile, LANES), (6, half, LANES), (width, width)
    field, fields = array(2, 2, tile, tile), array(count, 2, width, width)
    tabs = jnp.asarray(make_tables(width))
    grown = pltpu.VMEM((2, 4, tile + width, LANES), jnp.float32)
    packed = [
        pl.pallas_call(
            functools.partial(pack_kernel, piece=piece), out_shape=tuple([array(*side)] * 2),
            in_specs=[pl.BlockSpec(memory_space=pltpu.HBM)], out_specs=tuple(vmem(2)),
            scratch_shapes=[pltpu.VMEM((2, tile, tile), jnp.float32), pltpu.SemaphoreType.DMA],
            compiler_params=pltpu.CompilerParams(vmem_limit_bytes=GRANT),
        )(pltpu.with_memory_space_constraint(object_field, pltpu.HBM))
        for piece in range(2)
    ]
    halos = []
    cols = [meet_cols(packed[piece]) for piece in range(2)]
    for piece in range(2):
        strips = call(
            functools.partial(rows_kernel, piece=piece), [array(*edge)] * 2,
            (), (object_field, *cols[piece]),
        )
        halos.append((*cols[piece], *meet_rows(strips)))
    *sides, even, odd = halos[1]
    win, mid = call(
        functools.partial(first_kernel, group=2), [fields] * 2, (offset_row, offset_col),
        (object_field, *halos[0], probe, tabs), (grown,),
    )
    grad, down, mine, send = call(
        functools.partial(second_kernel, group=count), [fields] * 2 + [array(*plane)] * 2, (offset_row, offset_col, live),
        (object_field, *sides, odd, even, win, mid, intensity[0], tabs),
        (grown, pltpu.VMEM((2, *plane), jnp.float32)),
    )
    part, *strips, left, right = call(
        place_kernel, [field] + [array(2, *edge)] * 2 + [array(2, *side)] * 2,
        (offset_row, offset_col), (object_field, probe, down, grad),
        (pltpu.VMEM((2, 2, 4, tile + width, LANES), jnp.float32),),
    )
    mine = mine + swap(send, (1, 1))
    mine = mine + swap(mine, MASKS[0])
    rows = [None, None]
    mine, strips[1] = lax.optimization_barrier((mine, strips[1]))
    rows[1] = meet(strips[1], 0, 1)
    mine = mine + swap(mine, MASKS[1])
    mine, strips[0] = lax.optimization_barrier((mine, strips[0]))
    rows[0] = meet(strips[0], 0, 0)
    mine = mine + swap(mine, MASKS[2])
    along_y = [swap(mine, mask) for mask in Y_MASKS]
    mine = (mine + along_y[0]) + (along_y[1] + along_y[2])
    mine, *rows = lax.optimization_barrier((mine, *rows))
    strips = call(fold_kernel, [array(2, *side)] * 2, (), (left, right, *rows))
    cols = [None, None]
    mine, *strips = lax.optimization_barrier((mine, *strips))
    cols[0] = meet(strips[0], 1, 1)
    mine = mine + swap(mine, MASKS[3])
    mine, strips[1] = lax.optimization_barrier((mine, strips[1]))
    cols[1] = meet(strips[1], 1, 0)
    mine = mine + swap(mine, MASKS[4])
    mine, *cols = lax.optimization_barrier((mine, *cols))
    (new,) = call(finish_kernel, (field,), (), (part, *rows, *cols))
    other = swap(mine, (1, 1))
    count_all = count * lax.axis_size("row") * lax.axis_size("col")
    (new_probe,) = call(
        functools.partial(probe_kernel, scale=STEP_PROBE / count_all), (array(2, *plane),),
        (), (probe, mine, other),
    )
    return new, new_probe


def solution(mesh):
    placed = (
        P(None, None, "row", "col"),
        P(),
        P("row", "col", None, None),
        P("row", "col"),
        P("row", "col"),
        P("row", "col"),
    )
    return jax.shard_map(
        on_device,
        mesh=mesh,
        in_specs=placed,
        out_specs=(P(None, None, "row", "col"), P()),
        check_vma=False,
    )
```

```python
import functools
import math

import jax
import jax.numpy as jnp
import ml_dtypes
import numpy as np
from jax import lax
from jax.experimental import pallas as pl
from jax.experimental.pallas import tpu as pltpu
from jax.sharding import PartitionSpec as P

STEP_OBJECT = 0.03
STEP_PROBE = 2.0
FRESNEL_PHASE = 60.0
LANES = 128
BOTH = ("row", "col")
GRANT = 16 * 1024 * 1024
MASKS = ((16, 32), (4, 12), (12, 4), (32, 96), (96, 16))
Y_MASKS = ((128, 130), (130, 128), (2, 2))


def split_table(table):
    high = table.astype(ml_dtypes.bfloat16)
    low = (table - high.astype(np.float64)).astype(ml_dtypes.bfloat16)
    return high, low


def make_tables(width):
    index = np.arange(width)
    four = np.exp(-2j * math.pi * (np.outer(index, index) % width) / width) / math.sqrt(width)
    freq = np.where(index < width // 2, index, index - width) / width
    hop = np.conj(four) @ np.diag(np.exp(-1j * FRESNEL_PHASE * freq**2)) @ four
    forms = []
    for table in (hop, four):
        forms.append(np.block([[table.real, table.imag], [-table.imag, table.real]]))
        forms.append(np.block([[table.real, -table.imag], [table.imag, table.real]]))
    pairs = [split_table(form) for form in forms]
    return np.stack([np.stack(pair) for pair in pairs])


def split(value):
    high = value.astype(jnp.bfloat16)
    low = (value - high.astype(jnp.float32)).astype(jnp.bfloat16)
    return high, low


def mul3(left, right):
    dot = functools.partial(jnp.dot, preferred_element_type=jnp.float32)
    return dot(left[0], right[0]) + (dot(left[1], right[0]) + dot(left[0], right[1]))


def two_sided(tabs_ref, right, left, real, imag):
    width = real.shape[1]
    starts = range(0, real.shape[0], width)
    field = split(jnp.concatenate([real, imag], axis=1))
    half = mul3(field, (tabs_ref[right, 0], tabs_ref[right, 1]))
    field = jnp.concatenate(
        [
            jnp.concatenate([half[s : s + width, :width] for s in starts], axis=1),
            jnp.concatenate([half[s : s + width, width:] for s in starts], axis=1),
        ],
        axis=0,
    )
    full = mul3((tabs_ref[left, 0], tabs_ref[left, 1]), split(field))
    return tuple(
        jnp.concatenate([full[part * width : (part + 1) * width, s : s + width] for s in starts], axis=0)
        for part in range(2)
    )


def columns(piece_ref, first):
    half = LANES // 2
    left = jnp.where(first, piece_ref[0, :, :LANES], pltpu.roll(piece_ref[1, :, :LANES], half, 1))
    right = jnp.where(first, pltpu.roll(piece_ref[0, :, LANES:], half, 1), piece_ref[1, :, LANES:])
    return left, right


def pick(axis, even, odd):
    return jnp.where(lax.rem(lax.axis_index(BOTH[axis]), 2) == 0, even, odd)


def beside(axis, a, b):
    place = lax.axis_index(BOTH[axis])
    before = jnp.where(place == 0, 0.0, pick(axis, b, a))
    after = jnp.where(place == lax.axis_size(BOTH[axis]) - 1, 0.0, pick(axis, a, b))
    return before, after


def pack_kernel(obj_ref, colb_ref, cola_ref, held, sem, *, piece):
    first = lax.broadcasted_iota(jnp.int32, (held.shape[1], LANES), 1) < LANES // 2
    copy = pltpu.make_async_copy(obj_ref.at[piece], held, sem)
    copy.start()
    copy.wait()
    left, right = columns(held, first)
    cola_ref[...] = pick(1, right, left)
    colb_ref[...] = pick(1, left, right)


def rows_kernel(obj_ref, colb_ref, cola_ref, rowa_ref, rowb_ref, *, piece):
    half = LANES // 2
    low, high = slice(0, half), slice(obj_ref.shape[2] - half, obj_ref.shape[2])
    for part in range(2):
        for block in range(2):
            cols = slice(block * LANES, (block + 1) * LANES)
            top, bottom = obj_ref[piece, part, low, cols], obj_ref[piece, part, high, cols]
            rowa_ref[2 * part + block] = pick(0, bottom, top)
            rowb_ref[2 * part + block] = pick(0, top, bottom)
    tops = beside(1, cola_ref[low], colb_ref[low])
    bottoms = beside(1, cola_ref[high], colb_ref[high])
    for place, top, bottom in zip((4, 5), tops, bottoms):
        rowa_ref[place] = pick(0, bottom, top)
        rowb_ref[place] = pick(0, top, bottom)


def grow(ext, piece_ref, colb_ref, cola_ref, rowa_ref, rowb_ref):
    half = LANES // 2
    tile = piece_ref.shape[1]
    sides = beside(1, cola_ref[...], colb_ref[...])
    for part in range(2):
        for block in range(4):
            place = 2 * part + block - 1 if block in (1, 2) else 4 + block // 3
            top, bottom = beside(0, rowa_ref[place], rowb_ref[place])
            if block in (1, 2):
                middle = piece_ref[part, :, (block - 1) * LANES : block * LANES]
            else:
                middle = sides[block // 3]
            for strip, start in ((top, 0), (middle, half), (bottom, half + tile)):
                if (block == 0 and part == 0) or (block == 3 and part == 1):
                    strip = pltpu.roll(strip, half, 1)
                ext[part, block, start : start + strip.shape[0]] = strip


def place_window(row_ref, col_ref, slot):
    col = col_ref[0, slot] + LANES // 2
    return row_ref[0, slot], col // LANES, lax.rem(col, LANES)


def window(ext, row_ref, col_ref, slot, width):
    row, block, shift = place_window(row_ref, col_ref, slot)
    back = lax.rem(LANES - shift, LANES)
    keep = lax.broadcasted_iota(jnp.int32, (width, LANES), 1) < LANES - shift
    parts = []
    for part in range(2):
        near = pltpu.roll(ext[part, block, pl.ds(row, width), :], back, 1)
        far = pltpu.roll(ext[part, block + 1, pl.ds(row, width), :], back, 1)
        parts.append(jnp.where(keep, near, far))
    return parts


def windows(ext, row_ref, col_ref, slots, width):
    got = [window(ext, row_ref, col_ref, slot, width) for slot in slots]
    return tuple(jnp.concatenate([g[part] for g in got], axis=0) for part in range(2))


def stacked(ref, slots, part):
    return jnp.concatenate([ref[slot, part] for slot in slots], axis=0)


def store(ref, slots, values):
    width = ref.shape[2]
    for place, slot in enumerate(slots):
        for part in range(2):
            ref[slot, part] = values[part][place * width : (place + 1) * width]


def first_kernel(
    row_ref, col_ref, obj_ref, colb_ref, cola_ref, rowa_ref, rowb_ref, probe_ref, tabs_ref,
    win_ref, mid_ref, ext, *, group,
):
    width = probe_ref.shape[1]
    grow(ext, obj_ref.at[0], colb_ref, cola_ref, rowa_ref, rowb_ref)

    def some(index, _):
        slots = [group * index + place for place in range(group)]
        first_re, first_im = windows(ext, row_ref, col_ref, slots, width)
        probe_re, probe_im = (jnp.concatenate([probe_ref[p]] * group, axis=0) for p in range(2))
        wave_re = probe_re * first_re - probe_im * first_im
        wave_im = probe_re * first_im + probe_im * first_re
        store(win_ref, slots, (first_re, first_im))
        store(mid_ref, slots, two_sided(tabs_ref, 0, 1, wave_re, wave_im))
        return 0

    lax.fori_loop(0, row_ref.shape[1] // group, some, 0, unroll=True)


def second_kernel(
    row_ref, col_ref, live_ref, obj_ref, colb_ref, cola_ref, rowb_ref, rowa_ref,
    win_ref, mid_ref, measured_ref, tabs_ref,
    grad_ref, down_ref, keep_ref, send_ref,
    ext, sum_ref, *, group,
):
    width = win_ref.shape[2]
    grow(ext, obj_ref.at[1], colb_ref, cola_ref, rowa_ref, rowb_ref)
    sum_ref[...] = jnp.zeros_like(sum_ref)

    def some(index, _):
        slots = [group * index + place for place in range(group)]
        second_re, second_im = windows(ext, row_ref, col_ref, slots, width)
        mid_re, mid_im = (stacked(mid_ref, slots, part) for part in range(2))
        exit_re = mid_re * second_re - mid_im * second_im
        exit_im = mid_re * second_im + mid_im * second_re
        far_re, far_im = two_sided(tabs_ref, 2, 3, exit_re, exit_im)
        weights = []
        for place, slot in enumerate(slots):
            rows = slice(place * width, (place + 1) * width)
            active = jnp.where(slot < live_ref[0, 0], 2.0, 0.0)
            power = far_re[rows] * far_re[rows] + far_im[rows] * far_im[rows]
            weights.append((power - measured_ref[slot]) * active)
        weight = jnp.concatenate(weights, axis=0)
        chi_re, chi_im = two_sided(tabs_ref, 3, 2, weight * far_re, weight * far_im)
        grad_re = mid_re * chi_re + mid_im * chi_im
        grad_im = mid_re * chi_im - mid_im * chi_re
        store(grad_ref, slots, (grad_re, grad_im))
        back_re = second_re * chi_re + second_im * chi_im
        back_im = second_re * chi_im - second_im * chi_re
        down_re, down_im = two_sided(tabs_ref, 1, 0, back_re, back_im)
        store(down_ref, slots, (down_re, down_im))
        first_re, first_im = (stacked(win_ref, slots, part) for part in range(2))
        sum_re = first_re * down_re + first_im * down_im
        sum_im = first_re * down_im - first_im * down_re
        for part, value in enumerate((sum_re, sum_im)):
            total = value[:width]
            for start in range(width, group * width, width):
                total += value[start : start + width]
            sum_ref[part] += total
        return 0

    lax.fori_loop(0, row_ref.shape[1] // group, some, 0, unroll=True)
    keep_ref[...] = pick(1, sum_ref[0], sum_ref[1])
    send_ref[...] = pick(1, sum_ref[1], sum_ref[0])


def place_kernel(
    row_ref, col_ref, obj_ref, probe_ref, down_ref, second_ref,
    new_ref, rowa_ref, rowb_ref, left_ref, right_ref,
    grad,
):
    width = probe_ref.shape[1]
    tile = obj_ref.shape[2]
    half = width // 2
    grad[...] = jnp.zeros_like(grad)
    lane = lax.broadcasted_iota(jnp.int32, (width, LANES), 1)

    def deposit(slot, _):
        row, block, shift = place_window(row_ref, col_ref, slot)
        keep = lane >= shift
        probe_re, probe_im = probe_ref[0], probe_ref[1]
        down_re, down_im = down_ref[slot, 0], down_ref[slot, 1]
        values = (
            (probe_re * down_re + probe_im * down_im, probe_re * down_im - probe_im * down_re),
            (second_ref[slot, 0], second_ref[slot, 1]),
        )
        for piece in range(2):
            for part in range(2):
                value = pltpu.roll(values[piece][part], shift, 1)
                grad[piece, part, block, pl.ds(row, width), :] += jnp.where(keep, value, 0.0)
                grad[piece, part, block + 1, pl.ds(row, width), :] += jnp.where(keep, 0.0, value)
        return 0

    lax.fori_loop(0, row_ref.shape[1], deposit, 0)
    first = lax.broadcasted_iota(jnp.int32, (tile + width, LANES), 1) < half
    for piece in range(2):
        for part in range(2):
            for block in range(2):
                cols = slice(block * LANES, (block + 1) * LANES)
                top = grad[piece, part, 1 + block, :half]
                bottom = grad[piece, part, 1 + block, half + tile :]
                rowa_ref[piece, 2 * part + block] = pick(0, bottom, top)
                rowb_ref[piece, 2 * part + block] = pick(0, top, bottom)
                new_ref[piece, part, :, cols] = (
                    obj_ref[piece, part, :, cols]
                    - STEP_OBJECT * grad[piece, part, 1 + block, half : half + tile]
                )
        left = jnp.where(first, pltpu.roll(grad[piece, 0, 0], half, 1), grad[piece, 1, 0])
        right = jnp.where(first, grad[piece, 0, 3], pltpu.roll(grad[piece, 1, 3], half, 1))
        for place, strip, ref in ((4, left, left_ref), (5, right, right_ref)):
            top, bottom = strip[:half], strip[half + tile :]
            rowa_ref[piece, place] = pick(0, bottom, top)
            rowb_ref[piece, place] = pick(0, top, bottom)
            ref[piece] = strip[half : half + tile]


def fold_kernel(left_ref, right_ref, rowa_ref, rowb_ref, colb_ref, cola_ref):
    half = LANES // 2
    tile = left_ref.shape[1]
    for piece in range(2):
        sides = []
        for ref, place in ((left_ref, 4), (right_ref, 5)):
            top, bottom = beside(0, rowa_ref[piece, place], rowb_ref[piece, place])
            sides.append(
                (
                    ref[piece, :half] + top,
                    ref[piece, half : tile - half],
                    ref[piece, tile - half :] + bottom,
                )
            )
        for left, right, rows in zip(*sides, (slice(0, half), slice(half, tile - half), slice(tile - half, tile))):
            cola_ref[piece, rows] = pick(1, right, left)
            colb_ref[piece, rows] = pick(1, left, right)


def finish_kernel(
    part_ref, rowa_ref, rowb_ref, colb_ref, cola_ref, new_ref,
):
    tile = part_ref.shape[2]
    half = LANES // 2
    first = lax.broadcasted_iota(jnp.int32, (half, LANES), 1) < half
    for piece in range(2):
        for start in range(0, tile, half):
            rows = slice(start, start + half)
            sides = beside(1, cola_ref[piece, rows], colb_ref[piece, rows])
            for part in range(2):
                for block in range(2):
                    cols = slice(block * LANES, (block + 1) * LANES)
                    total = sides[block]
                    if block != part:
                        total = pltpu.roll(total, half, 1)
                    total = jnp.where(first == (block == 0), total, 0.0)
                    place = 2 * part + block
                    ends = beside(0, rowa_ref[piece, place], rowb_ref[piece, place])
                    if start == 0:
                        total += ends[0]
                    if start == tile - half:
                        total += ends[1]
                    new_ref[piece, part, rows, cols] = (
                        part_ref[piece, part, rows, cols] - STEP_OBJECT * total
                    )


def probe_kernel(probe_ref, mine_ref, other_ref, newp_ref, *, scale):
    newp_ref[0] = probe_ref[0] - scale * pick(1, mine_ref[...], other_ref[...])
    newp_ref[1] = probe_ref[1] - scale * pick(1, other_ref[...], mine_ref[...])


def vmem(count):
    return [pl.BlockSpec(memory_space=pltpu.VMEM)] * count


def smem(count):
    return [pl.BlockSpec(memory_space=pltpu.SMEM)] * count


def array(*shape):
    return jax.ShapeDtypeStruct(shape, jnp.float32)


def meet(strip, axis, odd):
    sizes = (lax.axis_size("row"), lax.axis_size("col"))
    pairs = []
    for spot in np.ndindex(*sizes):
        other = list(spot)
        place = ((spot[axis] + odd) ^ 1) - odd
        if 0 <= place < sizes[axis]:
            other[axis] = place
        else:
            other[1 - axis] ^= 1
        pairs.append((spot[0] * sizes[1] + spot[1], other[0] * sizes[1] + other[1]))
    return lax.ppermute(strip, BOTH, pairs)


def meet_rows(strips):
    return [meet(strips[0], 0, 0), meet(strips[1], 0, 1)]


def meet_cols(strips):
    return [meet(strips[0], 1, 1), meet(strips[1], 1, 0)]


def swap(value, masks):
    count = lax.axis_size("row") * lax.axis_size("col")
    return lax.ppermute(value, BOTH, [(i, i ^ masks[i % 2]) for i in range(count)])


def call(kernel, out_shape, scalars, arrays, scratch=()):
    return pl.pallas_call(
        kernel, out_shape=tuple(out_shape), in_specs=smem(len(scalars)) + vmem(len(arrays)),
        out_specs=tuple(vmem(len(out_shape))), scratch_shapes=list(scratch),
        compiler_params=pltpu.CompilerParams(vmem_limit_bytes=GRANT),
    )(*scalars, *arrays)


def on_device(object_field, probe, intensity, offset_row, offset_col, live):
    tile = object_field.shape[2]
    width = probe.shape[1]
    half = width // 2
    count = offset_row.shape[1]
    side, edge, plane = (tile, LANES), (6, half, LANES), (width, width)
    field, fields = array(2, 2, tile, tile), array(count, 2, width, width)
    tabs = jnp.asarray(make_tables(width))
    grown = pltpu.VMEM((2, 4, tile + width, LANES), jnp.float32)
    packed = [
        pl.pallas_call(
            functools.partial(pack_kernel, piece=piece), out_shape=tuple([array(*side)] * 2),
            in_specs=[pl.BlockSpec(memory_space=pltpu.HBM)], out_specs=tuple(vmem(2)),
            scratch_shapes=[pltpu.VMEM((2, tile, tile), jnp.float32), pltpu.SemaphoreType.DMA],
            compiler_params=pltpu.CompilerParams(vmem_limit_bytes=GRANT),
        )(pltpu.with_memory_space_constraint(object_field, pltpu.HBM))
        for piece in range(2)
    ]
    halos = []
    cols = [meet_cols(packed[piece]) for piece in range(2)]
    for piece in range(2):
        strips = call(
            functools.partial(rows_kernel, piece=piece), [array(*edge)] * 2,
            (), (object_field, *cols[piece]),
        )
        halos.append((*cols[piece], *meet_rows(strips)))
    *sides, even, odd = halos[1]
    win, mid = call(
        functools.partial(first_kernel, group=2), [fields] * 2, (offset_row, offset_col),
        (object_field, *halos[0], probe, tabs), (grown,),
    )
    grad, down, mine, send = call(
        functools.partial(second_kernel, group=count), [fields] * 2 + [array(*plane)] * 2, (offset_row, offset_col, live),
        (object_field, *sides, odd, even, win, mid, intensity[0], tabs),
        (grown, pltpu.VMEM((2, *plane), jnp.float32)),
    )
    part, *strips, left, right = call(
        place_kernel, [field] + [array(2, *edge)] * 2 + [array(2, *side)] * 2,
        (offset_row, offset_col), (object_field, probe, down, grad),
        (pltpu.VMEM((2, 2, 4, tile + width, LANES), jnp.float32),),
    )
    mine = mine + swap(send, (1, 1))
    mine = mine + swap(mine, MASKS[0])
    rows = [None, None]
    mine, strips[1] = lax.optimization_barrier((mine, strips[1]))
    rows[1] = meet(strips[1], 0, 1)
    mine = mine + swap(mine, MASKS[1])
    mine, strips[0] = lax.optimization_barrier((mine, strips[0]))
    rows[0] = meet(strips[0], 0, 0)
    mine = mine + swap(mine, MASKS[2])
    along_y = [swap(mine, mask) for mask in Y_MASKS]
    mine = (mine + along_y[0]) + (along_y[1] + along_y[2])
    mine, *rows = lax.optimization_barrier((mine, *rows))
    strips = call(fold_kernel, [array(2, *side)] * 2, (), (left, right, *rows))
    cols = [None, None]
    mine, *strips = lax.optimization_barrier((mine, *strips))
    cols[0] = meet(strips[0], 1, 1)
    mine = mine + swap(mine, MASKS[3])
    mine, strips[1] = lax.optimization_barrier((mine, strips[1]))
    cols[1] = meet(strips[1], 1, 0)
    mine = mine + swap(mine, MASKS[4])
    mine, *cols = lax.optimization_barrier((mine, *cols))
    (new,) = call(finish_kernel, (field,), (), (part, *rows, *cols))
    other = swap(mine, (1, 1))
    count_all = count * lax.axis_size("row") * lax.axis_size("col")
    (new_probe,) = call(
        functools.partial(probe_kernel, scale=STEP_PROBE / count_all), (array(2, *plane),),
        (), (probe, mine, other),
    )
    return new, new_probe


def solution(mesh):
    placed = (
        P(None, None, "row", "col"),
        P(),
        P("row", "col", None, None),
        P("row", "col"),
        P("row", "col"),
        P("row", "col"),
    )
    return jax.shard_map(
        on_device,
        mesh=mesh,
        in_specs=placed,
        out_specs=(P(None, None, "row", "col"), P()),
        check_vma=False,
    )
```

```python
import functools
import math

import jax
import jax.numpy as jnp
import ml_dtypes
import numpy as np
from jax import lax
from jax.experimental import pallas as pl
from jax.experimental.pallas import tpu as pltpu
from jax.sharding import PartitionSpec as P

STEP_OBJECT = 0.03
STEP_PROBE = 2.0
FRESNEL_PHASE = 60.0
LANES = 128
BOTH = ("row", "col")
GRANT = 16 * 1024 * 1024
MASKS = ((16, 32), (4, 12), (12, 4), (32, 96), (96, 16))
Y_MASKS = ((128, 130), (130, 128), (2, 2))


def split_table(table):
    high = table.astype(ml_dtypes.bfloat16)
    low = (table - high.astype(np.float64)).astype(ml_dtypes.bfloat16)
    return high, low


def make_tables(width):
    index = np.arange(width)
    four = np.exp(-2j * math.pi * (np.outer(index, index) % width) / width) / math.sqrt(width)
    freq = np.where(index < width // 2, index, index - width) / width
    hop = np.conj(four) @ np.diag(np.exp(-1j * FRESNEL_PHASE * freq**2)) @ four
    forms = []
    for table in (hop, four):
        forms.append(np.block([[table.real, table.imag], [-table.imag, table.real]]))
        forms.append(np.block([[table.real, -table.imag], [table.imag, table.real]]))
    pairs = [split_table(form) for form in forms]
    return np.stack([np.stack(pair) for pair in pairs])


def split(value):
    high = value.astype(jnp.bfloat16)
    low = (value - high.astype(jnp.float32)).astype(jnp.bfloat16)
    return high, low


def mul3(left, right):
    dot = functools.partial(jnp.dot, preferred_element_type=jnp.float32)
    return dot(left[0], right[0]) + (dot(left[1], right[0]) + dot(left[0], right[1]))


def two_sided(tabs_ref, right, left, real, imag):
    width = real.shape[1]
    starts = range(0, real.shape[0], width)
    field = split(jnp.concatenate([real, imag], axis=1))
    half = mul3(field, (tabs_ref[right, 0], tabs_ref[right, 1]))
    field = jnp.concatenate(
        [
            jnp.concatenate([half[s : s + width, :width] for s in starts], axis=1),
            jnp.concatenate([half[s : s + width, width:] for s in starts], axis=1),
        ],
        axis=0,
    )
    full = mul3((tabs_ref[left, 0], tabs_ref[left, 1]), split(field))
    return tuple(
        jnp.concatenate([full[part * width : (part + 1) * width, s : s + width] for s in starts], axis=0)
        for part in range(2)
    )


def columns(piece_ref, first):
    half = LANES // 2
    left = jnp.where(first, piece_ref[0, :, :LANES], pltpu.roll(piece_ref[1, :, :LANES], half, 1))
    right = jnp.where(first, pltpu.roll(piece_ref[0, :, LANES:], half, 1), piece_ref[1, :, LANES:])
    return left, right


def pick(axis, even, odd):
    return jnp.where(lax.rem(lax.axis_index(BOTH[axis]), 2) == 0, even, odd)


def beside(axis, a, b):
    place = lax.axis_index(BOTH[axis])
    before = jnp.where(place == 0, 0.0, pick(axis, b, a))
    after = jnp.where(place == lax.axis_size(BOTH[axis]) - 1, 0.0, pick(axis, a, b))
    return before, after


def pack_kernel(obj_ref, colb_ref, cola_ref, held, sem, *, piece):
    first = lax.broadcasted_iota(jnp.int32, (held.shape[1], LANES), 1) < LANES // 2
    copy = pltpu.make_async_copy(obj_ref.at[piece], held, sem)
    copy.start()
    copy.wait()
    left, right = columns(held, first)
    cola_ref[...] = pick(1, right, left)
    colb_ref[...] = pick(1, left, right)


def rows_kernel(obj_ref, colb_ref, cola_ref, rowa_ref, rowb_ref, *, piece):
    half = LANES // 2
    low, high = slice(0, half), slice(obj_ref.shape[2] - half, obj_ref.shape[2])
    for part in range(2):
        for block in range(2):
            cols = slice(block * LANES, (block + 1) * LANES)
            top, bottom = obj_ref[piece, part, low, cols], obj_ref[piece, part, high, cols]
            rowa_ref[2 * part + block] = pick(0, bottom, top)
            rowb_ref[2 * part + block] = pick(0, top, bottom)
    tops = beside(1, cola_ref[low], colb_ref[low])
    bottoms = beside(1, cola_ref[high], colb_ref[high])
    for place, top, bottom in zip((4, 5), tops, bottoms):
        rowa_ref[place] = pick(0, bottom, top)
        rowb_ref[place] = pick(0, top, bottom)


def grow(ext, piece_ref, colb_ref, cola_ref, rowa_ref, rowb_ref):
    half = LANES // 2
    tile = piece_ref.shape[1]
    sides = beside(1, cola_ref[...], colb_ref[...])
    for part in range(2):
        for block in range(4):
            place = 2 * part + block - 1 if block in (1, 2) else 4 + block // 3
            top, bottom = beside(0, rowa_ref[place], rowb_ref[place])
            if block in (1, 2):
                middle = piece_ref[part, :, (block - 1) * LANES : block * LANES]
            else:
                middle = sides[block // 3]
            for strip, start in ((top, 0), (middle, half), (bottom, half + tile)):
                if (block == 0 and part == 0) or (block == 3 and part == 1):
                    strip = pltpu.roll(strip, half, 1)
                ext[part, block, start : start + strip.shape[0]] = strip


def place_window(row_ref, col_ref, slot):
    col = col_ref[0, slot] + LANES // 2
    return row_ref[0, slot], col // LANES, lax.rem(col, LANES)


def window(ext, row_ref, col_ref, slot, width):
    row, block, shift = place_window(row_ref, col_ref, slot)
    back = lax.rem(LANES - shift, LANES)
    keep = lax.broadcasted_iota(jnp.int32, (width, LANES), 1) < LANES - shift
    parts = []
    for part in range(2):
        near = pltpu.roll(ext[part, block, pl.ds(row, width), :], back, 1)
        far = pltpu.roll(ext[part, block + 1, pl.ds(row, width), :], back, 1)
        parts.append(jnp.where(keep, near, far))
    return parts


def windows(ext, row_ref, col_ref, slots, width):
    got = [window(ext, row_ref, col_ref, slot, width) for slot in slots]
    return tuple(jnp.concatenate([g[part] for g in got], axis=0) for part in range(2))


def stacked(ref, slots, part):
    return jnp.concatenate([ref[slot, part] for slot in slots], axis=0)


def store(ref, slots, values):
    width = ref.shape[2]
    for place, slot in enumerate(slots):
        for part in range(2):
            ref[slot, part] = values[part][place * width : (place + 1) * width]


def first_kernel(
    row_ref, col_ref, obj_ref, colb_ref, cola_ref, rowa_ref, rowb_ref, probe_ref, tabs_ref,
    win_ref, mid_ref, ext, *, group,
):
    width = probe_ref.shape[1]
    grow(ext, obj_ref.at[0], colb_ref, cola_ref, rowa_ref, rowb_ref)

    def some(index, _):
        slots = [group * index + place for place in range(group)]
        first_re, first_im = windows(ext, row_ref, col_ref, slots, width)
        probe_re, probe_im = (jnp.concatenate([probe_ref[p]] * group, axis=0) for p in range(2))
        wave_re = probe_re * first_re - probe_im * first_im
        wave_im = probe_re * first_im + probe_im * first_re
        store(win_ref, slots, (first_re, first_im))
        store(mid_ref, slots, two_sided(tabs_ref, 0, 1, wave_re, wave_im))
        return 0

    lax.fori_loop(0, row_ref.shape[1] // group, some, 0, unroll=True)


def second_kernel(
    row_ref, col_ref, live_ref, obj_ref, colb_ref, cola_ref, rowa_ref, rowb_ref,
    win_ref, mid_ref, measured_ref, tabs_ref,
    grad_ref, down_ref, keep_ref, send_ref,
    ext, sum_ref, *, group,
):
    width = win_ref.shape[2]
    grow(ext, obj_ref.at[1], colb_ref, cola_ref, rowa_ref, rowb_ref)
    sum_ref[...] = jnp.zeros_like(sum_ref)

    def some(index, _):
        slots = [group * index + place for place in range(group)]
        second_re, second_im = windows(ext, row_ref, col_ref, slots, width)
        mid_re, mid_im = (stacked(mid_ref, slots, part) for part in range(2))
        exit_re = mid_re * second_re - mid_im * second_im
        exit_im = mid_re * second_im + mid_im * second_re
        far_re, far_im = two_sided(tabs_ref, 2, 3, exit_re, exit_im)
        weights = []
        for place, slot in enumerate(slots):
            rows = slice(place * width, (place + 1) * width)
            active = jnp.where(slot < live_ref[0, 0], 2.0, 0.0)
            power = far_re[rows] * far_re[rows] + far_im[rows] * far_im[rows]
            weights.append((power - measured_ref[slot]) * active)
        weight = jnp.concatenate(weights, axis=0)
        chi_re, chi_im = two_sided(tabs_ref, 3, 2, weight * far_re, weight * far_im)
        grad_re = mid_re * chi_re + mid_im * chi_im
        grad_im = mid_re * chi_im - mid_im * chi_re
        store(grad_ref, slots, (grad_re, grad_im))
        back_re = second_re * chi_re + second_im * chi_im
        back_im = second_re * chi_im - second_im * chi_re
        down_re, down_im = two_sided(tabs_ref, 1, 0, back_re, back_im)
        store(down_ref, slots, (down_re, down_im))
        first_re, first_im = (stacked(win_ref, slots, part) for part in range(2))
        sum_re = first_re * down_re + first_im * down_im
        sum_im = first_re * down_im - first_im * down_re
        for part, value in enumerate((sum_re, sum_im)):
            total = value[:width]
            for start in range(width, group * width, width):
                total += value[start : start + width]
            sum_ref[part] += total
        return 0

    lax.fori_loop(0, row_ref.shape[1] // group, some, 0, unroll=True)
    keep_ref[...] = pick(1, sum_ref[0], sum_ref[1])
    send_ref[...] = pick(1, sum_ref[1], sum_ref[0])


def place_kernel(
    row_ref, col_ref, obj_ref, probe_ref, down_ref, second_ref,
    new_ref, rowa_ref, rowb_ref, left_ref, right_ref,
    grad,
):
    width = probe_ref.shape[1]
    tile = obj_ref.shape[2]
    half = width // 2
    grad[...] = jnp.zeros_like(grad)
    lane = lax.broadcasted_iota(jnp.int32, (width, LANES), 1)

    def deposit(slot, _):
        row, block, shift = place_window(row_ref, col_ref, slot)
        keep = lane >= shift
        probe_re, probe_im = probe_ref[0], probe_ref[1]
        down_re, down_im = down_ref[slot, 0], down_ref[slot, 1]
        values = (
            (probe_re * down_re + probe_im * down_im, probe_re * down_im - probe_im * down_re),
            (second_ref[slot, 0], second_ref[slot, 1]),
        )
        for piece in range(2):
            for part in range(2):
                value = pltpu.roll(values[piece][part], shift, 1)
                grad[piece, part, block, pl.ds(row, width), :] += jnp.where(keep, value, 0.0)
                grad[piece, part, block + 1, pl.ds(row, width), :] += jnp.where(keep, 0.0, value)
        return 0

    lax.fori_loop(0, row_ref.shape[1], deposit, 0)
    first = lax.broadcasted_iota(jnp.int32, (tile + width, LANES), 1) < half
    for piece in range(2):
        for part in range(2):
            for block in range(2):
                cols = slice(block * LANES, (block + 1) * LANES)
                top = grad[piece, part, 1 + block, :half]
                bottom = grad[piece, part, 1 + block, half + tile :]
                rowa_ref[piece, 2 * part + block] = pick(0, bottom, top)
                rowb_ref[piece, 2 * part + block] = pick(0, top, bottom)
                new_ref[piece, part, :, cols] = (
                    obj_ref[piece, part, :, cols]
                    - STEP_OBJECT * grad[piece, part, 1 + block, half : half + tile]
                )
        left = jnp.where(first, pltpu.roll(grad[piece, 0, 0], half, 1), grad[piece, 1, 0])
        right = jnp.where(first, grad[piece, 0, 3], pltpu.roll(grad[piece, 1, 3], half, 1))
        for place, strip, ref in ((4, left, left_ref), (5, right, right_ref)):
            top, bottom = strip[:half], strip[half + tile :]
            rowa_ref[piece, place] = pick(0, bottom, top)
            rowb_ref[piece, place] = pick(0, top, bottom)
            ref[piece] = strip[half : half + tile]


def fold_kernel(left_ref, right_ref, rowa_ref, rowb_ref, colb_ref, cola_ref):
    half = LANES // 2
    tile = left_ref.shape[1]
    for piece in range(2):
        sides = []
        for ref, place in ((left_ref, 4), (right_ref, 5)):
            top, bottom = beside(0, rowa_ref[piece, place], rowb_ref[piece, place])
            sides.append(
                (
                    ref[piece, :half] + top,
                    ref[piece, half : tile - half],
                    ref[piece, tile - half :] + bottom,
                )
            )
        for left, right, rows in zip(*sides, (slice(0, half), slice(half, tile - half), slice(tile - half, tile))):
            cola_ref[piece, rows] = pick(1, right, left)
            colb_ref[piece, rows] = pick(1, left, right)


def finish_kernel(
    part_ref, rowa_ref, rowb_ref, colb_ref, cola_ref, new_ref,
):
    tile = part_ref.shape[2]
    half = LANES // 2
    first = lax.broadcasted_iota(jnp.int32, (half, LANES), 1) < half
    for piece in range(2):
        for start in range(0, tile, half):
            rows = slice(start, start + half)
            sides = beside(1, cola_ref[piece, rows], colb_ref[piece, rows])
            for part in range(2):
                for block in range(2):
                    cols = slice(block * LANES, (block + 1) * LANES)
                    total = sides[block]
                    if block != part:
                        total = pltpu.roll(total, half, 1)
                    total = jnp.where(first == (block == 0), total, 0.0)
                    place = 2 * part + block
                    ends = beside(0, rowa_ref[piece, place], rowb_ref[piece, place])
                    if start == 0:
                        total += ends[0]
                    if start == tile - half:
                        total += ends[1]
                    new_ref[piece, part, rows, cols] = (
                        part_ref[piece, part, rows, cols] - STEP_OBJECT * total
                    )


def probe_kernel(probe_ref, mine_ref, other_ref, newp_ref, *, scale):
    newp_ref[0] = probe_ref[0] - scale * pick(1, mine_ref[...], other_ref[...])
    newp_ref[1] = probe_ref[1] - scale * pick(1, other_ref[...], mine_ref[...])


def vmem(count):
    return [pl.BlockSpec(memory_space=pltpu.VMEM)] * count


def smem(count):
    return [pl.BlockSpec(memory_space=pltpu.SMEM)] * count


def array(*shape):
    return jax.ShapeDtypeStruct(shape, jnp.float32)


def meet(strip, axis, odd):
    sizes = (lax.axis_size("row"), lax.axis_size("col"))
    pairs = []
    for spot in np.ndindex(*sizes):
        other = list(spot)
        place = ((spot[axis] + odd) ^ 1) - odd
        if 0 <= place < sizes[axis]:
            other[axis] = place
        else:
            other[1 - axis] ^= 1
        pairs.append((spot[0] * sizes[1] + spot[1], other[0] * sizes[1] + other[1]))
    return lax.ppermute(strip, BOTH, pairs)


def meet_rows(strips):
    return [meet(strips[0], 0, 0), meet(strips[1], 0, 1)]


def meet_cols(strips):
    return [meet(strips[0], 1, 1), meet(strips[1], 1, 0)]


def swap(value, masks):
    count = lax.axis_size("row") * lax.axis_size("col")
    return lax.ppermute(value, BOTH, [(i, i ^ masks[i % 2]) for i in range(count)])


def call(kernel, out_shape, scalars, arrays, scratch=()):
    return pl.pallas_call(
        kernel, out_shape=tuple(out_shape), in_specs=smem(len(scalars)) + vmem(len(arrays)),
        out_specs=tuple(vmem(len(out_shape))), scratch_shapes=list(scratch),
        compiler_params=pltpu.CompilerParams(vmem_limit_bytes=GRANT),
    )(*scalars, *arrays)


def on_device(object_field, probe, intensity, offset_row, offset_col, live):
    tile = object_field.shape[2]
    width = probe.shape[1]
    half = width // 2
    count = offset_row.shape[1]
    side, edge, plane = (tile, LANES), (6, half, LANES), (width, width)
    field, fields = array(2, 2, tile, tile), array(count, 2, width, width)
    tabs = jnp.asarray(make_tables(width))
    grown = pltpu.VMEM((2, 4, tile + width, LANES), jnp.float32)
    packed = [
        pl.pallas_call(
            functools.partial(pack_kernel, piece=piece), out_shape=tuple([array(*side)] * 2),
            in_specs=[pl.BlockSpec(memory_space=pltpu.HBM)], out_specs=tuple(vmem(2)),
            scratch_shapes=[pltpu.VMEM((2, tile, tile), jnp.float32), pltpu.SemaphoreType.DMA],
            compiler_params=pltpu.CompilerParams(vmem_limit_bytes=GRANT),
        )(pltpu.with_memory_space_constraint(object_field, pltpu.HBM))
        for piece in range(2)
    ]
    halos = []
    cols = [meet_cols(packed[piece]) for piece in range(2)]
    for piece in range(2):
        strips = call(
            functools.partial(rows_kernel, piece=piece), [array(*edge)] * 2,
            (), (object_field, *cols[piece]),
        )
        halos.append((*cols[piece], *meet_rows(strips)))
    win, mid = call(
        functools.partial(first_kernel, group=2), [fields] * 2, (offset_row, offset_col),
        (object_field, *halos[0], probe, tabs), (grown,),
    )
    grad, down, mine, send = call(
        functools.partial(second_kernel, group=count), [fields] * 2 + [array(*plane)] * 2, (offset_row, offset_col, live),
        (object_field, *halos[1], win, mid, intensity[0], tabs),
        (grown, pltpu.VMEM((2, *plane), jnp.float32)),
    )
    part, *strips, left, right = call(
        place_kernel, [field] + [array(2, *edge)] * 2 + [array(2, *side)] * 2,
        (offset_row, offset_col), (object_field, probe, down, grad),
        (pltpu.VMEM((2, 2, 4, tile + width, LANES), jnp.float32),),
    )
    mine = mine + swap(send, (1, 1))
    mine = mine + swap(mine, MASKS[0])
    rows = [None, None]
    mine, strips[1] = lax.optimization_barrier((mine, strips[1]))
    rows[1] = meet(strips[1], 0, 1)
    mine = mine + swap(mine, MASKS[1])
    mine, strips[0] = lax.optimization_barrier((mine, strips[0]))
    rows[0] = meet(strips[0], 0, 0)
    mine = mine + swap(mine, MASKS[2])
    along_y = [swap(mine, mask) for mask in Y_MASKS]
    mine = (mine + along_y[0]) + (along_y[1] + along_y[2])
    mine, *rows = lax.optimization_barrier((mine, *rows))
    strips = call(fold_kernel, [array(2, *side)] * 2, (), (left, right, *rows))
    cols = [None, None]
    mine, *strips = lax.optimization_barrier((mine, *strips))
    cols[0] = meet(strips[0], 1, 1)
    mine = mine + swap(mine, MASKS[3])
    mine, strips[1] = lax.optimization_barrier((mine, strips[1]))
    cols[1] = meet(strips[1], 1, 0)
    mine = mine + swap(mine, MASKS[4])
    mine, *cols = lax.optimization_barrier((mine, *cols))
    (new,) = call(finish_kernel, (field,), (), (part, *rows, *cols))
    other = swap(mine, (1, 1))
    count_all = count * lax.axis_size("row") * lax.axis_size("col")
    (new_probe,) = call(
        functools.partial(probe_kernel, scale=STEP_PROBE / count_all), (array(2, *plane),),
        (), (probe, mine, other),
    )
    return new, new_probe


def solution(mesh):
    placed = (
        P(None, None, "row", "col"),
        P(),
        P("row", "col", None, None),
        P("row", "col"),
        P("row", "col"),
        P("row", "col"),
    )
    return jax.shard_map(
        on_device,
        mesh=mesh,
        in_specs=placed,
        out_specs=(P(None, None, "row", "col"), P()),
        check_vma=False,
    )
```
